512 devices in a mesh: row: 16 (over z, core), col: 32 (over x, y).
Axes of the slice: x: 4, y: 8, z: 8, core: 2. Of those that a mesh axis runs over, the one named last changes fastest.
Arguments:
- profiles: bfloat16 [50, 65536], P(None, ('col', 'row')), may hold values from -1.1953125 to 1.1953125
- cell_width: bfloat16 [65536], P(('col', 'row')), may hold values from 1 to 3
- basis: bfloat16 [64, 65536], P(None, ('col', 'row')), may hold values from -6 to 6
- block_lists: int32 [16, 32, 2, 128], P('row', 'col'), may hold values from 0 to 31, as said below
- block_counts: int32 [16, 32], P('row', 'col'), may hold values from 8 to 128, as said below
- landmarks: int32 [32], replicated, may hold values from 0 to 511, as said below
Outputs:
- row_scaling: float32 [65536], P('row')
- column_scaling: float32 [65536], P('col')
- ritz_basis: float32 [64, 65536], P(None, ('row', 'col'))
The draws below stay inside these ranges and needn't reach their ends.
Inputs may be any that keep to these rules, and one draw needn't show every extreme that they name: `block_lists`: in each tile the first block_counts slots name distinct blocks, row block below 32 and column block below 16; every block of the tile whose global row block and global column block differ by at most one is among them; later slots also name blocks of the tile. `block_counts`: A tile whose column cells lie among its own row cells has exactly 128 live slots. `landmarks`: Distinct, increasing, one in each aligned group of 16 consecutive blocks.
All inputs are finite; a program needn't handle non-finite values.
Results may differ from the reference program's by a relative error of at most 0.0057.
Values may be sent and summed in bfloat16 or wider, within the bound.
A program may use at most 64 MiB of HBM per device.

```python
import math
import jax
import jax.numpy as jnp
from jax import lax

BLK = 128
PCS = 50
COLS = 64
SWEEPS = 3
CB = 16
RB = 32
MAXB = 128
NCELLS = 65536
NBLK = 512
LB = 32
N_ROW = 16
N_COL = 32


def tile_draw(key):
    base_key = jax.random.fold_in(key, 11)
    spread = N_COL // N_ROW
    positions = jnp.arange(RB * CB, dtype=jnp.int32)

    def one_tile(tile_number):
        tile_key = jax.random.fold_in(base_key, tile_number)
        perm_key, extra_key = jax.random.split(tile_key)
        tile_row = tile_number // N_COL
        tile_col = tile_number % N_COL
        global_row = tile_row * RB + positions // CB
        global_col = tile_col * CB + positions % CB
        banded = (jnp.abs(global_row - global_col) <= 1).astype(jnp.int32)
        shuffled = jax.random.permutation(perm_key, positions)
        chosen = shuffled[jnp.argsort(1 - banded[shuffled], stable=True)][:MAXB]
        diagonal_tile = tile_col // spread == tile_row
        extra_blocks = jax.random.randint(extra_key, (), CB // 2, 2 * CB)
        block_total = jnp.where(diagonal_tile, MAXB, jnp.sum(banded) + extra_blocks).astype(jnp.int32)
        return (jnp.stack([chosen // CB, chosen % CB]).astype(jnp.int32), block_total)
    slot_lists, totals = jax.vmap(one_tile)(jnp.arange(N_ROW * N_COL, dtype=jnp.int32))
    return (slot_lists.reshape(N_ROW, N_COL, 2, MAXB), totals.reshape(N_ROW, N_COL))


def draw_block_lists(key, part):
    return tile_draw(key)[0]


def draw_block_counts(key, part):
    return tile_draw(key)[1]


def draw_landmarks(key, part):
    offsets = jax.random.randint(jax.random.fold_in(key, 23), (LB,), 0, 16)
    return (jnp.arange(LB, dtype=jnp.int32) * 16 + offsets).astype(jnp.int32)


def levels(key, shape, cuts, least, top_value):
    level = 1.0
    for dim, parts in cuts:
        steps = jax.random.uniform(jax.random.fold_in(jax.random.fold_in(key, 6), dim), (parts,), jnp.float32, least / len(cuts), top_value / len(cuts))
        level = level * jnp.repeat(jnp.exp(steps), shape[dim] // parts).reshape((-1,) + (1,) * (len(shape) - 1 - dim))
    return level


def normal_values(own_key, shape, deviation, most, cuts=(), held_as=jnp.bfloat16):
    array = deviation * jax.random.normal(own_key, shape, jnp.float32)
    if cuts:
        array = array * levels(own_key, shape, cuts, -0.22, 0.18)
    return jnp.clip(array, -most, most).astype(held_as)


def setup_inputs(seed: int = 0) -> dict:
    keys = jax.random.split(jax.random.key(seed), 7)
    profiles = normal_values(keys[0], (PCS, NCELLS), 0.2, 1.1953125, ((1, 512),))
    cell_width = jnp.clip(jnp.exp(math.log(3.0) - 1.0986123 * jax.random.uniform(keys[1], (NCELLS,), jnp.float32) ** levels(keys[1], (NCELLS,), ((0, 512),), -0.2, 0.2)), 1.0, 3.0).astype(jnp.bfloat16)
    basis = normal_values(keys[2], (COLS, NCELLS), 1.0, 6.0, ((1, 512),))
    block_lists = draw_block_lists(jax.random.fold_in(keys[6], 71), 0)
    block_counts = draw_block_counts(jax.random.fold_in(keys[6], 71), 0)
    landmarks = draw_landmarks(jax.random.fold_in(keys[6], 71), 0)
    return dict(profiles=profiles, cell_width=cell_width, basis=basis, block_lists=block_lists, block_counts=block_counts, landmarks=landmarks)


affinity_scale = 0.001953125
highest = lax.Precision.HIGHEST

def reference(profiles, cell_width, basis, block_lists, block_counts, landmarks):
    slab_slots = 256
    row_tiles = jnp.arange(N_ROW, dtype=jnp.int32)[:, None, None]
    col_tiles = jnp.arange(N_COL, dtype=jnp.int32)[None, :, None]
    slot_index = jnp.arange(MAXB, dtype=jnp.int32)[None, None, :]
    global_rows = (row_tiles * RB + block_lists[:, :, 0, :]).reshape(-1).astype(jnp.int32)
    global_cols = (col_tiles * CB + block_lists[:, :, 1, :]).reshape(-1).astype(jnp.int32)
    live_flag = (slot_index < block_counts[:, :, None]).astype(jnp.int32).reshape(-1)
    live_order = jnp.argsort(1 - live_flag, stable=True)
    padding = jnp.zeros((slab_slots,), jnp.int32)
    row_sorted = jnp.concatenate([global_rows[live_order], padding])
    col_sorted = jnp.concatenate([global_cols[live_order], padding])
    live_sorted = jnp.concatenate([live_flag[live_order], padding]).astype(jnp.float32)
    trip_count = ((jnp.sum(live_flag) + slab_slots - 1) // slab_slots).astype(jnp.int32)
    prof_blocks = profiles.reshape(PCS, NBLK, BLK)
    square_norms = jnp.sum(jnp.square(profiles.astype(jnp.float32)), axis=0).reshape(NBLK, BLK)
    widths = cell_width.astype(jnp.float32).reshape(NBLK, BLK)

    def kernel_at(number):
        first_slot = (number * slab_slots).astype(jnp.int32)
        row_slots = lax.dynamic_slice_in_dim(row_sorted, first_slot, slab_slots)
        col_slots = lax.dynamic_slice_in_dim(col_sorted, first_slot, slab_slots)
        live_mask = lax.dynamic_slice_in_dim(live_sorted, first_slot, slab_slots)
        left_prof = jnp.take(prof_blocks, row_slots, axis=1).astype(jnp.float32)
        right_prof = jnp.take(prof_blocks, col_slots, axis=1).astype(jnp.float32)
        inner_product = jnp.einsum('pkb,pkd->kbd', left_prof, right_prof, precision=highest)
        distance = square_norms[row_slots][:, :, None] + square_norms[col_slots][:, None, :] - 2.0 * inner_product
        width_pair = widths[row_slots][:, :, None] * widths[col_slots][:, None, :]
        kernel = jnp.exp(-distance / width_pair) * (affinity_scale * live_mask)[:, None, None]
        return (kernel, row_slots, col_slots)

    def apply_affinity(update, initial):

        def advance(number, totals):
            return update(totals, kernel_at(number))
        return lax.fori_loop(0, trip_count, advance, initial)

    def column_pass(row_scaling):

        def update(totals, pieces):
            kernel, row_slots, col_slots = pieces
            partial_value = jnp.einsum('kbd,kb->kd', kernel, row_scaling[row_slots], precision=highest)
            return totals.at[col_slots].add(partial_value)
        return 1.0 / apply_affinity(update, jnp.zeros((NBLK, BLK), jnp.float32))

    def row_pass(column_scaling):

        def update(totals, pieces):
            kernel, row_slots, col_slots = pieces
            partial_value = jnp.einsum('kbd,kd->kb', kernel, column_scaling[col_slots], precision=highest)
            return totals.at[row_slots].add(partial_value)
        return 1.0 / apply_affinity(update, jnp.zeros((NBLK, BLK), jnp.float32))
    row_scaling = jnp.ones((NBLK, BLK), jnp.float32)
    column_scaling = jnp.ones((NBLK, BLK), jnp.float32)
    for sweep_number in range(SWEEPS):
        column_scaling = column_pass(row_scaling)
        row_scaling = row_pass(column_scaling)
    scaled_basis = (basis.astype(jnp.float32) * column_scaling.reshape(-1)[None, :]).astype(jnp.bfloat16)
    scaled_basis = lax.optimization_barrier(scaled_basis).astype(jnp.float32).reshape(COLS, NBLK, BLK)

    def subspace_update(totals, pieces):
        kernel, row_slots, col_slots = pieces
        picked = jnp.take(scaled_basis, col_slots, axis=1)
        half_kernel = lax.optimization_barrier(kernel.astype(jnp.bfloat16)).astype(jnp.float32)
        partial_value = jnp.einsum('ckd,kbd->ckb', picked, half_kernel, precision=highest)
        return totals.at[:, row_slots].add(partial_value)
    summed = apply_affinity(subspace_update, jnp.zeros((COLS, NBLK, BLK), jnp.float32))
    projected = summed.reshape(COLS, NCELLS) * row_scaling.reshape(-1)[None, :]
    landmark_mask = jnp.zeros((NBLK,), jnp.float32).at[landmarks].set(1.0)
    cell_mask = jnp.repeat(landmark_mask, BLK)
    masked = projected * cell_mask[None, :]
    gram_matrix = jnp.dot(masked, masked.T, precision=highest) / (LB * BLK)
    lower_factor = jnp.linalg.cholesky(gram_matrix)
    ritz_basis = jax.scipy.linalg.solve_triangular(lower_factor, projected, lower=True)
    return (row_scaling.reshape(-1), column_scaling.reshape(-1), ritz_basis)
```

```python
import functools

import jax
import jax.numpy as jnp
from jax import lax
from jax.experimental import pallas as pl
from jax.experimental.pallas import tpu as pltpu
from jax.sharding import PartitionSpec as P

BLK = 128
PCS = 50
COLS = 64
SWEEPS = 3
KDIM = 64
CP = 16
RP = 32
SCALE = 512.0
MESH = pl.DeviceIdType.MESH
highest = lax.Precision.HIGHEST
f32 = jnp.float32
bf16 = jnp.bfloat16

ROW, COL, ROWKEY, COLKEY, KEEP, LAST, HAS, MARK = range(8)


def slot_table(slot_lists, count, landmarks, own_block, row_blocks):
    slots = slot_lists.shape[1]
    number = jnp.arange(slots, dtype=jnp.int32)
    live = number < count
    row = slot_lists[0]
    col = slot_lists[1]
    key = jnp.where(live, row, RP) * slots + number
    rank = jnp.sum((key[None, :] < key[:, None]).astype(jnp.int32), axis=1)
    place = (rank[None, :] == number[:, None]).astype(jnp.int32)
    pick = lambda v: jnp.sum(place * v[None, :], axis=1)
    rows, cols, lives = pick(row), pick(col), pick(live.astype(jnp.int32))
    rowkey = jnp.where(lives > 0, rows, RP)
    colkey = jnp.where(lives > 0, cols, CP)
    before = jnp.concatenate([jnp.full((1,), -1, jnp.int32), rowkey[:-1]])
    keep = (before == rowkey).astype(jnp.int32)
    upto = jnp.sum((rowkey[None, :] <= number[:, None]).astype(jnp.int32), axis=1)
    has = jnp.any(rowkey[None, :] == number[:, None], axis=1).astype(jnp.int32)
    last = jnp.clip(upto - 1, 0, slots - 1)
    mark = jnp.broadcast_to(jnp.any(landmarks == own_block).astype(jnp.int32), (slots,))
    return jnp.stack([rows, cols, rowkey, colkey, keep, last, has, mark])


def tile_kernel(
    dims,
    prof_ref,
    width_ref,
    basis_ref,
    idx,
    gram_ref,
    proj_ref,
    rows_ref,
    cols_ref,
    msg32,
    rowout,
    colbuf,
    basisbuf,
    rowbuf,
    left,
    uleft,
    uright,
    hot16,
    hot32,
    rhi,
    rlo,
    chi,
    clo,
    sbas,
    aff,
    sums,
    share,
    zvec,
    xvec,
    yvec,
    xshare,
    yshare,
    xgram,
    ygram,
    zgram,
    send_sem,
    recv_sem,
):
    NR, NC, NX, NY, slots = dims
    me_r = lax.axis_index("row")
    me_c = lax.axis_index("col")
    me_x = me_c // NY
    me_y = me_c % NY
    to_r = me_c // 2
    to_c = (me_c % 2) * NR + me_r
    from_c = 2 * me_r + me_c // NR
    from_r = me_c % NR
    moves = (to_r != me_r) | (to_c != me_c)

    def zdev(d):
        return (lax.rem(me_r + d, NR), me_c)

    def xdev(d):
        return (me_r, lax.rem(me_x + d, NX) * NY + me_y)

    def ydev(d):
        return (me_r, me_x * NY + lax.rem(me_y + d, NY))

    groups = {"z": (NR, zdev), "x": (NX, xdev), "y": (NY, ydev)}
    sent = []

    def push(axis, src_of, dst, number):
        size, device = groups[axis]
        for d in range(1, size):
            pltpu.make_async_remote_copy(
                src_ref=src_of(d),
                dst_ref=dst.at[d],
                send_sem=send_sem.at[number],
                recv_sem=recv_sem.at[number],
                device_id=device(d),
                device_id_type=MESH,
            ).start()
        region = dst.at[pl.ds(1, size - 1)]
        sent.append((region, number))
        return lambda: pltpu.make_async_copy(region, region, recv_sem.at[number]).wait()

    prof = prof_ref[...].astype(f32)
    half = jnp.sum(prof * prof, axis=0, keepdims=True) * -0.5
    h1 = half.astype(bf16).astype(f32)
    h2 = (half - h1).astype(bf16).astype(f32)
    h3 = half - h1 - h2
    width = width_ref[...].astype(f32)
    ones = jnp.ones((1, BLK), f32)
    msg32[...] = jnp.zeros_like(msg32)
    for side in range(2):
        msg32[side, 0:PCS, :] = prof
        a, b = (50, 53) if side == 0 else (53, 50)
        msg32[side, a : a + 1, :] = h1
        msg32[side, a + 1 : a + 2, :] = h2
        msg32[side, a + 2 : a + 3, :] = h3
        for n in range(3):
            msg32[side, b + n : b + n + 1, :] = ones
        w = 56 + side
        msg32[side, w : w + 1, :] = width
    colbuf[0] = msg32[1].astype(bf16)
    basisbuf[0] = basis_ref[...]
    outgoing = rowout.at[0]
    rowout[0] = msg32[0].astype(bf16)

    barrier = pltpu.get_barrier_semaphore()
    for size, device in groups.values():
        for d in range(1, size):
            pl.semaphore_signal(barrier, inc=1, device_id=device(d), device_id_type=MESH)

    @pl.when(moves)
    def _():
        pl.semaphore_signal(barrier, inc=1, device_id=(to_r, to_c), device_id_type=MESH)
        pl.semaphore_signal(barrier, inc=1, device_id=(from_r, from_c), device_id_type=MESH)

    near = NR + NX + NY - 3

    it16 = lax.broadcasted_iota(jnp.int32, (CP, BLK), 0)
    it32 = lax.broadcasted_iota(jnp.int32, (RP, BLK), 0)

    def tables(k, carry):
        hot32[k] = (it32 == k).astype(f32).astype(bf16)
        return carry

    lax.fori_loop(0, RP + 1, tables, 0)

    def tables16(k, carry):
        hot16[k] = (it16 == k).astype(f32).astype(bf16)
        return carry

    lax.fori_loop(0, CP + 1, tables16, 0)

    pl.semaphore_wait(barrier, near + 2 * moves.astype(jnp.int32))

    move = pltpu.make_async_remote_copy(
        src_ref=outgoing,
        dst_ref=rowbuf.at[0],
        send_sem=send_sem.at[0],
        recv_sem=recv_sem.at[0],
        device_id=(to_r, to_c),
        device_id_type=MESH,
    )
    stay = pltpu.make_async_copy(outgoing, rowbuf.at[0], recv_sem.at[0])

    @pl.when(moves)
    def _():
        move.start()

    @pl.when(jnp.logical_not(moves))
    def _():
        stay.start()

    wait_col = push("z", lambda d: colbuf.at[0], colbuf, 1)

    @pl.when(moves)
    def _():
        move.wait_recv()
        move.wait_send()

    @pl.when(jnp.logical_not(moves))
    def _():
        stay.wait()

    for d in range(1, NX):
        pltpu.make_async_remote_copy(
            src_ref=rowbuf.at[0],
            dst_ref=rowbuf.at[d],
            send_sem=send_sem.at[2],
            recv_sem=recv_sem.at[2],
            device_id=xdev(d),
            device_id_type=MESH,
        ).start()
    region = rowbuf.at[pl.ds(1, NX - 1)]
    sent.append((region, 2))
    pltpu.make_async_copy(region, region, recv_sem.at[2]).wait()
    for d in range(1, NY):
        pltpu.make_async_remote_copy(
            src_ref=rowbuf.at[pl.ds(0, NX)],
            dst_ref=rowbuf.at[pl.ds(d * NX, NX)],
            send_sem=send_sem.at[3],
            recv_sem=recv_sem.at[3],
            device_id=ydev(d),
            device_id_type=MESH,
        ).start()
    region_y = rowbuf.at[pl.ds(NX, (NY - 1) * NX)]
    sent.append((region_y, 3))

    wait_basis = push("z", lambda d: basisbuf.at[0], basisbuf, 4)
    wait_col()

    def col_place(j):
        return lax.rem(me_r - j + NR, NR)

    def row_place(i):
        return lax.rem(me_y - lax.rem(i, NY) + NY, NY) * NX + lax.rem(me_x - i // NY + NX, NX)

    def col_prepare(n, carry):
        turned = colbuf[n].astype(f32).T
        left[n] = turned.astype(bf16)
        w = jnp.broadcast_to(turned[:, 57:58], (BLK, BLK))
        uleft[n] = (2.0 * 1.4426950408889634) / w
        return carry

    lax.fori_loop(0, NR, col_prepare, 0)

    pltpu.make_async_copy(region_y, region_y, recv_sem.at[3]).wait()

    def row_prepare(n, carry):
        w = rowbuf[n].astype(f32)[56:57, :]
        uright[n] = jnp.broadcast_to(1.0 / w, (8, BLK))
        return carry

    lax.fori_loop(0, NC, row_prepare, 0)

    def build(s, carry):
        j = col_place(idx[COL, s])
        i = row_place(idx[ROW, s])
        d = jnp.dot(left[j], rowbuf[i], preferred_element_type=f32)
        e = d * uleft[j] * uright[i][0:1, :]
        aff[s] = jnp.exp2(e).astype(bf16)
        return carry

    lax.fori_loop(0, slots, build, 0, unroll=4)

    def col_pass():
        def step(s, acc):
            i = idx[ROW, s]
            hot = hot16[idx[COLKEY, s]]
            lhs = jnp.concatenate([rhi[i] * hot, rlo[i] * hot], axis=0)
            return acc + lax.dot_general(
                lhs, aff[s], (((1,), (1,)), ((), ())), preferred_element_type=f32
            )

        acc = lax.fori_loop(0, slots, step, jnp.zeros((2 * CP, BLK), f32), unroll=4)
        return acc[0:CP] + acc[CP:]

    def row_pass():
        def step(s, acc):
            j = idx[COL, s]
            hot = hot32[idx[ROWKEY, s]]
            lhs = jnp.concatenate([chi[j] * hot, clo[j] * hot], axis=0)
            return acc + jnp.dot(lhs, aff[s], preferred_element_type=f32)

        acc = lax.fori_loop(0, slots, step, jnp.zeros((2 * RP, BLK), f32), unroll=4)
        return acc[0:RP] + acc[RP:]

    def col_total(k, part):
        buf = zvec.at[k]
        buf[0] = part
        wait = push("z", lambda d: buf.at[0], buf, 5 + k)
        wait()
        total = buf[lax.rem(me_r, NR)]
        for r in range(1, NR):
            total = total + buf[lax.rem(me_r - r + NR, NR)]
        return total

    def row_total(k, part, during=None):
        bx = xvec.at[k]
        bx[0] = part
        wait = push("x", lambda d: bx.at[0], bx, 8 + k)
        if during is not None:
            during()
        wait()
        total = bx[me_x]
        for x in range(1, NX):
            total = total + bx[lax.rem(me_x - x + NX, NX)]
        by = yvec.at[k]
        by[0] = total
        push("y", lambda d: by.at[0], by, 11 + k)()
        total = by[me_y]
        for y in range(1, NY):
            total = total + by[lax.rem(me_y - y + NY, NY)]
        return total

    def spread(vec, blocks, width_, hi_ref, lo_ref):
        for n in range(blocks):
            v = jnp.broadcast_to(vec[n : n + 1, :], (width_, BLK))
            hi = v.astype(bf16)
            hi_ref[n] = hi
            lo_ref[n] = (v - hi.astype(f32)).astype(bf16)

    rhi[...] = jnp.ones_like(rhi)
    rlo[...] = jnp.zeros_like(rlo)
    for k in range(SWEEPS):
        cvec = SCALE / col_total(k, col_pass())
        spread(cvec, NR, RP, chi, clo)
        if k < SWEEPS - 1:
            rvec = SCALE / row_total(k, row_pass())
            spread(rvec, NC, CP, rhi, rlo)
    cols_ref[...] = cvec

    wait_basis()
    for j in range(NR):
        block = basisbuf[col_place(j)].astype(f32) * cvec[j : j + 1, :]
        sbas[j] = block.astype(bf16)

    def subspace():
        def step(s, acc):
            keep = idx[KEEP, s].astype(f32)
            acc = acc * keep + jnp.dot(sbas[idx[COL, s]], aff[s], preferred_element_type=f32)
            sums[s] = acc
            return acc

        lax.fori_loop(0, slots, step, jnp.zeros((COLS, BLK), f32), unroll=4)

        def pick(i, carry):
            share[i] = sums[idx[LAST, i]] * idx[HAS, i].astype(f32)
            return carry

        lax.fori_loop(0, NC, pick, 0)

    rvec = SCALE / row_total(SWEEPS - 1, row_pass(), subspace)
    rows_ref[...] = rvec

    def own_part(x):
        return share.at[pl.ds(x * NY, NY)]

    wait = push("x", lambda d: own_part(lax.rem(me_x + d, NX)), xshare, 14)
    wait()

    def add_x(n, carry):
        total = jnp.zeros((COLS, BLK), f32) + share[me_x * NY + n]
        for d in range(1, NX):
            total = total + xshare[d, n]
        xshare[0, n] = total
        return carry

    lax.fori_loop(0, NY, add_x, 0)
    wait = push("y", lambda d: xshare.at[0, lax.rem(me_y + d, NY)], yshare, 15)
    wait()
    total = xshare[0, me_y]
    for d in range(1, NY):
        total = total + yshare[d]
    proj = total * (rows_ref[pl.ds(me_c, 1), :] * (1.0 / SCALE))
    proj_ref[...] = proj

    masked = proj * idx[MARK, 0].astype(f32)
    gram = lax.dot_general(
        masked, masked, (((1,), (1,)), ((), ())), precision=highest, preferred_element_type=f32
    )
    half_rows = COLS // 2
    packed = jnp.concatenate([gram[:half_rows], gram[half_rows:]], axis=1)
    for axis, buf, number, size, me in (
        ("x", xgram, 16, NX, me_x),
        ("y", ygram, 17, NY, me_y),
        ("z", zgram, 18, NR, me_r),
    ):
        buf[0] = packed
        push(axis, lambda d, buf=buf: buf.at[0], buf, number)()
        packed = buf[me]
        for n in range(1, size):
            packed = packed + buf[lax.rem(me - n + size, size)]
    gram_ref[...] = packed

    for region, number in sent:
        pltpu.make_async_copy(region, region, send_sem.at[number]).wait()


def finish_kernel(gram_ref, proj_ref, rows_in, cols_in, ritz_ref, rows_ref, cols_ref, *, cells):
    rows_ref[...] = rows_in[...]
    cols_ref[...] = cols_in[...]
    half_rows = COLS // 2
    packed = gram_ref[...] * (1.0 / cells)
    gram = jnp.concatenate([packed[:, :COLS], packed[:, COLS:]], axis=0)
    proj = proj_ref[...]
    number = lax.broadcasted_iota(jnp.int32, (COLS, 1), 0)
    for k in range(COLS):
        scale = 1.0 / jnp.sqrt(gram[k : k + 1, k : k + 1])
        grow = gram[k : k + 1, :] * scale
        prow = proj[k : k + 1, :] * scale
        ritz_ref[k : k + 1, :] = prow
        factor = jnp.where(number > k, gram[:, k : k + 1] * scale, 0.0)
        gram = gram - factor * grow
        proj = proj - factor * prow


def body(mesh_sizes, profiles, cell_width, basis, block_lists, block_counts, landmarks):
    NR, NC, NX, NY = mesh_sizes
    slots = block_lists.shape[-1]
    own_block = lax.axis_index("row") * NC + lax.axis_index("col")
    table = slot_table(block_lists[0, 0], block_counts[0, 0], landmarks, own_block, NC)
    vmem = pl.BlockSpec(memory_space=pltpu.VMEM)
    smem = pl.BlockSpec(memory_space=pltpu.SMEM)
    half_rows = COLS // 2
    gram, proj, rows, cols = pl.pallas_call(
        functools.partial(tile_kernel, (NR, NC, NX, NY, slots)),
        out_shape=(
            jax.ShapeDtypeStruct((half_rows, BLK), f32),
            jax.ShapeDtypeStruct((COLS, BLK), f32),
            jax.ShapeDtypeStruct((RP, BLK), f32),
            jax.ShapeDtypeStruct((CP, BLK), f32),
        ),
        in_specs=[vmem, vmem, vmem, smem],
        out_specs=(vmem,) * 4,
        scratch_shapes=[
            pltpu.VMEM((2, KDIM, BLK), f32),
            pltpu.VMEM((1, KDIM, BLK), bf16),
            pltpu.VMEM((NR, KDIM, BLK), bf16),
            pltpu.VMEM((NR, COLS, BLK), bf16),
            pltpu.VMEM((NC, KDIM, BLK), bf16),
            pltpu.VMEM((NR, BLK, KDIM), bf16),
            pltpu.VMEM((NR, BLK, BLK), f32),
            pltpu.VMEM((NC, 8, BLK), f32),
            pltpu.VMEM((CP + 1, CP, BLK), bf16),
            pltpu.VMEM((RP + 1, RP, BLK), bf16),
            pltpu.VMEM((NC, CP, BLK), bf16),
            pltpu.VMEM((NC, CP, BLK), bf16),
            pltpu.VMEM((NR, RP, BLK), bf16),
            pltpu.VMEM((NR, RP, BLK), bf16),
            pltpu.VMEM((NR, COLS, BLK), bf16),
            pltpu.VMEM((slots, BLK, BLK), bf16),
            pltpu.VMEM((slots, COLS, BLK), f32),
            pltpu.VMEM((NC, COLS, BLK), f32),
            pltpu.VMEM((SWEEPS, NR, CP, BLK), f32),
            pltpu.VMEM((SWEEPS, NX, RP, BLK), f32),
            pltpu.VMEM((SWEEPS, NY, RP, BLK), f32),
            pltpu.VMEM((NX, NY, COLS, BLK), f32),
            pltpu.VMEM((NY, COLS, BLK), f32),
            pltpu.VMEM((NX, half_rows, BLK), f32),
            pltpu.VMEM((NY, half_rows, BLK), f32),
            pltpu.VMEM((NR, half_rows, BLK), f32),
            pltpu.SemaphoreType.DMA((20,)),
            pltpu.SemaphoreType.DMA((20,)),
        ],
        compiler_params=pltpu.CompilerParams(collective_id=0, has_side_effects=True),
        name="tile",
    )(profiles, cell_width.reshape(1, BLK), basis, table)
    ritz, rows, cols = pl.pallas_call(
        functools.partial(finish_kernel, cells=landmarks.shape[0] * BLK),
        out_shape=(
            jax.ShapeDtypeStruct((COLS, BLK), f32),
            jax.ShapeDtypeStruct((RP, BLK), f32),
            jax.ShapeDtypeStruct((CP, BLK), f32),
        ),
        in_specs=[vmem] * 4,
        out_specs=(vmem,) * 3,
        name="finish",
    )(gram, proj, rows, cols)
    return rows[:NC].reshape(-1), cols[:NR].reshape(-1), ritz


def solution(mesh):
    NR, NC = mesh.shape["row"], mesh.shape["col"]
    NX = {32: 4, 4: 2}[NC]
    placed = (
        P(None, ("col", "row")),
        P(("col", "row")),
        P(None, ("col", "row")),
        P("row", "col", None, None),
        P("row", "col"),
        P(),
    )
    return jax.shard_map(
        functools.partial(body, (NR, NC, NX, NC // NX)),
        mesh=mesh,
        in_specs=placed,
        out_specs=(P("row"), P("col"), P(None, ("row", "col"))),
        check_vma=False,
    )
```

```python
import functools

import jax
import jax.numpy as jnp
from jax import lax
from jax.experimental import pallas as pl
from jax.experimental.pallas import tpu as pltpu
from jax.sharding import PartitionSpec as P

BLK = 128
PCS = 50
COLS = 64
SWEEPS = 3
KDIM = 64
CP = 16
RP = 32
SCALE = 512.0
MESH = pl.DeviceIdType.MESH
highest = lax.Precision.HIGHEST
f32 = jnp.float32
bf16 = jnp.bfloat16

ROW, COL, ROWKEY, COLKEY, KEEP, LAST, HAS, MARK = range(8)


def slot_table(slot_lists, count, landmarks, own_block, row_blocks):
    slots = slot_lists.shape[1]
    number = jnp.arange(slots, dtype=jnp.int32)
    live = number < count
    row = slot_lists[0]
    col = slot_lists[1]
    key = jnp.where(live, row, RP) * slots + number
    rank = jnp.sum((key[None, :] < key[:, None]).astype(jnp.int32), axis=1)
    place = (rank[None, :] == number[:, None]).astype(jnp.int32)
    pick = lambda v: jnp.sum(place * v[None, :], axis=1)
    rows, cols, lives = pick(row), pick(col), pick(live.astype(jnp.int32))
    rowkey = jnp.where(lives > 0, rows, RP)
    colkey = jnp.where(lives > 0, cols, CP)
    before = jnp.concatenate([jnp.full((1,), -1, jnp.int32), rowkey[:-1]])
    keep = (before == rowkey).astype(jnp.int32)
    upto = jnp.sum((rowkey[None, :] <= number[:, None]).astype(jnp.int32), axis=1)
    has = jnp.any(rowkey[None, :] == number[:, None], axis=1).astype(jnp.int32)
    last = jnp.clip(upto - 1, 0, slots - 1)
    mark = jnp.broadcast_to(jnp.any(landmarks == own_block).astype(jnp.int32), (slots,))
    return jnp.stack([rows, cols, rowkey, colkey, keep, last, has, mark])


def tile_kernel(
    dims,
    prof_ref,
    width_ref,
    basis_ref,
    idx,
    gram_ref,
    proj_ref,
    rows_ref,
    cols_ref,
    msg32,
    rowout,
    colbuf,
    basisbuf,
    rowbuf,
    left,
    uleft,
    uright,
    hot,
    rsplit,
    csplit,
    sbas,
    aff,
    sums,
    rowsums,
    rowpick,
    share,
    zvec,
    xvec,
    yvec,
    xshare,
    ysend,
    yshare,
    xgram,
    ygram,
    zgram,
    send_sem,
    recv_sem,
):
    NR, NC, NX, NY, slots = dims
    me_r = lax.axis_index("row")
    me_c = lax.axis_index("col")
    me_x = me_c // NY
    me_y = me_c % NY
    to_r = me_c // 2
    to_c = (me_c % 2) * NR + me_r
    from_c = 2 * me_r + me_c // NR
    from_r = me_c % NR
    moves = (to_r != me_r) | (to_c != me_c)

    def zdev(d):
        return (lax.rem(me_r + d, NR), me_c)

    def xdev(d):
        return (me_r, lax.rem(me_x + d, NX) * NY + me_y)

    def ydev(d):
        return (me_r, me_x * NY + lax.rem(me_y + d, NY))

    awaited = {}

    def expect(region, number):
        awaited[number] = region

        def wait():
            del awaited[number]
            pltpu.make_async_copy(region, region, recv_sem.at[number]).wait()

        return wait

    def drain():
        for number, region in list(awaited.items()):
            pltpu.make_async_copy(region, region, recv_sem.at[number]).wait()
        for region, number in sent:
            pltpu.make_async_copy(region, region, send_sem.at[number]).wait()

    groups = {"z": (NR, zdev), "x": (NX, xdev), "y": (NY, ydev)}
    sent = []

    def push(axis, src_of, dst, number):
        size, device = groups[axis]
        for d in range(1, size):
            pltpu.make_async_remote_copy(
                src_ref=src_of(d),
                dst_ref=dst.at[d],
                send_sem=send_sem.at[number],
                recv_sem=recv_sem.at[number],
                device_id=device(d),
                device_id_type=MESH,
            ).start()
        region = dst.at[pl.ds(1, size - 1)]
        sent.append((region, number))
        return expect(region, number)

    prof = prof_ref[...].astype(f32)
    half = jnp.sum(prof * prof, axis=0, keepdims=True) * -0.5
    h1 = half.astype(bf16).astype(f32)
    h2 = (half - h1).astype(bf16).astype(f32)
    h3 = half - h1 - h2
    width = width_ref[...].astype(f32)
    ones = jnp.ones((1, BLK), f32)
    msg32[...] = jnp.zeros_like(msg32)
    for side in range(2):
        msg32[side, 0:PCS, :] = prof
        a, b = (50, 53) if side == 0 else (53, 50)
        msg32[side, a : a + 1, :] = h1
        msg32[side, a + 1 : a + 2, :] = h2
        msg32[side, a + 2 : a + 3, :] = h3
        for n in range(3):
            msg32[side, b + n : b + n + 1, :] = ones
        w = 56 + side
        msg32[side, w : w + 1, :] = width
    colbuf[0] = msg32[1].astype(bf16)
    basisbuf[0] = basis_ref[...]
    outgoing = rowout.at[0]
    rowout[0] = msg32[0].astype(bf16)

    barrier = pltpu.get_barrier_semaphore()
    for size, device in groups.values():
        for d in range(1, size):
            pl.semaphore_signal(barrier, inc=1, device_id=device(d), device_id_type=MESH)

    @pl.when(moves)
    def _():
        pl.semaphore_signal(barrier, inc=1, device_id=(to_r, to_c), device_id_type=MESH)
        pl.semaphore_signal(barrier, inc=1, device_id=(from_r, from_c), device_id_type=MESH)

    near = NR + NX + NY - 3

    it = lax.broadcasted_iota(jnp.int32, (2 * CP, BLK), 0)

    def tables(k, carry):
        hot[k] = ((it == k) | (it == k + CP)).astype(f32).astype(bf16)
        return carry

    lax.fori_loop(0, CP, tables, 0)
    hot[CP] = jnp.zeros((2 * CP, BLK), bf16)

    pl.semaphore_wait(barrier, near + 2 * moves.astype(jnp.int32))

    move = pltpu.make_async_remote_copy(
        src_ref=outgoing,
        dst_ref=rowbuf.at[0],
        send_sem=send_sem.at[0],
        recv_sem=recv_sem.at[0],
        device_id=(to_r, to_c),
        device_id_type=MESH,
    )
    stay = pltpu.make_async_copy(outgoing, rowbuf.at[0], recv_sem.at[0])

    @pl.when(moves)
    def _():
        move.start()

    @pl.when(jnp.logical_not(moves))
    def _():
        stay.start()

    wait_col = push("z", lambda d: colbuf.at[0], colbuf, 1)

    @pl.when(moves)
    def _():
        move.wait_recv()
        move.wait_send()

    @pl.when(jnp.logical_not(moves))
    def _():
        stay.wait()

    for d in range(1, NY):
        pltpu.make_async_remote_copy(
            src_ref=rowbuf.at[0],
            dst_ref=rowbuf.at[d],
            send_sem=send_sem.at[2],
            recv_sem=recv_sem.at[2],
            device_id=ydev(d),
            device_id_type=MESH,
        ).start()
    region = rowbuf.at[pl.ds(1, NY - 1)]
    sent.append((region, 2))
    pltpu.make_async_copy(region, region, recv_sem.at[2]).wait()
    for d in range(1, NX):
        pltpu.make_async_remote_copy(
            src_ref=rowbuf.at[pl.ds(0, NY)],
            dst_ref=rowbuf.at[pl.ds(d * NY, NY)],
            send_sem=send_sem.at[3],
            recv_sem=recv_sem.at[3],
            device_id=xdev(d),
            device_id_type=MESH,
        ).start()
    region_x = rowbuf.at[pl.ds(NY, (NX - 1) * NY)]
    sent.append((region_x, 3))
    wait_rows = expect(region_x, 3)

    wait_col()

    def col_place(j):
        return lax.rem(me_r - j + NR, NR)

    def row_place(i):
        return lax.rem(me_x - i // NY + NX, NX) * NY + lax.rem(me_y - lax.rem(i, NY) + NY, NY)

    def col_prepare(n, carry):
        turned = colbuf[n].astype(f32).T
        left[n] = turned.astype(bf16)
        w = jnp.broadcast_to(turned[:, 57:58], (BLK, BLK))
        uleft[n] = (2.0 * 1.4426950408889634) / w
        return carry

    lax.fori_loop(0, NR, col_prepare, 0)

    wait_rows()

    def row_prepare(n, carry):
        w = rowbuf[n].astype(f32)[56:57, :]
        uright[n] = jnp.broadcast_to(1.0 / w, (8, BLK))
        return carry

    lax.fori_loop(0, NC, row_prepare, 0)

    pairs = slots // 2

    def build(p, carry):
        for h in range(2):
            j = col_place(idx[COL, 2 * p + h])
            i = row_place(idx[ROW, 2 * p + h])
            d = jnp.dot(left[j], rowbuf[i], preferred_element_type=f32)
            e = d * uleft[j] * uright[i][0:1, :]
            aff[p, :, h * BLK : (h + 1) * BLK] = jnp.exp2(e).astype(bf16)
        return carry

    lax.fori_loop(0, pairs, build, 0, unroll=4)

    def col_pass():
        def step(p, acc):
            s, t = 2 * p, 2 * p + 1
            lhs = jnp.concatenate(
                [
                    rsplit[idx[ROW, s]] * hot[idx[COLKEY, s]],
                    rsplit[idx[ROW, t]] * hot[idx[COLKEY, t]],
                ],
                axis=1,
            )
            return acc + lax.dot_general(
                lhs, aff[p], (((1,), (1,)), ((), ())), preferred_element_type=f32
            )

        acc = lax.fori_loop(0, pairs, step, jnp.zeros((2 * CP, BLK), f32), unroll=8)
        return acc[0:CP] + acc[CP:]

    sub8 = lax.broadcasted_iota(jnp.int32, (8, BLK), 0)

    def row_pass():
        def step(p, acc):
            s, t = 2 * p, 2 * p + 1
            lhs = csplit[idx[COL, s], 0] + csplit[idx[COL, t], 1]
            both = jnp.dot(lhs, aff[p], preferred_element_type=f32)
            acc = acc * idx[KEEP, s].astype(f32) + jnp.where(sub8 < 2, both[:, :BLK], 0.0)
            rowsums[s] = acc
            acc = acc * idx[KEEP, t].astype(f32) + jnp.where(sub8 < 2, 0.0, both[:, BLK:])
            rowsums[t] = acc
            return acc

        lax.fori_loop(0, pairs, step, jnp.zeros((8, BLK), f32), unroll=8)
        for i in range(NC):
            rowpick[i] = rowsums[idx[LAST, i]] * idx[HAS, i].astype(f32)
        return jnp.sum(rowpick[...], axis=1)

    def col_total(k, part):
        buf = zvec.at[k]
        buf[0] = part
        wait = push("z", lambda d: buf.at[0], buf, 5 + k)
        wait()
        total = buf[lax.rem(me_r, NR)]
        for r in range(1, NR):
            total = total + buf[lax.rem(me_r - r + NR, NR)]
        return total

    def row_total(k, part):
        bx = xvec.at[k]
        bx[0] = part
        wait = push("x", lambda d: bx.at[0], bx, 8 + k)
        wait()
        total = bx[me_x]
        for x in range(1, NX):
            total = total + bx[lax.rem(me_x - x + NX, NX)]
        by = yvec.at[k]
        by[0] = total
        push("y", lambda d: by.at[0], by, 11 + k)()
        total = by[me_y]
        for y in range(1, NY):
            total = total + by[lax.rem(me_y - y + NY, NY)]
        return total

    def split(v):
        hi = v.astype(bf16).astype(f32)
        return hi, v - hi

    def spread_rows(vec):
        for n in range(NC):
            hi, lo = split(jnp.broadcast_to(vec[n : n + 1, :], (CP, BLK)))
            rsplit[n] = jnp.concatenate([hi, lo], axis=0).astype(bf16)

    def spread_cols(vec):
        for n in range(NR):
            hi, lo = split(jnp.broadcast_to(vec[n : n + 1, :], (8, BLK)))
            even = jnp.where(sub8 % 2 == 0, hi, lo)
            csplit[n, 0] = jnp.where(sub8 < 2, even, 0.0).astype(bf16)
            csplit[n, 1] = jnp.where((sub8 >= 2) & (sub8 < 4), even, 0.0).astype(bf16)

    first = lax.broadcasted_iota(jnp.int32, (NC, 2 * CP, BLK), 1)
    rsplit[...] = jnp.where(first < CP, 1.0, 0.0).astype(bf16)
    for k in range(SWEEPS):
        part = col_pass()
        cols_ref[...] = part
        cvec = SCALE / col_total(k, part)
        spread_cols(cvec)
        if k < SWEEPS - 1:
            part = row_pass()
            rows_ref[...] = part
            if k == 0:
                wait_basis = push("z", lambda d: basisbuf.at[0], basisbuf, 4)
            rvec = SCALE / row_total(k, part)
            spread_rows(rvec)
    cols_ref[...] = cvec

    wait_basis()
    for j in range(NR):
        block = basisbuf[col_place(j)].astype(f32) * cvec[j : j + 1, :]
        sbas[j] = block.astype(bf16)

    def subspace(p, acc):
        for h in range(2):
            s = 2 * p + h
            product = jnp.dot(
                sbas[idx[COL, s]],
                aff[p, :, h * BLK : (h + 1) * BLK],
                preferred_element_type=f32,
            )
            acc = acc * idx[KEEP, s].astype(f32) + product
            sums[s] = acc
        return acc

    lax.fori_loop(0, pairs, subspace, jnp.zeros((COLS, BLK), f32), unroll=4)

    def pick(i, carry):
        share[i] = (sums[idx[LAST, i]] * idx[HAS, i].astype(f32)).astype(share.dtype)
        return carry

    lax.fori_loop(0, NC, pick, 0)

    def own_part(x):
        return share.at[pl.ds(x * NY, NY)]

    wait_share = push("x", lambda d: own_part(lax.rem(me_x + d, NX)), xshare, 14)
    part = row_pass()
    rvec = SCALE / row_total(SWEEPS - 1, part)
    rows_ref[...] = rvec
    wait_share()

    def add_x(n, carry):
        total = share[me_x * NY + n].astype(f32)
        for d in range(1, NX):
            total = total + xshare[d, n].astype(f32)
        ysend[n] = total
        return carry

    lax.fori_loop(0, NY, add_x, 0)
    push("y", lambda d: ysend.at[lax.rem(me_y + d, NY)], yshare, 15)()
    total = ysend[me_y]
    for d in range(1, NY):
        total = total + yshare[d]
    proj = total * (rows_ref[pl.ds(me_c, 1), :] * (1.0 / SCALE))
    proj_ref[...] = proj

    masked = proj * idx[MARK, 0].astype(f32)
    gram = lax.dot_general(
        masked, masked, (((1,), (1,)), ((), ())), precision=highest, preferred_element_type=f32
    )
    half_rows = COLS // 2
    packed = jnp.concatenate([gram[:half_rows], gram[half_rows:]], axis=1)
    for axis, buf, number, size, me in (
        ("x", xgram, 16, NX, me_x),
        ("y", ygram, 17, NY, me_y),
        ("z", zgram, 18, NR, me_r),
    ):
        buf[0] = packed
        push(axis, lambda d, buf=buf: buf.at[0], buf, number)()
        packed = buf[me]
        for n in range(1, size):
            packed = packed + buf[lax.rem(me - n + size, size)]
    gram_ref[...] = packed

    drain()


def finish_kernel(gram_ref, proj_ref, rows_in, cols_in, ritz_ref, rows_ref, cols_ref, *, cells):
    rows_ref[...] = rows_in[...]
    cols_ref[...] = cols_in[...]
    half_rows = COLS // 2
    packed = gram_ref[...] * (1.0 / cells)
    gram = jnp.concatenate([packed[:, :COLS], packed[:, COLS:]], axis=0)
    proj = proj_ref[...]
    gs = [gram[n : n + 8] for n in range(0, COLS, 8)]
    ps = [proj[n : n + 8] for n in range(0, COLS, 8)]
    for k in range(COLS):
        top, row = k // 8, k % 8
        cols = [jnp.broadcast_to(g[:, k : k + 1], (8, BLK)) for g in gs[top:]]
        pivot = cols[0][row : row + 1, :]
        inv = 1.0 / pivot
        grow = gs[top][row : row + 1, :] * inv[:, :COLS]
        prow = ps[top][row : row + 1, :]
        ritz_ref[k : k + 1, :] = prow * (1.0 / jnp.sqrt(pivot))
        prow = prow * inv
        for n in range(top, COLS // 8):
            col = cols[n - top]
            gs[n] = gs[n] - col[:, :COLS] * grow
            ps[n] = ps[n] - col * prow


def body(mesh_sizes, profiles, cell_width, basis, block_lists, block_counts, landmarks):
    NR, NC, NX, NY = mesh_sizes
    slots = block_lists.shape[-1]
    own_block = lax.axis_index("row") * NC + lax.axis_index("col")
    table = slot_table(block_lists[0, 0], block_counts[0, 0], landmarks, own_block, NC)
    vmem = pl.BlockSpec(memory_space=pltpu.VMEM)
    smem = pl.BlockSpec(memory_space=pltpu.SMEM)
    half_rows = COLS // 2
    gram, proj, rows, cols = pl.pallas_call(
        functools.partial(tile_kernel, (NR, NC, NX, NY, slots)),
        out_shape=(
            jax.ShapeDtypeStruct((half_rows, BLK), f32),
            jax.ShapeDtypeStruct((COLS, BLK), f32),
            jax.ShapeDtypeStruct((NC, BLK), f32),
            jax.ShapeDtypeStruct((CP, BLK), f32),
        ),
        in_specs=[vmem, vmem, vmem, smem],
        out_specs=(vmem,) * 4,
        scratch_shapes=[
            pltpu.VMEM((2, KDIM, BLK), f32),
            pltpu.VMEM((1, KDIM, BLK), bf16),
            pltpu.VMEM((NR, KDIM, BLK), bf16),
            pltpu.VMEM((NR, COLS, BLK), bf16),
            pltpu.VMEM((NC, KDIM, BLK), bf16),
            pltpu.VMEM((NR, BLK, KDIM), bf16),
            pltpu.VMEM((NR, BLK, BLK), f32),
            pltpu.VMEM((NC, 8, BLK), f32),
            pltpu.VMEM((CP + 1, 2 * CP, BLK), bf16),
            pltpu.VMEM((NC, 2 * CP, BLK), bf16),
            pltpu.VMEM((NR, 2, 8, BLK), bf16),
            pltpu.VMEM((NR, COLS, BLK), bf16),
            pltpu.VMEM((slots // 2, BLK, 2 * BLK), bf16),
            pltpu.VMEM((slots, COLS, BLK), f32),
            pltpu.VMEM((slots, 8, BLK), f32),
            pltpu.VMEM((NC, 8, BLK), f32),
            pltpu.VMEM((NC, COLS, BLK), f32),
            pltpu.VMEM((SWEEPS, NR, CP, BLK), f32),
            pltpu.VMEM((SWEEPS, NX, NC, BLK), f32),
            pltpu.VMEM((SWEEPS, NY, NC, BLK), f32),
            pltpu.VMEM((NX, NY, COLS, BLK), f32),
            pltpu.VMEM((NY, COLS, BLK), f32),
            pltpu.VMEM((NY, COLS, BLK), f32),
            pltpu.VMEM((NX, half_rows, BLK), f32),
            pltpu.VMEM((NY, half_rows, BLK), f32),
            pltpu.VMEM((NR, half_rows, BLK), f32),
            pltpu.SemaphoreType.DMA((20,)),
            pltpu.SemaphoreType.DMA((20,)),
        ],
        compiler_params=pltpu.CompilerParams(collective_id=0, has_side_effects=True),
        name="tile",
    )(profiles, cell_width.reshape(1, BLK), basis, table)
    ritz, rows, cols = pl.pallas_call(
        functools.partial(finish_kernel, cells=landmarks.shape[0] * BLK),
        out_shape=(
            jax.ShapeDtypeStruct((COLS, BLK), f32),
            jax.ShapeDtypeStruct((NC, BLK), f32),
            jax.ShapeDtypeStruct((CP, BLK), f32),
        ),
        in_specs=[vmem] * 4,
        out_specs=(vmem,) * 3,
        name="finish",
    )(gram, proj, rows, cols)
    return rows.reshape(-1), cols[:NR].reshape(-1), ritz


def solution(mesh):
    NR, NC = mesh.shape["row"], mesh.shape["col"]
    NX = {32: 4, 4: 2}[NC]
    placed = (
        P(None, ("col", "row")),
        P(("col", "row")),
        P(None, ("col", "row")),
        P("row", "col", None, None),
        P("row", "col"),
        P(),
    )
    return jax.shard_map(
        functools.partial(body, (NR, NC, NX, NC // NX)),
        mesh=mesh,
        in_specs=placed,
        out_specs=(P("row"), P("col"), P(None, ("row", "col"))),
        check_vma=False,
    )
```

```python
import functools

import jax
import jax.numpy as jnp
from jax import lax
from jax.experimental import pallas as pl
from jax.experimental.pallas import tpu as pltpu
from jax.sharding import PartitionSpec as P

BLK = 128
PCS = 50
COLS = 64
SWEEPS = 3
KDIM = 64
CP = 16
RP = 32
SCALE = 512.0
MESH = pl.DeviceIdType.MESH
highest = lax.Precision.HIGHEST
f32 = jnp.float32
bf16 = jnp.bfloat16

ROW, COL, ROWKEY, COLKEY, KEEP, LAST, HAS = range(7)


def slot_table(lists_ref, count, table_ref):
    slots = lists_ref.shape[-1]
    lane = lax.broadcasted_iota(jnp.int32, (1, slots), 1)
    live = (lane < count).astype(jnp.int32)
    packed = live * 1024 + lists_ref[0, 0, 0:1, :] * 32 + lists_ref[0, 0, 1:2, :]
    down = jnp.broadcast_to(packed, (slots, slots)).T
    number = lax.broadcasted_iota(jnp.int32, (slots, slots), 0)
    across = lax.broadcasted_iota(jnp.int32, (slots, slots), 1)
    unlive = lambda v: jnp.where(v >= 1024, (v >> 5) & 31, RP)
    key_across = unlive(packed) * slots + lane
    key_down = unlive(down) * slots + number
    rank = jnp.sum((key_down < key_across).astype(jnp.int32), axis=0, keepdims=True)
    place = jnp.broadcast_to(rank, (slots, slots)).T == across
    order = jnp.sum(jnp.where(place, down, 0), axis=0, keepdims=True)
    rowkey = unlive(order)
    rows_down = unlive(down)
    upto = jnp.sum((rows_down <= across).astype(jnp.int32), axis=0, keepdims=True)
    here = jnp.sum((rows_down == across).astype(jnp.int32), axis=0, keepdims=True)
    key8 = jnp.broadcast_to(rowkey, (8, slots))
    before = jnp.where(lane == 0, -1, pltpu.roll(key8, 1, 1)[0:1])
    table_ref[ROW : ROW + 1, :] = (order >> 5) & 31
    table_ref[COL : COL + 1, :] = order & 31
    table_ref[ROWKEY : ROWKEY + 1, :] = rowkey
    table_ref[COLKEY : COLKEY + 1, :] = jnp.where(order >= 1024, order & 31, CP)
    table_ref[KEEP : KEEP + 1, :] = (before == rowkey).astype(jnp.int32)
    table_ref[LAST : LAST + 1, :] = jnp.maximum(upto - 1, 0)
    table_ref[HAS : HAS + 1, :] = jnp.minimum(here, 1)


def tile_kernel(
    dims,
    prof_ref,
    width_ref,
    basis_ref,
    lists_ref,
    count_ref,
    marks_ref,
    gram_ref,
    proj_ref,
    rows_ref,
    cols_ref,
    table_ref,
    idx,
    msg32,
    rowout,
    colbuf,
    basisbuf,
    rowbuf,
    left,
    uleft,
    uright,
    hot,
    rsplit,
    csplit,
    sbas,
    aff,
    sums,
    rowsums,
    rowpick,
    share,
    zvec,
    xvec,
    yvec,
    xshare,
    ysend,
    yshare,
    gparts,
    zgram,
    xgram,
    ygram,
    zall,
    send_sem,
    recv_sem,
):
    NR, NC, NX, NY, slots = dims
    me_r = lax.axis_index("row")
    me_c = lax.axis_index("col")
    me_x = me_c // NY
    me_y = me_c % NY
    own_block = (me_c % 2) * NR + me_r
    to_r = me_c // 2
    to_x = own_block // NY
    own_y = lax.rem(own_block, NY)
    stays = (to_r == me_r) & (to_x == me_x)

    def zdev(d):
        return (lax.rem(me_r + d, NR), me_c)

    def xdev(d):
        return (me_r, lax.rem(me_x + d, NX) * NY + me_y)

    def ydev(d):
        return (me_r, me_x * NY + lax.rem(me_y + d, NY))

    awaited = {}

    def expect(region, number):
        awaited[number] = region

        def wait():
            del awaited[number]
            pltpu.make_async_copy(region, region, recv_sem.at[number]).wait()

        return wait

    def drain():
        pl.when(stays)(lambda: moved(NY - 1))
        pl.when(jnp.logical_not(stays))(lambda: moved(NY))
        for number, region in list(awaited.items()):
            pltpu.make_async_copy(region, region, recv_sem.at[number]).wait()
        for region, number in sent:
            pltpu.make_async_copy(region, region, send_sem.at[number]).wait()

    groups = {"z": (NR, zdev), "x": (NX, xdev), "y": (NY, ydev)}
    sent = []

    def push(axis, src_of, dst, number):
        size, device = groups[axis]
        for d in range(1, size):
            pltpu.make_async_remote_copy(
                src_ref=src_of(d),
                dst_ref=dst.at[d],
                send_sem=send_sem.at[number],
                recv_sem=recv_sem.at[number],
                device_id=device(d),
                device_id_type=MESH,
            ).start()
        region = dst.at[pl.ds(1, size - 1)]
        sent.append((region, number))
        return expect(region, number)

    prof = prof_ref[...].astype(f32)
    half = jnp.sum(prof * prof, axis=0, keepdims=True) * -0.5
    h1 = half.astype(bf16).astype(f32)
    h2 = (half - h1).astype(bf16).astype(f32)
    h3 = half - h1 - h2
    width = width_ref[...].astype(f32)
    ones = jnp.ones((1, BLK), f32)
    msg32[...] = jnp.zeros_like(msg32)
    for side in range(2):
        msg32[side, 0:PCS, :] = prof
        a, b = (50, 53) if side == 0 else (53, 50)
        msg32[side, a : a + 1, :] = h1
        msg32[side, a + 1 : a + 2, :] = h2
        msg32[side, a + 2 : a + 3, :] = h3
        for n in range(3):
            msg32[side, b + n : b + n + 1, :] = ones
        w = 56 + side
        msg32[side, w : w + 1, :] = width
    colbuf[0] = msg32[1].astype(bf16)
    basisbuf[0] = basis_ref[...]
    outgoing = rowout.at[0]
    rowout[0] = msg32[0].astype(bf16)

    barrier = pltpu.get_barrier_semaphore()
    for size, device in groups.values():
        for d in range(1, size):
            pl.semaphore_signal(barrier, inc=1, device_id=device(d), device_id_type=MESH)

    for n in range(NY):
        block = me_x * NY + n
        source = (lax.rem(block, NR), 2 * me_r + block // NR)

        @pl.when((source[0] != me_r) | (source[1] != me_c))
        def _(source=source):
            pl.semaphore_signal(barrier, inc=1, device_id=source, device_id_type=MESH)

    near = NR + NX + NY - 3
    far = NY - stays.astype(jnp.int32)

    it = lax.broadcasted_iota(jnp.int32, (2 * CP, BLK), 0)

    def tables(k, carry):
        hot[k] = ((it == k) | (it == k + CP)).astype(f32).astype(bf16)
        return carry

    lax.fori_loop(0, CP, tables, 0)
    hot[CP] = jnp.zeros((2 * CP, BLK), bf16)

    slot_table(lists_ref, count_ref[0, 0], table_ref)
    tabled = pltpu.make_async_copy(table_ref, idx, recv_sem.at[20])
    tabled.start()
    pl.semaphore_wait(barrier, near + far)

    for n in range(NY):
        here = stays & (me_y == n)

        @pl.when(jnp.logical_not(here))
        def _(n=n):
            pltpu.make_async_remote_copy(
                src_ref=rowout.at[0],
                dst_ref=rowbuf.at[own_y],
                send_sem=send_sem.at[0],
                recv_sem=recv_sem.at[0],
                device_id=(to_r, to_x * NY + n),
                device_id_type=MESH,
            ).start()

        @pl.when(here)
        def _():
            pltpu.make_async_copy(rowout.at[0], rowbuf.at[own_y], recv_sem.at[0]).start()

    wait_col = push("z", lambda d: colbuf.at[0], colbuf, 1)
    own_rows = rowbuf.at[pl.ds(0, NY)]
    pltpu.make_async_copy(own_rows, own_rows, recv_sem.at[0]).wait()

    def moved(blocks):
        region = rowbuf.at[pl.ds(0, blocks)]
        pltpu.make_async_copy(region, region, send_sem.at[0]).wait()

    for d in range(1, NX):
        pltpu.make_async_remote_copy(
            src_ref=rowbuf.at[pl.ds(0, NY)],
            dst_ref=rowbuf.at[pl.ds(d * NY, NY)],
            send_sem=send_sem.at[3],
            recv_sem=recv_sem.at[3],
            device_id=xdev(d),
            device_id_type=MESH,
        ).start()
    region_x = rowbuf.at[pl.ds(NY, (NX - 1) * NY)]
    sent.append((region_x, 3))
    wait_rows = expect(region_x, 3)

    wait_col()

    def col_place(j):
        return lax.rem(me_r - j + NR, NR)

    def row_place(i):
        return lax.rem(me_x - i // NY + NX, NX) * NY + lax.rem(i, NY)

    def col_prepare(n, carry):
        turned = colbuf[n].astype(f32).T
        left[n] = turned.astype(bf16)
        w = jnp.broadcast_to(turned[:, 57:58], (BLK, BLK))
        uleft[n] = (2.0 * 1.4426950408889634) / w
        return carry

    lax.fori_loop(0, NR, col_prepare, 0)

    wait_rows()

    def row_prepare(n, carry):
        w = rowbuf[n].astype(f32)[56:57, :]
        uright[n] = jnp.broadcast_to(1.0 / w, (8, BLK))
        return carry

    lax.fori_loop(0, NC, row_prepare, 0)

    tabled.wait()

    pairs = slots // 2

    def build(p, carry):
        for h in range(2):
            j = col_place(idx[COL, 2 * p + h])
            i = row_place(idx[ROW, 2 * p + h])
            d = jnp.dot(left[j], rowbuf[i], preferred_element_type=f32)
            e = d * uleft[j] * uright[i][0:1, :]
            aff[p, :, h * BLK : (h + 1) * BLK] = jnp.exp2(e).astype(bf16)
        return carry

    lax.fori_loop(0, pairs, build, 0, unroll=4)

    def col_pass():
        def step(p, acc):
            s, t = 2 * p, 2 * p + 1
            lhs = jnp.concatenate(
                [
                    rsplit[idx[ROW, s]] * hot[idx[COLKEY, s]],
                    rsplit[idx[ROW, t]] * hot[idx[COLKEY, t]],
                ],
                axis=1,
            )
            return acc + lax.dot_general(
                lhs, aff[p], (((1,), (1,)), ((), ())), preferred_element_type=f32
            )

        acc = lax.fori_loop(0, pairs, step, jnp.zeros((2 * CP, BLK), f32), unroll=8)
        return acc[0:CP] + acc[CP:]

    sub8 = lax.broadcasted_iota(jnp.int32, (8, BLK), 0)

    def row_pass():
        def step(p, acc):
            s, t = 2 * p, 2 * p + 1
            lhs = csplit[idx[COL, s], 0] + csplit[idx[COL, t], 1]
            both = jnp.dot(lhs, aff[p], preferred_element_type=f32)
            acc = acc * idx[KEEP, s].astype(f32) + jnp.where(sub8 < 2, both[:, :BLK], 0.0)
            rowsums[s] = acc
            acc = acc * idx[KEEP, t].astype(f32) + jnp.where(sub8 < 2, 0.0, both[:, BLK:])
            rowsums[t] = acc
            return acc

        lax.fori_loop(0, pairs, step, jnp.zeros((8, BLK), f32), unroll=8)
        for i in range(NC):
            rowpick[i] = rowsums[idx[LAST, i]] * idx[HAS, i].astype(f32)
        return jnp.sum(rowpick[...], axis=1)

    def col_total(k, part):
        buf = zvec.at[k]
        buf[0] = part
        wait = push("z", lambda d: buf.at[0], buf, 5 + k)
        wait()
        total = buf[lax.rem(me_r, NR)]
        for r in range(1, NR):
            total = total + buf[lax.rem(me_r - r + NR, NR)]
        return total

    def row_over_x(k, part):
        bx = xvec.at[k]
        bx[0] = part
        wait = push("x", lambda d: bx.at[0], bx, 8 + k)

        def finish():
            wait()
            total = bx[me_x]
            for x in range(1, NX):
                total = total + bx[lax.rem(me_x - x + NX, NX)]
            return total

        return finish

    def row_over_y(k, part):
        by = yvec.at[k]
        by[0] = part
        wait = push("y", lambda d: by.at[0], by, 11 + k)

        def finish():
            wait()
            total = by[me_y]
            for y in range(1, NY):
                total = total + by[lax.rem(me_y - y + NY, NY)]
            return total

        return finish

    def row_total(k, part):
        return row_over_y(k, row_over_x(k, part)())()

    def split(v):
        hi = v.astype(bf16).astype(f32)
        return hi, v - hi

    def spread_rows(vec):
        for n in range(NC):
            hi, lo = split(jnp.broadcast_to(vec[n : n + 1, :], (CP, BLK)))
            rsplit[n] = jnp.concatenate([hi, lo], axis=0).astype(bf16)

    def spread_cols(vec):
        for n in range(NR):
            hi, lo = split(jnp.broadcast_to(vec[n : n + 1, :], (8, BLK)))
            even = jnp.where(sub8 % 2 == 0, hi, lo)
            csplit[n, 0] = jnp.where(sub8 < 2, even, 0.0).astype(bf16)
            csplit[n, 1] = jnp.where((sub8 >= 2) & (sub8 < 4), even, 0.0).astype(bf16)

    first = lax.broadcasted_iota(jnp.int32, (NC, 2 * CP, BLK), 1)
    rsplit[...] = jnp.where(first < CP, 1.0, 0.0).astype(bf16)
    for k in range(SWEEPS):
        part = col_pass()
        cols_ref[...] = part
        cvec = SCALE / col_total(k, part)
        spread_cols(cvec)
        if k < SWEEPS - 1:
            part = row_pass()
            rows_ref[...] = part
            if k == 0:
                wait_basis = push("z", lambda d: basisbuf.at[0], basisbuf, 4)
            rvec = SCALE / row_total(k, part)
            spread_rows(rvec)
    cols_ref[...] = cvec

    over_x = row_over_x(SWEEPS - 1, row_pass())
    wait_basis()
    for j in range(NR):
        block = basisbuf[col_place(j)].astype(f32) * cvec[j : j + 1, :]
        sbas[j] = block.astype(bf16)

    def subspace(p, acc):
        for h in range(2):
            s = 2 * p + h
            product = jnp.dot(
                sbas[idx[COL, s]],
                aff[p, :, h * BLK : (h + 1) * BLK],
                preferred_element_type=f32,
            )
            acc = acc * idx[KEEP, s].astype(f32) + product
            sums[s] = acc
        return acc

    lax.fori_loop(0, pairs, subspace, jnp.zeros((COLS, BLK), f32), unroll=4)

    def pick(i, carry):
        share[i] = (sums[idx[LAST, i]] * idx[HAS, i].astype(f32)).astype(share.dtype)
        return carry

    lax.fori_loop(0, NC, pick, 0)

    def own_part(x):
        return share.at[pl.ds(x * NY, NY)]

    over_y = row_over_y(SWEEPS - 1, over_x())
    wait_share = push("x", lambda d: own_part(lax.rem(me_x + d, NX)), xshare, 14)
    rvec = SCALE / over_y()
    rows_ref[...] = rvec
    wait_share()

    def add_x(n, carry):
        total = share[me_x * NY + n].astype(f32)
        for d in range(1, NX):
            total = total + xshare[d, n].astype(f32)
        ysend[n] = total
        return carry

    lax.fori_loop(0, NY, add_x, 0)
    push("y", lambda d: ysend.at[lax.rem(me_y + d, NY)], yshare, 15)()
    total = ysend[me_y]
    for d in range(1, NY):
        total = total + yshare[d]
    proj = total * (rows_ref[pl.ds(me_c, 1), :] * (1.0 / SCALE))
    proj_ref[...] = proj

    cells = me_r * NC + me_c
    mark = jnp.int32(0)
    for n in range(marks_ref.shape[0]):
        mark = mark + (marks_ref[n] == cells).astype(jnp.int32)
    masked = proj * mark.astype(f32)
    gram = lax.dot_general(
        masked, masked, (((1,), (1,)), ((), ())), precision=highest, preferred_element_type=f32
    )
    half_rows = COLS // 2
    packed = jnp.concatenate([gram[:half_rows], gram[half_rows:]], axis=1)
    part_rows = half_rows // NR
    for n in range(NR):
        gparts[n] = packed[n * part_rows : (n + 1) * part_rows]
    zgram[0] = gparts[me_r]
    push("z", lambda d: gparts.at[lax.rem(me_r + d, NR)], zgram, 16)()
    total = zgram[me_r]
    for n in range(1, NR):
        total = total + zgram[lax.rem(me_r - n + NR, NR)]
    for axis, buf, number, size, me in (
        ("x", xgram, 17, NX, me_x),
        ("y", ygram, 18, NY, me_y),
    ):
        buf[0] = total
        push(axis, lambda d, buf=buf: buf.at[0], buf, number)()
        total = buf[me]
        for n in range(1, size):
            total = total + buf[lax.rem(me - n + size, size)]
    zall[0] = total
    push("z", lambda d: zall.at[0], zall, 19)()
    for n in range(NR):
        gram_ref[n * part_rows : (n + 1) * part_rows, :] = zall[lax.rem(me_r - n + NR, NR)]
    drain()


def finish_kernel(gram_ref, proj_ref, rows_in, cols_in, ritz_ref, rows_ref, cols_ref, *, cells):
    rows_ref[...] = rows_in[...]
    cols_ref[...] = cols_in[...]
    half_rows = COLS // 2
    packed = gram_ref[...] * (1.0 / cells)
    gram = jnp.concatenate([packed[:, :COLS], packed[:, COLS:]], axis=0)
    proj = proj_ref[...]
    gs = [gram[n : n + 8] for n in range(0, COLS, 8)]
    ps = [proj[n : n + 8] for n in range(0, COLS, 8)]
    wide = 4
    for k in range(0, COLS, wide):
        top, row = k // 8, k % 8
        cols = [
            [jnp.broadcast_to(g[:, k + m : k + m + 1], (8, BLK)) for g in gs[top:]]
            for m in range(wide)
        ]
        flat = lambda v, i: jnp.broadcast_to(v[row + i : row + i + 1, :], (8, v.shape[1]))
        d = [[flat(cols[m][0], i) for m in range(wide)] for i in range(wide)]
        grow = [flat(gs[top], i) for i in range(wide)]
        prow = [flat(ps[top], i) for i in range(wide)]
        inv = []
        for i in range(wide):
            inv.append(1.0 / d[i][i])
            for j in range(i + 1, wide):
                factor = d[j][i] * inv[i]
                for m in range(j, wide):
                    d[j][m] = d[j][m] - factor * d[i][m]
                    d[m][j] = d[j][m]
                grow[j] = grow[j] - factor[:, :COLS] * grow[i]
                prow[j] = prow[j] - factor * prow[i]
                cols[j] = [a - factor * b for a, b in zip(cols[j], cols[i])]
        for i in range(wide):
            scale = 1.0 / jnp.sqrt(d[i][i][0:1])
            ritz_ref[k + i : k + i + 1, :] = prow[i][0:1] * scale
        for i in range(wide):
            grow[i] = grow[i] * inv[i][:, :COLS]
            prow[i] = prow[i] * inv[i]
        for n in range(top, COLS // 8):
            for i in range(wide):
                col = cols[i][n - top]
                gs[n] = gs[n] - col[:, :COLS] * grow[i]
                ps[n] = ps[n] - col * prow[i]


def body(mesh_sizes, profiles, cell_width, basis, block_lists, block_counts, landmarks):
    NR, NC, NX, NY = mesh_sizes
    slots = block_lists.shape[-1]
    vmem = pl.BlockSpec(memory_space=pltpu.VMEM)
    smem = pl.BlockSpec(memory_space=pltpu.SMEM)
    half_rows = COLS // 2
    gram, proj, rows, cols = pl.pallas_call(
        functools.partial(tile_kernel, (NR, NC, NX, NY, slots)),
        out_shape=(
            jax.ShapeDtypeStruct((half_rows, BLK), f32),
            jax.ShapeDtypeStruct((COLS, BLK), f32),
            jax.ShapeDtypeStruct((NC, BLK), f32),
            jax.ShapeDtypeStruct((CP, BLK), f32),
        ),
        in_specs=[vmem, vmem, vmem, vmem, smem, smem],
        out_specs=(vmem,) * 4,
        scratch_shapes=[
            pltpu.VMEM((8, slots), jnp.int32),
            pltpu.SMEM((8, slots), jnp.int32),
            pltpu.VMEM((2, KDIM, BLK), f32),
            pltpu.VMEM((1, KDIM, BLK), bf16),
            pltpu.VMEM((NR, KDIM, BLK), bf16),
            pltpu.VMEM((NR, COLS, BLK), bf16),
            pltpu.VMEM((NC, KDIM, BLK), bf16),
            pltpu.VMEM((NR, BLK, KDIM), bf16),
            pltpu.VMEM((NR, BLK, BLK), f32),
            pltpu.VMEM((NC, 8, BLK), f32),
            pltpu.VMEM((CP + 1, 2 * CP, BLK), bf16),
            pltpu.VMEM((NC, 2 * CP, BLK), bf16),
            pltpu.VMEM((NR, 2, 8, BLK), bf16),
            pltpu.VMEM((NR, COLS, BLK), bf16),
            pltpu.VMEM((slots // 2, BLK, 2 * BLK), bf16),
            pltpu.VMEM((slots, COLS, BLK), f32),
            pltpu.VMEM((slots, 8, BLK), f32),
            pltpu.VMEM((NC, 8, BLK), f32),
            pltpu.VMEM((NC, COLS, BLK), f32),
            pltpu.VMEM((SWEEPS, NR, CP, BLK), f32),
            pltpu.VMEM((SWEEPS, NX, NC, BLK), f32),
            pltpu.VMEM((SWEEPS, NY, NC, BLK), f32),
            pltpu.VMEM((NX, NY, COLS, BLK), f32),
            pltpu.VMEM((NY, COLS, BLK), f32),
            pltpu.VMEM((NY, COLS, BLK), f32),
            pltpu.VMEM((NR, half_rows // NR, BLK), f32),
            pltpu.VMEM((NR, half_rows // NR, BLK), f32),
            pltpu.VMEM((NX, half_rows // NR, BLK), f32),
            pltpu.VMEM((NY, half_rows // NR, BLK), f32),
            pltpu.VMEM((NR, half_rows // NR, BLK), f32),
            pltpu.SemaphoreType.DMA((21,)),
            pltpu.SemaphoreType.DMA((21,)),
        ],
        compiler_params=pltpu.CompilerParams(collective_id=0, has_side_effects=True),
        name="tile",
    )(profiles, cell_width.reshape(1, BLK), basis, block_lists, block_counts, landmarks)
    ritz, rows, cols = pl.pallas_call(
        functools.partial(finish_kernel, cells=landmarks.shape[0] * BLK),
        out_shape=(
            jax.ShapeDtypeStruct((COLS, BLK), f32),
            jax.ShapeDtypeStruct((NC, BLK), f32),
            jax.ShapeDtypeStruct((CP, BLK), f32),
        ),
        in_specs=[vmem] * 4,
        out_specs=(vmem,) * 3,
        name="finish",
    )(gram, proj, rows, cols)
    return rows.reshape(-1), cols[:NR].reshape(-1), ritz


def solution(mesh):
    NR, NC = mesh.shape["row"], mesh.shape["col"]
    NX = {32: 4, 4: 2}[NC]
    placed = (
        P(None, ("col", "row")),
        P(("col", "row")),
        P(None, ("col", "row")),
        P("row", "col", None, None),
        P("row", "col"),
        P(),
    )
    return jax.shard_map(
        functools.partial(body, (NR, NC, NX, NC // NX)),
        mesh=mesh,
        in_specs=placed,
        out_specs=(P("row"), P("col"), P(None, ("row", "col"))),
        check_vma=False,
    )
```

```python
import functools

import jax
import jax.numpy as jnp
from jax import lax
from jax.experimental import pallas as pl
from jax.experimental.pallas import tpu as pltpu
from jax.sharding import PartitionSpec as P

BLK = 128
PCS = 50
COLS = 64
SWEEPS = 3
KDIM = 64
CP = 16
RP = 32
SCALE = 512.0
MESH = pl.DeviceIdType.MESH
highest = lax.Precision.HIGHEST
f32 = jnp.float32
bf16 = jnp.bfloat16

ROW, COL, ROWKEY, COLKEY, KEEP, LAST, HAS = range(7)


def slot_table(lists_ref, count, table_ref):
    slots = lists_ref.shape[-1]
    lane = lax.broadcasted_iota(jnp.int32, (1, slots), 1)
    live = (lane < count).astype(jnp.int32)
    packed = live * 1024 + lists_ref[0, 0, 0:1, :] * 32 + lists_ref[0, 0, 1:2, :]
    down = jnp.broadcast_to(packed, (slots, slots)).T
    number = lax.broadcasted_iota(jnp.int32, (slots, slots), 0)
    across = lax.broadcasted_iota(jnp.int32, (slots, slots), 1)
    unlive = lambda v: jnp.where(v >= 1024, (v >> 5) & 31, RP)
    key_across = unlive(packed) * slots + lane
    key_down = unlive(down) * slots + number
    rank = jnp.sum((key_down < key_across).astype(jnp.int32), axis=0, keepdims=True)
    place = jnp.broadcast_to(rank, (slots, slots)).T == across
    order = jnp.sum(jnp.where(place, down, 0), axis=0, keepdims=True)
    rowkey = unlive(order)
    rows_down = unlive(down)
    upto = jnp.sum((rows_down <= across).astype(jnp.int32), axis=0, keepdims=True)
    here = jnp.sum((rows_down == across).astype(jnp.int32), axis=0, keepdims=True)
    key8 = jnp.broadcast_to(rowkey, (8, slots))
    before = jnp.where(lane == 0, -1, pltpu.roll(key8, 1, 1)[0:1])
    table_ref[ROW : ROW + 1, :] = (order >> 5) & 31
    table_ref[COL : COL + 1, :] = order & 31
    table_ref[ROWKEY : ROWKEY + 1, :] = rowkey
    table_ref[COLKEY : COLKEY + 1, :] = jnp.where(order >= 1024, order & 31, CP)
    table_ref[KEEP : KEEP + 1, :] = (before == rowkey).astype(jnp.int32)
    table_ref[LAST : LAST + 1, :] = jnp.maximum(upto - 1, 0)
    table_ref[HAS : HAS + 1, :] = jnp.minimum(here, 1)


def tile_kernel(
    dims,
    prof_ref,
    width_ref,
    basis_ref,
    lists_ref,
    count_ref,
    marks_ref,
    gram_ref,
    proj_ref,
    rows_ref,
    cols_ref,
    table_ref,
    idx,
    msg32,
    rowout,
    colbuf,
    basisbuf,
    rowbuf,
    left,
    uleft,
    uright,
    hot,
    rsplit,
    csplit,
    sbas,
    aff,
    sums,
    rowsums,
    rowpick,
    share,
    zvec,
    xvec,
    yvec,
    xshare,
    ysend,
    yshare,
    rlast,
    markx,
    gotx,
    marky,
    goty,
    gparts,
    zgram,
    xgram,
    ygram,
    zall,
    send_sem,
    recv_sem,
):
    NR, NC, NX, NY, slots = dims
    me_r = lax.axis_index("row")
    me_c = lax.axis_index("col")
    me_x = me_c // NY
    me_y = me_c % NY
    own_block = (me_c % 2) * NR + me_r
    to_r = me_c // 2
    to_x = own_block // NY
    own_y = lax.rem(own_block, NY)
    stays = (to_r == me_r) & (to_x == me_x)

    def zdev(d):
        return (lax.rem(me_r + d, NR), me_c)

    def xdev(d):
        return (me_r, lax.rem(me_x + d, NX) * NY + me_y)

    def ydev(d):
        return (me_r, me_x * NY + lax.rem(me_y + d, NY))

    awaited = {}

    def expect(region, number):
        awaited[number] = region

        def wait():
            del awaited[number]
            pltpu.make_async_copy(region, region, recv_sem.at[number]).wait()

        return wait

    def drain():
        pl.when(stays)(lambda: moved(NY - 1))
        pl.when(jnp.logical_not(stays))(lambda: moved(NY))
        for number, region in list(awaited.items()):
            pltpu.make_async_copy(region, region, recv_sem.at[number]).wait()
        for region, number in sent:
            pltpu.make_async_copy(region, region, send_sem.at[number]).wait()

    groups = {"z": (NR, zdev), "x": (NX, xdev), "y": (NY, ydev)}
    sent = []

    def push(axis, src_of, dst, number):
        size, device = groups[axis]
        for d in range(1, size):
            pltpu.make_async_remote_copy(
                src_ref=src_of(d),
                dst_ref=dst.at[d],
                send_sem=send_sem.at[number],
                recv_sem=recv_sem.at[number],
                device_id=device(d),
                device_id_type=MESH,
            ).start()
        region = dst.at[pl.ds(1, size - 1)]
        sent.append((region, number))
        return expect(region, number)

    prof = prof_ref[...].astype(f32)
    half = jnp.sum(prof * prof, axis=0, keepdims=True) * -0.5
    h1 = half.astype(bf16).astype(f32)
    h2 = (half - h1).astype(bf16).astype(f32)
    h3 = half - h1 - h2
    width = width_ref[...].astype(f32)
    ones = jnp.ones((1, BLK), f32)
    msg32[...] = jnp.zeros_like(msg32)
    for side in range(2):
        msg32[side, 0:PCS, :] = prof
        a, b = (50, 53) if side == 0 else (53, 50)
        msg32[side, a : a + 1, :] = h1
        msg32[side, a + 1 : a + 2, :] = h2
        msg32[side, a + 2 : a + 3, :] = h3
        for n in range(3):
            msg32[side, b + n : b + n + 1, :] = ones
        w = 56 + side
        msg32[side, w : w + 1, :] = width
    colbuf[0] = msg32[1].astype(bf16)
    basisbuf[0] = basis_ref[...]
    outgoing = rowout.at[0]
    rowout[0] = msg32[0].astype(bf16)

    barrier = pltpu.get_barrier_semaphore()
    for size, device in groups.values():
        for d in range(1, size):
            pl.semaphore_signal(barrier, inc=1, device_id=device(d), device_id_type=MESH)

    for n in range(NY):
        block = me_x * NY + n
        source = (lax.rem(block, NR), 2 * me_r + block // NR)

        @pl.when((source[0] != me_r) | (source[1] != me_c))
        def _(source=source):
            pl.semaphore_signal(barrier, inc=1, device_id=source, device_id_type=MESH)

    near = NR + NX + NY - 3
    far = NY - stays.astype(jnp.int32)

    it = lax.broadcasted_iota(jnp.int32, (2 * CP, BLK), 0)

    def tables(k, carry):
        hot[k] = ((it == k) | (it == k + CP)).astype(f32).astype(bf16)
        return carry

    lax.fori_loop(0, CP, tables, 0)
    hot[CP] = jnp.zeros((2 * CP, BLK), bf16)

    pl.semaphore_wait(barrier, near + far)

    for n in range(NY):
        here = stays & (me_y == n)

        @pl.when(jnp.logical_not(here))
        def _(n=n):
            pltpu.make_async_remote_copy(
                src_ref=rowout.at[0],
                dst_ref=rowbuf.at[own_y],
                send_sem=send_sem.at[0],
                recv_sem=recv_sem.at[0],
                device_id=(to_r, to_x * NY + n),
                device_id_type=MESH,
            ).start()

        @pl.when(here)
        def _():
            pltpu.make_async_copy(rowout.at[0], rowbuf.at[own_y], recv_sem.at[0]).start()

    wait_col = push("z", lambda d: colbuf.at[0], colbuf, 1)
    slot_table(lists_ref, count_ref[0, 0], table_ref)
    tabled = pltpu.make_async_copy(table_ref, idx, recv_sem.at[20])
    tabled.start()
    tabled.wait()
    own_rows = rowbuf.at[pl.ds(0, NY)]
    pltpu.make_async_copy(own_rows, own_rows, recv_sem.at[0]).wait()

    def moved(blocks):
        region = rowbuf.at[pl.ds(0, blocks)]
        pltpu.make_async_copy(region, region, send_sem.at[0]).wait()

    for d in range(1, NX):
        pltpu.make_async_remote_copy(
            src_ref=rowbuf.at[pl.ds(0, NY)],
            dst_ref=rowbuf.at[pl.ds(d * NY, NY)],
            send_sem=send_sem.at[3],
            recv_sem=recv_sem.at[3],
            device_id=xdev(d),
            device_id_type=MESH,
        ).start()
    region_x = rowbuf.at[pl.ds(NY, (NX - 1) * NY)]
    sent.append((region_x, 3))
    wait_rows = expect(region_x, 3)

    wait_col()

    def col_place(j):
        return lax.rem(me_r - j + NR, NR)

    def row_place(i):
        return lax.rem(me_x - i // NY + NX, NX) * NY + lax.rem(i, NY)

    def col_prepare(n, carry):
        turned = colbuf[n].astype(f32).T
        left[n] = turned.astype(bf16)
        w = jnp.broadcast_to(turned[:, 57:58], (BLK, BLK))
        uleft[n] = (2.0 * 1.4426950408889634) / w
        return carry

    lax.fori_loop(0, NR, col_prepare, 0)

    wait_rows()

    def row_prepare(n, carry):
        w = rowbuf[n].astype(f32)[56:57, :]
        uright[n] = jnp.broadcast_to(1.0 / w, (8, BLK))
        return carry

    lax.fori_loop(0, NC, row_prepare, 0)

    pairs = slots // 2

    def build(p, carry):
        for h in range(2):
            j = col_place(idx[COL, 2 * p + h])
            i = row_place(idx[ROW, 2 * p + h])
            d = jnp.dot(left[j], rowbuf[i], preferred_element_type=f32)
            e = d * uleft[j] * uright[i][0:1, :]
            aff[p, :, h * BLK : (h + 1) * BLK] = jnp.exp2(e).astype(bf16)
        return carry

    lax.fori_loop(0, pairs, build, 0, unroll=4)

    def col_pass():
        def step(p, acc):
            s, t = 2 * p, 2 * p + 1
            lhs = jnp.concatenate(
                [
                    rsplit[idx[ROW, s]] * hot[idx[COLKEY, s]],
                    rsplit[idx[ROW, t]] * hot[idx[COLKEY, t]],
                ],
                axis=1,
            )
            return acc + lax.dot_general(
                lhs, aff[p], (((1,), (1,)), ((), ())), preferred_element_type=f32
            )

        acc = lax.fori_loop(0, pairs, step, jnp.zeros((2 * CP, BLK), f32), unroll=8)
        return acc[0:CP] + acc[CP:]

    sub8 = lax.broadcasted_iota(jnp.int32, (8, BLK), 0)

    def row_pass():
        def step(p, acc):
            s, t = 2 * p, 2 * p + 1
            lhs = csplit[idx[COL, s], 0] + csplit[idx[COL, t], 1]
            both = jnp.dot(lhs, aff[p], preferred_element_type=f32)
            acc = acc * idx[KEEP, s].astype(f32) + jnp.where(sub8 < 2, both[:, :BLK], 0.0)
            rowsums[s] = acc
            acc = acc * idx[KEEP, t].astype(f32) + jnp.where(sub8 < 2, 0.0, both[:, BLK:])
            rowsums[t] = acc
            return acc

        lax.fori_loop(0, pairs, step, jnp.zeros((8, BLK), f32), unroll=8)
        for i in range(NC):
            rowpick[i] = rowsums[idx[LAST, i]] * idx[HAS, i].astype(f32)
        return jnp.sum(rowpick[...], axis=1)

    def col_total(k, part):
        buf = zvec.at[k]
        buf[0] = part
        wait = push("z", lambda d: buf.at[0], buf, 5 + k)
        wait()
        total = buf[lax.rem(me_r, NR)]
        for r in range(1, NR):
            total = total + buf[lax.rem(me_r - r + NR, NR)]
        return total

    def row_over_x(k, part):
        bx = xvec.at[k]
        bx[0] = part
        wait = push("x", lambda d: bx.at[0], bx, 8 + k)

        def finish():
            wait()
            total = bx[me_x]
            for x in range(1, NX):
                total = total + bx[lax.rem(me_x - x + NX, NX)]
            return total

        return finish

    def row_over_y(k, part):
        by = yvec.at[k]
        by[0] = part
        wait = push("y", lambda d: by.at[0], by, 11 + k)

        def finish():
            wait()
            total = by[me_y]
            for y in range(1, NY):
                total = total + by[lax.rem(me_y - y + NY, NY)]
            return total

        return finish

    def row_total(k, part):
        return row_over_y(k, row_over_x(k, part)())()

    def split(v):
        hi = v.astype(bf16).astype(f32)
        return hi, v - hi

    def spread_rows(vec):
        for n in range(NC):
            hi, lo = split(jnp.broadcast_to(vec[n : n + 1, :], (CP, BLK)))
            rsplit[n] = jnp.concatenate([hi, lo], axis=0).astype(bf16)

    def spread_cols(vec):
        for n in range(NR):
            hi, lo = split(jnp.broadcast_to(vec[n : n + 1, :], (8, BLK)))
            even = jnp.where(sub8 % 2 == 0, hi, lo)
            csplit[n, 0] = jnp.where(sub8 < 2, even, 0.0).astype(bf16)
            csplit[n, 1] = jnp.where((sub8 >= 2) & (sub8 < 4), even, 0.0).astype(bf16)

    first = lax.broadcasted_iota(jnp.int32, (NC, 2 * CP, BLK), 1)
    rsplit[...] = jnp.where(first < CP, 1.0, 0.0).astype(bf16)
    for k in range(SWEEPS):
        part = col_pass()
        cols_ref[...] = part
        cvec = SCALE / col_total(k, part)
        spread_cols(cvec)
        if k < SWEEPS - 1:
            part = row_pass()
            rows_ref[...] = part
            if k == 0:
                wait_basis = push("z", lambda d: basisbuf.at[0], basisbuf, 4)
            rvec = SCALE / row_total(k, part)
            spread_rows(rvec)
    cols_ref[...] = cvec

    over_x = row_over_x(SWEEPS - 1, row_pass())
    wait_basis()
    for j in range(NR):
        block = basisbuf[col_place(j)].astype(f32) * cvec[j : j + 1, :]
        sbas[j] = block.astype(bf16)

    def subspace(p, acc):
        for h in range(2):
            s = 2 * p + h
            product = jnp.dot(
                sbas[idx[COL, s]],
                aff[p, :, h * BLK : (h + 1) * BLK],
                preferred_element_type=f32,
            )
            acc = acc * idx[KEEP, s].astype(f32) + product
            sums[s] = acc
        return acc

    lax.fori_loop(0, pairs, subspace, jnp.zeros((COLS, BLK), f32), unroll=4)

    def pick(i, carry):
        share[i] = sums[idx[LAST, i]] * idx[HAS, i].astype(f32)
        return carry

    lax.fori_loop(0, NC, pick, 0)

    marked = [jnp.clip(marks_ref[2 * me_r + h] - me_r * NC, 0, NC - 1) for h in range(2)]
    both = jnp.concatenate([share[n] for n in marked], axis=0).T
    x_cells, y_cells = BLK // NX, BLK // NC
    for x in range(NX):
        markx[x] = both[x * x_cells : (x + 1) * x_cells]
    wait_markx = push("x", lambda d: markx.at[lax.rem(me_x + d, NX)], gotx, 21)
    over_y = row_over_y(SWEEPS - 1, over_x())

    def own_part(x):
        return share.at[pl.ds(x * NY, NY)]

    wait_share = push("x", lambda d: own_part(lax.rem(me_x + d, NX)), xshare, 14)
    wait_markx()
    total = markx[me_x]
    for d in range(1, NX):
        total = total + gotx[d]
    for y in range(NY):
        marky[y] = total[y * y_cells : (y + 1) * y_cells]
    wait_marky = push("y", lambda d: marky.at[lax.rem(me_y + d, NY)], goty, 22)
    rvec = SCALE / over_y()
    rows_ref[...] = rvec
    for n in range(NC):
        rlast[n] = jnp.broadcast_to(rvec[n : n + 1, :], (max(8, y_cells), BLK))
    first_cell = me_x * x_cells + me_y * y_cells
    lanes = lax.broadcasted_iota(jnp.int32, (y_cells, BLK), 1)
    own = lanes == first_cell + lax.broadcasted_iota(jnp.int32, (y_cells, BLK), 0)
    scales = [
        jnp.sum(jnp.where(own, rlast[n][0:y_cells], 0.0), axis=1, keepdims=True)
        for n in marked
    ]
    wait_marky()
    total = marky[me_y]
    for d in range(1, NY):
        total = total + goty[d]
    masked = total * (jnp.where(lanes < COLS, scales[0], scales[1]) * (1.0 / SCALE))
    gram = jnp.zeros((COLS, COLS), f32)
    for h in range(2):
        cells = masked[:, h * COLS : (h + 1) * COLS]
        gram = gram + lax.dot_general(
            cells, cells, (((0,), (0,)), ((), ())), precision=highest, preferred_element_type=f32
        )
    half_rows = COLS // 2
    packed = jnp.concatenate([gram[:half_rows], gram[half_rows:]], axis=1)
    part_rows = half_rows // NR
    for n in range(NR):
        gparts[n] = packed[n * part_rows : (n + 1) * part_rows]
    zgram[0] = gparts[me_r]
    push("z", lambda d: gparts.at[lax.rem(me_r + d, NR)], zgram, 16)()
    total = zgram[me_r]
    for n in range(1, NR):
        total = total + zgram[lax.rem(me_r - n + NR, NR)]

    def over(axis, buf, number, value):
        buf[0] = value
        return push(axis, lambda d: buf.at[0], buf, number)

    def added(buf, size, me):
        total = buf[me]
        for n in range(1, size):
            total = total + buf[lax.rem(me - n + size, size)]
        return total

    over("y", ygram, 18, total)()
    wait_xgram = over("x", xgram, 17, added(ygram, NY, me_y))
    wait_share()

    def add_x(n, carry):
        total = share[me_x * NY + n]
        for d in range(1, NX):
            total = total + xshare[d, n]
        ysend[n] = total
        return carry

    lax.fori_loop(0, NY, add_x, 0)
    wait_yshare = push("y", lambda d: ysend.at[lax.rem(me_y + d, NY)], yshare, 15)
    wait_xgram()
    wait_zall = over("z", zall, 19, added(xgram, NX, me_x))
    wait_yshare()
    total = ysend[me_y]
    for d in range(1, NY):
        total = total + yshare[d]
    proj_ref[...] = total * (rows_ref[pl.ds(me_c, 1), :] * (1.0 / SCALE))
    wait_zall()
    for n in range(NR):
        gram_ref[n * part_rows : (n + 1) * part_rows, :] = zall[lax.rem(me_r - n + NR, NR)]
    drain()


def finish_kernel(gram_ref, proj_ref, rows_in, cols_in, ritz_ref, rows_ref, cols_ref, *, cells):
    rows_ref[...] = rows_in[...]
    cols_ref[...] = cols_in[...]
    half_rows = COLS // 2
    packed = gram_ref[...] * (1.0 / cells)
    gram = jnp.concatenate([packed[:, :COLS], packed[:, COLS:]], axis=0)
    proj = proj_ref[...]
    gs = [gram[n : n + 8] for n in range(0, COLS, 8)]
    ps = [proj[n : n + 8] for n in range(0, COLS, 8)]
    wide = 4
    for k in range(0, COLS, wide):
        top, row = k // 8, k % 8
        cols = [
            [jnp.broadcast_to(g[:, k + m : k + m + 1], (8, BLK)) for g in gs[top:]]
            for m in range(wide)
        ]
        flat = lambda v, i: jnp.broadcast_to(v[row + i : row + i + 1, :], (8, v.shape[1]))
        d = [[flat(cols[m][0], i) for m in range(wide)] for i in range(wide)]
        grow = [flat(gs[top], i) for i in range(wide)]
        prow = [flat(ps[top], i) for i in range(wide)]
        inv = []
        for i in range(wide):
            inv.append(1.0 / d[i][i])
            for j in range(i + 1, wide):
                factor = d[j][i] * inv[i]
                for m in range(j, wide):
                    d[j][m] = d[j][m] - factor * d[i][m]
                    d[m][j] = d[j][m]
                grow[j] = grow[j] - factor[:, :COLS] * grow[i]
                prow[j] = prow[j] - factor * prow[i]
                cols[j] = [a - factor * b for a, b in zip(cols[j], cols[i])]
        for i in range(wide):
            scale = 1.0 / jnp.sqrt(d[i][i][0:1])
            ritz_ref[k + i : k + i + 1, :] = prow[i][0:1] * scale
        for i in range(wide):
            grow[i] = grow[i] * inv[i][:, :COLS]
            prow[i] = prow[i] * inv[i]
        for n in range(top, COLS // 8):
            for i in range(wide):
                col = cols[i][n - top]
                gs[n] = gs[n] - col[:, :COLS] * grow[i]
                ps[n] = ps[n] - col * prow[i]


def body(mesh_sizes, profiles, cell_width, basis, block_lists, block_counts, landmarks):
    NR, NC, NX, NY = mesh_sizes
    slots = block_lists.shape[-1]
    vmem = pl.BlockSpec(memory_space=pltpu.VMEM)
    smem = pl.BlockSpec(memory_space=pltpu.SMEM)
    half_rows = COLS // 2
    gram, proj, rows, cols = pl.pallas_call(
        functools.partial(tile_kernel, (NR, NC, NX, NY, slots)),
        out_shape=(
            jax.ShapeDtypeStruct((half_rows, BLK), f32),
            jax.ShapeDtypeStruct((COLS, BLK), f32),
            jax.ShapeDtypeStruct((NC, BLK), f32),
            jax.ShapeDtypeStruct((CP, BLK), f32),
        ),
        in_specs=[vmem, vmem, vmem, vmem, smem, smem],
        out_specs=(vmem,) * 4,
        scratch_shapes=[
            pltpu.VMEM((8, slots), jnp.int32),
            pltpu.SMEM((8, slots), jnp.int32),
            pltpu.VMEM((2, KDIM, BLK), f32),
            pltpu.VMEM((1, KDIM, BLK), bf16),
            pltpu.VMEM((NR, KDIM, BLK), bf16),
            pltpu.VMEM((NR, COLS, BLK), bf16),
            pltpu.VMEM((NC, KDIM, BLK), bf16),
            pltpu.VMEM((NR, BLK, KDIM), bf16),
            pltpu.VMEM((NR, BLK, BLK), f32),
            pltpu.VMEM((NC, 8, BLK), f32),
            pltpu.VMEM((CP + 1, 2 * CP, BLK), bf16),
            pltpu.VMEM((NC, 2 * CP, BLK), bf16),
            pltpu.VMEM((NR, 2, 8, BLK), bf16),
            pltpu.VMEM((NR, COLS, BLK), bf16),
            pltpu.VMEM((slots // 2, BLK, 2 * BLK), bf16),
            pltpu.VMEM((slots, COLS, BLK), f32),
            pltpu.VMEM((slots, 8, BLK), f32),
            pltpu.VMEM((NC, 8, BLK), f32),
            pltpu.VMEM((NC, COLS, BLK), f32),
            pltpu.VMEM((SWEEPS, NR, CP, BLK), f32),
            pltpu.VMEM((SWEEPS, NX, NC, BLK), f32),
            pltpu.VMEM((SWEEPS, NY, NC, BLK), f32),
            pltpu.VMEM((NX, NY, COLS, BLK), f32),
            pltpu.VMEM((NY, COLS, BLK), f32),
            pltpu.VMEM((NY, COLS, BLK), f32),
            pltpu.VMEM((NC, max(8, BLK // NC), BLK), f32),
            pltpu.VMEM((NX, BLK // NX, BLK), f32),
            pltpu.VMEM((NX, BLK // NX, BLK), f32),
            pltpu.VMEM((NY, BLK // NC, BLK), f32),
            pltpu.VMEM((NY, BLK // NC, BLK), f32),
            pltpu.VMEM((NR, half_rows // NR, BLK), f32),
            pltpu.VMEM((NR, half_rows // NR, BLK), f32),
            pltpu.VMEM((NX, half_rows // NR, BLK), f32),
            pltpu.VMEM((NY, half_rows // NR, BLK), f32),
            pltpu.VMEM((NR, half_rows // NR, BLK), f32),
            pltpu.SemaphoreType.DMA((23,)),
            pltpu.SemaphoreType.DMA((23,)),
        ],
        compiler_params=pltpu.CompilerParams(collective_id=0, has_side_effects=True),
        name="tile",
    )(profiles, cell_width.reshape(1, BLK), basis, block_lists, block_counts, landmarks)
    ritz, rows, cols = pl.pallas_call(
        functools.partial(finish_kernel, cells=landmarks.shape[0] * BLK),
        out_shape=(
            jax.ShapeDtypeStruct((COLS, BLK), f32),
            jax.ShapeDtypeStruct((NC, BLK), f32),
            jax.ShapeDtypeStruct((CP, BLK), f32),
        ),
        in_specs=[vmem] * 4,
        out_specs=(vmem,) * 3,
        name="finish",
    )(gram, proj, rows, cols)
    return rows.reshape(-1), cols[:NR].reshape(-1), ritz


def solution(mesh):
    NR, NC = mesh.shape["row"], mesh.shape["col"]
    NX = {32: 4, 4: 2}[NC]
    placed = (
        P(None, ("col", "row")),
        P(("col", "row")),
        P(None, ("col", "row")),
        P("row", "col", None, None),
        P("row", "col"),
        P(),
    )
    return jax.shard_map(
        functools.partial(body, (NR, NC, NX, NC // NX)),
        mesh=mesh,
        in_specs=placed,
        out_specs=(P("row"), P("col"), P(None, ("row", "col"))),
        check_vma=False,
    )
```

```python
import functools

import jax
import jax.numpy as jnp
from jax import lax
from jax.experimental import pallas as pl
from jax.experimental.pallas import tpu as pltpu
from jax.sharding import PartitionSpec as P

BLK = 128
PCS = 50
COLS = 64
SWEEPS = 3
KDIM = 64
CP = 16
RP = 32
SCALE = 512.0
MESH = pl.DeviceIdType.MESH
highest = lax.Precision.HIGHEST
f32 = jnp.float32
bf16 = jnp.bfloat16

ROW, COL, ROWKEY, COLKEY, KEEP, LAST, HAS = range(7)


def far_first(size):
    return sorted(range(1, size), key=lambda d: abs(2 * d - size))


def slot_table(lists_ref, count, table_ref):
    slots = lists_ref.shape[-1]
    lane = lax.broadcasted_iota(jnp.int32, (1, slots), 1)
    live = (lane < count).astype(jnp.int32)
    packed = live * 1024 + lists_ref[0, 0, 0:1, :] * 32 + lists_ref[0, 0, 1:2, :]
    down = jnp.broadcast_to(packed, (slots, slots)).T
    number = lax.broadcasted_iota(jnp.int32, (slots, slots), 0)
    across = lax.broadcasted_iota(jnp.int32, (slots, slots), 1)
    unlive = lambda v: jnp.where(v >= 1024, (v >> 5) & 31, RP)
    key_across = unlive(packed) * slots + lane
    key_down = unlive(down) * slots + number
    rank = jnp.sum((key_down < key_across).astype(jnp.int32), axis=0, keepdims=True)
    place = jnp.broadcast_to(rank, (slots, slots)).T == across
    order = jnp.sum(jnp.where(place, down, 0), axis=0, keepdims=True)
    rowkey = unlive(order)
    rows_down = unlive(down)
    upto = jnp.sum((rows_down <= across).astype(jnp.int32), axis=0, keepdims=True)
    here = jnp.sum((rows_down == across).astype(jnp.int32), axis=0, keepdims=True)
    key8 = jnp.broadcast_to(rowkey, (8, slots))
    before = jnp.where(lane == 0, -1, pltpu.roll(key8, 1, 1)[0:1])
    table_ref[ROW : ROW + 1, :] = (order >> 5) & 31
    table_ref[COL : COL + 1, :] = order & 31
    table_ref[ROWKEY : ROWKEY + 1, :] = rowkey
    table_ref[COLKEY : COLKEY + 1, :] = jnp.where(order >= 1024, order & 31, CP)
    table_ref[KEEP : KEEP + 1, :] = (before == rowkey).astype(jnp.int32)
    table_ref[LAST : LAST + 1, :] = jnp.maximum(upto - 1, 0)
    table_ref[HAS : HAS + 1, :] = jnp.minimum(here, 1)


def tile_kernel(
    dims,
    prof_hbm,
    width_hbm,
    basis_hbm,
    lists_hbm,
    count_ref,
    marks_ref,
    gram_ref,
    proj_ref,
    rows_ref,
    cols_ref,
    prof_ref,
    width_ref,
    lists_ref,
    input_sem,
    table_ref,
    idx,
    msg32,
    rowout,
    colbuf,
    basisbuf,
    rowbuf,
    left,
    uleft,
    uright,
    hot,
    rsplit,
    csplit,
    sbas,
    aff,
    sums,
    rowsums,
    rowpick,
    share,
    zvec,
    xvec,
    yvec,
    xshare,
    ysend,
    yshare,
    rlast,
    markx,
    gotx,
    marky,
    goty,
    gparts,
    zgram,
    xgram,
    ygram,
    zall,
    send_sem,
    recv_sem,
):
    NR, NC, NX, NY, slots = dims
    me_r = lax.axis_index("row")
    me_c = lax.axis_index("col")
    me_x = me_c // NY
    me_y = me_c % NY
    own_block = (me_c % 2) * NR + me_r
    to_r = me_c // 2
    to_x = own_block // NY
    own_y = lax.rem(own_block, NY)
    stays = (to_r == me_r) & (to_x == me_x)

    def zdev(d):
        return (lax.rem(me_r + d, NR), me_c)

    def xdev(d):
        return (me_r, lax.rem(me_x + d, NX) * NY + me_y)

    def ydev(d):
        return (me_r, me_x * NY + lax.rem(me_y + d, NY))

    awaited = {}

    def expect(region, number):
        awaited[number] = region

        def wait():
            del awaited[number]
            pltpu.make_async_copy(region, region, recv_sem.at[number]).wait()

        return wait

    def drain():
        pl.when(stays)(lambda: moved(NY - 1))
        pl.when(jnp.logical_not(stays))(lambda: moved(NY))
        for number, region in list(awaited.items()):
            pltpu.make_async_copy(region, region, recv_sem.at[number]).wait()
        for region, number in sent:
            pltpu.make_async_copy(region, region, send_sem.at[number]).wait()

    groups = {"z": (NR, zdev), "x": (NX, xdev), "y": (NY, ydev)}
    sent = []

    def push(axis, src_of, dst, number):
        size, device = groups[axis]
        for d in far_first(size):
            pltpu.make_async_remote_copy(
                src_ref=src_of(d),
                dst_ref=dst.at[d],
                send_sem=send_sem.at[number],
                recv_sem=recv_sem.at[number],
                device_id=device(d),
                device_id_type=MESH,
            ).start()
        region = dst.at[pl.ds(1, size - 1)]
        sent.append((region, number))
        return expect(region, number)

    inputs = [
        pltpu.make_async_copy(src, dst, input_sem.at[n])
        for n, (src, dst) in enumerate(
            (
                (prof_hbm, prof_ref),
                (width_hbm, width_ref),
                (lists_hbm, lists_ref),
                (basis_hbm, basisbuf.at[0]),
            )
        )
    ]
    for copy in inputs:
        copy.start()
    barrier = pltpu.get_barrier_semaphore()
    for size, device in groups.values():
        for d in far_first(size):
            pl.semaphore_signal(barrier, inc=1, device_id=device(d), device_id_type=MESH)
    for n in range(NY):
        block = me_x * NY + n
        source = (lax.rem(block, NR), 2 * me_r + block // NR)

        @pl.when((source[0] != me_r) | (source[1] != me_c))
        def _(source=source):
            pl.semaphore_signal(barrier, inc=1, device_id=source, device_id_type=MESH)
    for copy in inputs:
        copy.wait()

    prof = prof_ref[...].astype(f32)
    half = jnp.sum(prof * prof, axis=0, keepdims=True) * -0.5
    h1 = half.astype(bf16).astype(f32)
    h2 = (half - h1).astype(bf16).astype(f32)
    h3 = half - h1 - h2
    width = width_ref[...].astype(f32)
    ones = jnp.ones((1, BLK), f32)
    msg32[...] = jnp.zeros_like(msg32)
    for side in range(2):
        msg32[side, 0:PCS, :] = prof
        a, b = (50, 53) if side == 0 else (53, 50)
        msg32[side, a : a + 1, :] = h1
        msg32[side, a + 1 : a + 2, :] = h2
        msg32[side, a + 2 : a + 3, :] = h3
        for n in range(3):
            msg32[side, b + n : b + n + 1, :] = ones
        w = 56 + side
        msg32[side, w : w + 1, :] = width
    colbuf[0] = msg32[1].astype(bf16)
    outgoing = rowout.at[0]
    rowout[0] = msg32[0].astype(bf16)

    near = NR + NX + NY - 3
    far = NY - stays.astype(jnp.int32)

    it = lax.broadcasted_iota(jnp.int32, (2 * CP, BLK), 0)

    def tables(k, carry):
        hot[k] = ((it == k) | (it == k + CP)).astype(f32).astype(bf16)
        return carry

    lax.fori_loop(0, CP, tables, 0)
    hot[CP] = jnp.zeros((2 * CP, BLK), bf16)

    pl.semaphore_wait(barrier, near + far)

    for n in range(NY):
        here = stays & (me_y == n)

        @pl.when(jnp.logical_not(here))
        def _(n=n):
            pltpu.make_async_remote_copy(
                src_ref=rowout.at[0],
                dst_ref=rowbuf.at[own_y],
                send_sem=send_sem.at[0],
                recv_sem=recv_sem.at[0],
                device_id=(to_r, to_x * NY + n),
                device_id_type=MESH,
            ).start()

        @pl.when(here)
        def _():
            pltpu.make_async_copy(rowout.at[0], rowbuf.at[own_y], recv_sem.at[0]).start()

    wait_col = push("z", lambda d: colbuf.at[0], colbuf, 1)
    slot_table(lists_ref, count_ref[0, 0], table_ref)
    tabled = pltpu.make_async_copy(table_ref, idx, recv_sem.at[20])
    tabled.start()
    tabled.wait()
    own_rows = rowbuf.at[pl.ds(0, NY)]
    pltpu.make_async_copy(own_rows, own_rows, recv_sem.at[0]).wait()

    def moved(blocks):
        region = rowbuf.at[pl.ds(0, blocks)]
        pltpu.make_async_copy(region, region, send_sem.at[0]).wait()

    for d in far_first(NX):
        pltpu.make_async_remote_copy(
            src_ref=rowbuf.at[pl.ds(0, NY)],
            dst_ref=rowbuf.at[pl.ds(d * NY, NY)],
            send_sem=send_sem.at[3],
            recv_sem=recv_sem.at[3],
            device_id=xdev(d),
            device_id_type=MESH,
        ).start()
    region_x = rowbuf.at[pl.ds(NY, (NX - 1) * NY)]
    sent.append((region_x, 3))
    wait_rows = expect(region_x, 3)

    wait_col()

    def col_place(j):
        return lax.rem(me_r - j + NR, NR)

    def row_place(i):
        return lax.rem(me_x - i // NY + NX, NX) * NY + lax.rem(i, NY)

    def col_prepare(n, carry):
        turned = colbuf[n].astype(f32).T
        left[n] = turned.astype(bf16)
        w = jnp.broadcast_to(turned[:, 57:58], (BLK, BLK))
        uleft[n] = (2.0 * 1.4426950408889634) / w
        return carry

    lax.fori_loop(0, NR, col_prepare, 0)

    wait_rows()

    def row_prepare(n, carry):
        w = rowbuf[n].astype(f32)[56:57, :]
        uright[n] = jnp.broadcast_to(1.0 / w, (8, BLK))
        return carry

    lax.fori_loop(0, NC, row_prepare, 0)

    pairs = slots // 2

    def build(p, carry):
        for h in range(2):
            j = col_place(idx[COL, 2 * p + h])
            i = row_place(idx[ROW, 2 * p + h])
            d = jnp.dot(left[j], rowbuf[i], preferred_element_type=f32)
            e = d * uleft[j] * uright[i][0:1, :]
            aff[p, :, h * BLK : (h + 1) * BLK] = jnp.exp2(e).astype(bf16)
        return carry

    lax.fori_loop(0, pairs, build, 0, unroll=8)

    def col_pass():
        def step(p, acc):
            s, t = 2 * p, 2 * p + 1
            lhs = jnp.concatenate(
                [
                    rsplit[idx[ROW, s]] * hot[idx[COLKEY, s]],
                    rsplit[idx[ROW, t]] * hot[idx[COLKEY, t]],
                ],
                axis=1,
            )
            return acc + lax.dot_general(
                lhs, aff[p], (((1,), (1,)), ((), ())), preferred_element_type=f32
            )

        acc = lax.fori_loop(0, pairs, step, jnp.zeros((2 * CP, BLK), f32), unroll=8)
        return acc[0:CP] + acc[CP:]

    sub8 = lax.broadcasted_iota(jnp.int32, (8, BLK), 0)

    def row_pass():
        def step(p, acc):
            s, t = 2 * p, 2 * p + 1
            lhs = csplit[idx[COL, s], 0] + csplit[idx[COL, t], 1]
            both = jnp.dot(lhs, aff[p], preferred_element_type=f32)
            acc = acc * idx[KEEP, s].astype(f32) + jnp.where(sub8 < 2, both[:, :BLK], 0.0)
            rowsums[s] = acc
            acc = acc * idx[KEEP, t].astype(f32) + jnp.where(sub8 < 2, 0.0, both[:, BLK:])
            rowsums[t] = acc
            return acc

        lax.fori_loop(0, pairs, step, jnp.zeros((8, BLK), f32), unroll=8)
        for i in range(NC):
            rowpick[i] = rowsums[idx[LAST, i]] * idx[HAS, i].astype(f32)
        return jnp.sum(rowpick[...], axis=1)

    def col_total(k, part):
        buf = zvec.at[k]
        buf[0] = part
        wait = push("z", lambda d: buf.at[0], buf, 5 + k)
        wait()
        total = buf[lax.rem(me_r, NR)]
        for r in range(1, NR):
            total = total + buf[lax.rem(me_r - r + NR, NR)]
        return total

    def row_over_x(k, part):
        bx = xvec.at[k]
        bx[0] = part
        wait = push("x", lambda d: bx.at[0], bx, 8 + k)

        def finish():
            wait()
            total = bx[me_x]
            for x in range(1, NX):
                total = total + bx[lax.rem(me_x - x + NX, NX)]
            return total

        return finish

    def row_over_y(k, part):
        by = yvec.at[k]
        by[0] = part
        wait = push("y", lambda d: by.at[0], by, 11 + k)

        def finish():
            wait()
            total = by[me_y]
            for y in range(1, NY):
                total = total + by[lax.rem(me_y - y + NY, NY)]
            return total

        return finish

    def row_total(k, part):
        return row_over_y(k, row_over_x(k, part)())()

    def split(v):
        hi = v.astype(bf16).astype(f32)
        return hi, v - hi

    def spread_rows(vec):
        for n in range(NC):
            hi, lo = split(jnp.broadcast_to(vec[n : n + 1, :], (CP, BLK)))
            rsplit[n] = jnp.concatenate([hi, lo], axis=0).astype(bf16)

    def spread_cols(vec):
        for n in range(NR):
            hi, lo = split(jnp.broadcast_to(vec[n : n + 1, :], (8, BLK)))
            even = jnp.where(sub8 % 2 == 0, hi, lo)
            csplit[n, 0] = jnp.where(sub8 < 2, even, 0.0).astype(bf16)
            csplit[n, 1] = jnp.where((sub8 >= 2) & (sub8 < 4), even, 0.0).astype(bf16)

    first = lax.broadcasted_iota(jnp.int32, (NC, 2 * CP, BLK), 1)
    rsplit[...] = jnp.where(first < CP, 1.0, 0.0).astype(bf16)
    for k in range(SWEEPS):
        part = col_pass()
        cols_ref[...] = part
        cvec = SCALE / col_total(k, part)
        spread_cols(cvec)
        if k < SWEEPS - 1:
            part = row_pass()
            rows_ref[...] = part
            if k == 0:
                wait_basis = push("z", lambda d: basisbuf.at[0], basisbuf, 4)
            rvec = SCALE / row_total(k, part)
            spread_rows(rvec)
    cols_ref[...] = cvec

    over_x = row_over_x(SWEEPS - 1, row_pass())
    wait_basis()
    for j in range(NR):
        block = basisbuf[col_place(j)].astype(f32) * cvec[j : j + 1, :]
        sbas[j] = block.astype(bf16)

    def subspace(p, acc):
        for h in range(2):
            s = 2 * p + h
            product = jnp.dot(
                sbas[idx[COL, s]],
                aff[p, :, h * BLK : (h + 1) * BLK],
                preferred_element_type=f32,
            )
            acc = acc * idx[KEEP, s].astype(f32) + product
            sums[s] = acc
        return acc

    lax.fori_loop(0, pairs, subspace, jnp.zeros((COLS, BLK), f32), unroll=4)

    def pick(i, carry):
        share[i] = sums[idx[LAST, i]] * idx[HAS, i].astype(f32)
        return carry

    lax.fori_loop(0, NC, pick, 0)

    marked = [jnp.clip(marks_ref[2 * me_r + h] - me_r * NC, 0, NC - 1) for h in range(2)]
    both = jnp.concatenate([share[n] for n in marked], axis=0).T
    x_cells, y_cells = BLK // NX, BLK // NC
    for x in range(NX):
        markx[x] = both[x * x_cells : (x + 1) * x_cells]
    wait_markx = push("x", lambda d: markx.at[lax.rem(me_x + d, NX)], gotx, 21)
    over_y = row_over_y(SWEEPS - 1, over_x())

    def own_part(x):
        return share.at[pl.ds(x * NY, NY)]

    wait_share = push("x", lambda d: own_part(lax.rem(me_x + d, NX)), xshare, 14)
    wait_markx()
    total = markx[me_x]
    for d in range(1, NX):
        total = total + gotx[d]
    for y in range(NY):
        marky[y] = total[y * y_cells : (y + 1) * y_cells]
    wait_marky = push("y", lambda d: marky.at[lax.rem(me_y + d, NY)], goty, 22)
    rvec = SCALE / over_y()
    rows_ref[...] = rvec
    for n in range(NC):
        rlast[n] = jnp.broadcast_to(rvec[n : n + 1, :], (max(8, y_cells), BLK))
    first_cell = me_x * x_cells + me_y * y_cells
    lanes = lax.broadcasted_iota(jnp.int32, (y_cells, BLK), 1)
    own = lanes == first_cell + lax.broadcasted_iota(jnp.int32, (y_cells, BLK), 0)
    scales = [
        jnp.sum(jnp.where(own, rlast[n][0:y_cells], 0.0), axis=1, keepdims=True)
        for n in marked
    ]
    wait_marky()
    total = marky[me_y]
    for d in range(1, NY):
        total = total + goty[d]
    masked = total * (jnp.where(lanes < COLS, scales[0], scales[1]) * (1.0 / SCALE))
    gram = jnp.zeros((COLS, COLS), f32)
    for h in range(2):
        cells = masked[:, h * COLS : (h + 1) * COLS]
        gram = gram + lax.dot_general(
            cells, cells, (((0,), (0,)), ((), ())), precision=highest, preferred_element_type=f32
        )
    half_rows = COLS // 2
    packed = jnp.concatenate([gram[:half_rows], gram[half_rows:]], axis=1)
    part_rows = half_rows // NR
    for n in range(NR):
        gparts[n] = packed[n * part_rows : (n + 1) * part_rows]
    zgram[0] = gparts[me_r]
    push("z", lambda d: gparts.at[lax.rem(me_r + d, NR)], zgram, 16)()
    total = zgram[me_r]
    for n in range(1, NR):
        total = total + zgram[lax.rem(me_r - n + NR, NR)]

    def over(axis, buf, number, value):
        buf[0] = value
        return push(axis, lambda d: buf.at[0], buf, number)

    def added(buf, size, me):
        total = buf[me]
        for n in range(1, size):
            total = total + buf[lax.rem(me - n + size, size)]
        return total

    over("y", ygram, 18, total)()
    wait_xgram = over("x", xgram, 17, added(ygram, NY, me_y))
    wait_share()

    def add_x(n, carry):
        total = share[me_x * NY + n]
        for d in range(1, NX):
            total = total + xshare[d, n]
        ysend[n] = total
        return carry

    lax.fori_loop(0, NY, add_x, 0)
    wait_yshare = push("y", lambda d: ysend.at[lax.rem(me_y + d, NY)], yshare, 15)
    wait_xgram()
    wait_zall = over("z", zall, 19, added(xgram, NX, me_x))
    wait_yshare()
    total = ysend[me_y]
    for d in range(1, NY):
        total = total + yshare[d]
    proj_ref[...] = total * (rows_ref[pl.ds(me_c, 1), :] * (1.0 / SCALE))
    wait_zall()
    for n in range(NR):
        gram_ref[n * part_rows : (n + 1) * part_rows, :] = zall[lax.rem(me_r - n + NR, NR)]
    drain()


def finish_kernel(gram_ref, proj_ref, rows_in, cols_in, ritz_ref, rows_ref, cols_ref, *, cells):
    rows_ref[...] = rows_in[...]
    cols_ref[...] = cols_in[...]
    half_rows = COLS // 2
    packed = gram_ref[...] * (1.0 / cells)
    gram = jnp.concatenate([packed[:, :COLS], packed[:, COLS:]], axis=0)
    proj = proj_ref[...]
    gs = [gram[n : n + 8] for n in range(0, COLS, 8)]
    ps = [proj[n : n + 8] for n in range(0, COLS, 8)]
    wide = 4
    for k in range(0, COLS, wide):
        top, row = k // 8, k % 8
        cols = [
            [jnp.broadcast_to(g[:, k + m : k + m + 1], (8, BLK)) for g in gs[top:]]
            for m in range(wide)
        ]
        flat = lambda v, i: jnp.broadcast_to(v[row + i : row + i + 1, :], (8, v.shape[1]))
        d = [[flat(cols[m][0], i) for m in range(wide)] for i in range(wide)]
        grow = [flat(gs[top], i) for i in range(wide)]
        prow = [flat(ps[top], i) for i in range(wide)]
        inv = []
        for i in range(wide):
            inv.append(1.0 / d[i][i])
            for j in range(i + 1, wide):
                factor = d[j][i] * inv[i]
                for m in range(j, wide):
                    d[j][m] = d[j][m] - factor * d[i][m]
                    d[m][j] = d[j][m]
                grow[j] = grow[j] - factor[:, :COLS] * grow[i]
                prow[j] = prow[j] - factor * prow[i]
                cols[j] = [a - factor * b for a, b in zip(cols[j], cols[i])]
        for i in range(wide):
            scale = 1.0 / jnp.sqrt(d[i][i][0:1])
            ritz_ref[k + i : k + i + 1, :] = prow[i][0:1] * scale
        for i in range(wide):
            grow[i] = grow[i] * inv[i][:, :COLS]
            prow[i] = prow[i] * inv[i]
        for n in range(top, COLS // 8):
            for i in range(wide):
                col = cols[i][n - top]
                gs[n] = gs[n] - col[:, :COLS] * grow[i]
                ps[n] = ps[n] - col * prow[i]


def body(mesh_sizes, profiles, cell_width, basis, block_lists, block_counts, landmarks):
    NR, NC, NX, NY = mesh_sizes
    slots = block_lists.shape[-1]
    vmem = pl.BlockSpec(memory_space=pltpu.VMEM)
    hbm = pl.BlockSpec(memory_space=pltpu.HBM)
    smem = pl.BlockSpec(memory_space=pltpu.SMEM)
    half_rows = COLS // 2
    gram, proj, rows, cols = pl.pallas_call(
        functools.partial(tile_kernel, (NR, NC, NX, NY, slots)),
        out_shape=(
            jax.ShapeDtypeStruct((half_rows, BLK), f32),
            jax.ShapeDtypeStruct((COLS, BLK), f32),
            jax.ShapeDtypeStruct((NC, BLK), f32),
            jax.ShapeDtypeStruct((CP, BLK), f32),
        ),
        in_specs=[hbm, hbm, hbm, hbm, smem, smem],
        out_specs=(vmem,) * 4,
        scratch_shapes=[
            pltpu.VMEM((PCS, BLK), bf16),
            pltpu.VMEM((1, BLK), bf16),
            pltpu.VMEM((1, 1, 2, slots), jnp.int32),
            pltpu.SemaphoreType.DMA((4,)),
            pltpu.VMEM((8, slots), jnp.int32),
            pltpu.SMEM((8, slots), jnp.int32),
            pltpu.VMEM((2, KDIM, BLK), f32),
            pltpu.VMEM((1, KDIM, BLK), bf16),
            pltpu.VMEM((NR, KDIM, BLK), bf16),
            pltpu.VMEM((NR, COLS, BLK), bf16),
            pltpu.VMEM((NC, KDIM, BLK), bf16),
            pltpu.VMEM((NR, BLK, KDIM), bf16),
            pltpu.VMEM((NR, BLK, BLK), f32),
            pltpu.VMEM((NC, 8, BLK), f32),
            pltpu.VMEM((CP + 1, 2 * CP, BLK), bf16),
            pltpu.VMEM((NC, 2 * CP, BLK), bf16),
            pltpu.VMEM((NR, 2, 8, BLK), bf16),
            pltpu.VMEM((NR, COLS, BLK), bf16),
            pltpu.VMEM((slots // 2, BLK, 2 * BLK), bf16),
            pltpu.VMEM((slots, COLS, BLK), f32),
            pltpu.VMEM((slots, 8, BLK), f32),
            pltpu.VMEM((NC, 8, BLK), f32),
            pltpu.VMEM((NC, COLS, BLK), f32),
            pltpu.VMEM((SWEEPS, NR, CP, BLK), f32),
            pltpu.VMEM((SWEEPS, NX, NC, BLK), f32),
            pltpu.VMEM((SWEEPS, NY, NC, BLK), f32),
            pltpu.VMEM((NX, NY, COLS, BLK), f32),
            pltpu.VMEM((NY, COLS, BLK), f32),
            pltpu.VMEM((NY, COLS, BLK), f32),
            pltpu.VMEM((NC, max(8, BLK // NC), BLK), f32),
            pltpu.VMEM((NX, BLK // NX, BLK), f32),
            pltpu.VMEM((NX, BLK // NX, BLK), f32),
            pltpu.VMEM((NY, BLK // NC, BLK), f32),
            pltpu.VMEM((NY, BLK // NC, BLK), f32),
            pltpu.VMEM((NR, half_rows // NR, BLK), f32),
            pltpu.VMEM((NR, half_rows // NR, BLK), f32),
            pltpu.VMEM((NX, half_rows // NR, BLK), f32),
            pltpu.VMEM((NY, half_rows // NR, BLK), f32),
            pltpu.VMEM((NR, half_rows // NR, BLK), f32),
            pltpu.SemaphoreType.DMA((23,)),
            pltpu.SemaphoreType.DMA((23,)),
        ],
        compiler_params=pltpu.CompilerParams(collective_id=0, has_side_effects=True),
        name="tile",
    )(profiles, cell_width.reshape(1, BLK), basis, block_lists, block_counts, landmarks)
    ritz, rows, cols = pl.pallas_call(
        functools.partial(finish_kernel, cells=landmarks.shape[0] * BLK),
        out_shape=(
            jax.ShapeDtypeStruct((COLS, BLK), f32),
            jax.ShapeDtypeStruct((NC, BLK), f32),
            jax.ShapeDtypeStruct((CP, BLK), f32),
        ),
        in_specs=[vmem] * 4,
        out_specs=(vmem,) * 3,
        name="finish",
    )(gram, proj, rows, cols)
    return rows.reshape(-1), cols[:NR].reshape(-1), ritz


def solution(mesh):
    NR, NC = mesh.shape["row"], mesh.shape["col"]
    NX = {32: 4, 4: 2}[NC]
    placed = (
        P(None, ("col", "row")),
        P(("col", "row")),
        P(None, ("col", "row")),
        P("row", "col", None, None),
        P("row", "col"),
        P(),
    )
    return jax.shard_map(
        functools.partial(body, (NR, NC, NX, NC // NX)),
        mesh=mesh,
        in_specs=placed,
        out_specs=(P("row"), P("col"), P(None, ("row", "col"))),
        check_vma=False,
    )
```

```python
import functools

import jax
import jax.numpy as jnp
from jax import lax
from jax.experimental import pallas as pl
from jax.experimental.pallas import tpu as pltpu
from jax.sharding import PartitionSpec as P

BLK = 128
PCS = 50
COLS = 64
SWEEPS = 3
KDIM = 64
CP = 16
RP = 32
SCALE = 512.0
MESH = pl.DeviceIdType.MESH
highest = lax.Precision.HIGHEST
f32 = jnp.float32
bf16 = jnp.bfloat16

ROW, COL, ROWKEY, COLKEY, KEEP, LAST, HAS = range(7)


def far_first(size):
    return sorted(range(1, size), key=lambda d: abs(2 * d - size))


def slot_table(lists_ref, count, table_ref):
    slots = lists_ref.shape[-1]
    lane = lax.broadcasted_iota(jnp.int32, (1, slots), 1)
    live = (lane < count).astype(jnp.int32)
    packed = live * 1024 + lists_ref[0, 0, 0:1, :] * 32 + lists_ref[0, 0, 1:2, :]
    down = jnp.broadcast_to(packed, (slots, slots)).T
    number = lax.broadcasted_iota(jnp.int32, (slots, slots), 0)
    across = lax.broadcasted_iota(jnp.int32, (slots, slots), 1)
    unlive = lambda v: jnp.where(v >= 1024, (v >> 5) & 31, RP)
    key_across = unlive(packed) * slots + lane
    key_down = unlive(down) * slots + number
    rank = jnp.sum((key_down < key_across).astype(jnp.int32), axis=0, keepdims=True)
    place = jnp.broadcast_to(rank, (slots, slots)).T == across
    order = jnp.sum(jnp.where(place, down, 0), axis=0, keepdims=True)
    rowkey = unlive(order)
    rows_down = unlive(down)
    upto = jnp.sum((rows_down <= across).astype(jnp.int32), axis=0, keepdims=True)
    here = jnp.sum((rows_down == across).astype(jnp.int32), axis=0, keepdims=True)
    key8 = jnp.broadcast_to(rowkey, (8, slots))
    before = jnp.where(lane == 0, -1, pltpu.roll(key8, 1, 1)[0:1])
    table_ref[ROW : ROW + 1, :] = (order >> 5) & 31
    table_ref[COL : COL + 1, :] = order & 31
    table_ref[ROWKEY : ROWKEY + 1, :] = rowkey
    table_ref[COLKEY : COLKEY + 1, :] = jnp.where(order >= 1024, order & 31, CP)
    table_ref[KEEP : KEEP + 1, :] = (before == rowkey).astype(jnp.int32)
    table_ref[LAST : LAST + 1, :] = jnp.maximum(upto - 1, 0)
    table_ref[HAS : HAS + 1, :] = jnp.minimum(here, 1)


def tile_kernel(
    dims,
    prof_hbm,
    width_hbm,
    basis_hbm,
    lists_hbm,
    count_ref,
    marks_ref,
    gram_ref,
    proj_ref,
    rows_ref,
    cols_ref,
    prof_ref,
    width_ref,
    lists_ref,
    input_sem,
    table_ref,
    idx,
    msg32,
    rowout,
    colbuf,
    basisbuf,
    rowbuf,
    left,
    uleft,
    uright,
    hot,
    rsplit,
    csplit,
    sbas,
    aff,
    sums,
    rowsums,
    rowpick,
    share,
    zvec,
    xvec,
    yvec,
    zlast,
    xlast,
    ylast,
    xshare,
    ysend,
    yshare,
    rlast,
    marks,
    gotmarks,
    gparts,
    zgram,
    pgram,
    zall,
    send_sem,
    recv_sem,
):
    NR, NC, NX, NY, slots = dims
    me_r = lax.axis_index("row")
    me_c = lax.axis_index("col")
    me_x = me_c // NY
    me_y = me_c % NY
    own_block = (me_c % 2) * NR + me_r
    to_r = me_c // 2
    to_x = own_block // NY
    own_y = lax.rem(own_block, NY)
    stays = (to_r == me_r) & (to_x == me_x)

    def zdev(d):
        return (lax.rem(me_r + d, NR), me_c)

    def xdev(d):
        return (me_r, lax.rem(me_x + d, NX) * NY + me_y)

    def ydev(d):
        return (me_r, me_x * NY + lax.rem(me_y + d, NY))

    awaited = {}

    def expect(region, number):
        awaited[number] = region

        def wait():
            del awaited[number]
            pltpu.make_async_copy(region, region, recv_sem.at[number]).wait()

        return wait

    def drain():
        pl.when(stays)(lambda: moved(NY - 1))
        pl.when(jnp.logical_not(stays))(lambda: moved(NY))
        for number, region in list(awaited.items()):
            pltpu.make_async_copy(region, region, recv_sem.at[number]).wait()
        for region, number in sent:
            pltpu.make_async_copy(region, region, send_sem.at[number]).wait()

    def pdev(d):
        return (me_r, lax.rem(me_c + d, NC))

    def hops(d):
        return min(d // NY, NX - d // NY) + min(d % NY, NY - d % NY)

    groups = {"z": (NR, zdev), "x": (NX, xdev), "y": (NY, ydev), "p": (NC, pdev)}
    steps = {axis: far_first(groups[axis][0]) for axis in "zxy"}
    steps["p"] = sorted(range(1, NC), key=lambda d: -hops(d))
    sent = []

    def push(axis, src_of, dst, number):
        size, device = groups[axis]
        for d in steps[axis]:
            pltpu.make_async_remote_copy(
                src_ref=src_of(d),
                dst_ref=dst.at[d],
                send_sem=send_sem.at[number],
                recv_sem=recv_sem.at[number],
                device_id=device(d),
                device_id_type=MESH,
            ).start()
        region = dst.at[pl.ds(1, size - 1)]
        sent.append((region, number))
        return expect(region, number)

    inputs = [
        pltpu.make_async_copy(src, dst, input_sem.at[n])
        for n, (src, dst) in enumerate(
            (
                (prof_hbm, prof_ref),
                (width_hbm, width_ref),
                (lists_hbm, lists_ref),
                (basis_hbm, basisbuf.at[0]),
            )
        )
    ]
    for copy in inputs:
        copy.start()
    barrier = pltpu.get_barrier_semaphore()
    for axis in "pz":
        for d in steps[axis]:
            pl.semaphore_signal(
                barrier, inc=1, device_id=groups[axis][1](d), device_id_type=MESH
            )
    for n in range(NY):
        block = me_x * NY + n
        source = (lax.rem(block, NR), 2 * me_r + block // NR)

        @pl.when((source[0] != me_r) | (source[1] != me_c))
        def _(source=source):
            pl.semaphore_signal(barrier, inc=1, device_id=source, device_id_type=MESH)
    for copy in inputs:
        copy.wait()

    prof = prof_ref[...].astype(f32)
    half = jnp.sum(prof * prof, axis=0, keepdims=True) * -0.5
    h1 = half.astype(bf16).astype(f32)
    h2 = (half - h1).astype(bf16).astype(f32)
    h3 = half - h1 - h2
    width = width_ref[...].astype(f32)
    ones = jnp.ones((1, BLK), f32)
    msg32[...] = jnp.zeros_like(msg32)
    for side in range(2):
        msg32[side, 0:PCS, :] = prof
        a, b = (50, 53) if side == 0 else (53, 50)
        msg32[side, a : a + 1, :] = h1
        msg32[side, a + 1 : a + 2, :] = h2
        msg32[side, a + 2 : a + 3, :] = h3
        for n in range(3):
            msg32[side, b + n : b + n + 1, :] = ones
        w = 56 + side
        msg32[side, w : w + 1, :] = width
    colbuf[0] = msg32[1].astype(bf16)
    outgoing = rowout.at[0]
    rowout[0] = msg32[0].astype(bf16)

    near = NR + NC - 2
    far = NY - stays.astype(jnp.int32)

    it = lax.broadcasted_iota(jnp.int32, (2 * CP, BLK), 0)

    def tables(k, carry):
        hot[k] = ((it == k) | (it == k + CP)).astype(f32).astype(bf16)
        return carry

    lax.fori_loop(0, CP, tables, 0)
    hot[CP] = jnp.zeros((2 * CP, BLK), bf16)

    pl.semaphore_wait(barrier, near + far)

    for n in range(NY):
        here = stays & (me_y == n)

        @pl.when(jnp.logical_not(here))
        def _(n=n):
            pltpu.make_async_remote_copy(
                src_ref=rowout.at[0],
                dst_ref=rowbuf.at[own_y],
                send_sem=send_sem.at[0],
                recv_sem=recv_sem.at[0],
                device_id=(to_r, to_x * NY + n),
                device_id_type=MESH,
            ).start()

        @pl.when(here)
        def _():
            pltpu.make_async_copy(rowout.at[0], rowbuf.at[own_y], recv_sem.at[0]).start()

    wait_col = push("z", lambda d: colbuf.at[0], colbuf, 1)
    slot_table(lists_ref, count_ref[0, 0], table_ref)
    tabled = pltpu.make_async_copy(table_ref, idx, recv_sem.at[20])
    tabled.start()
    tabled.wait()
    own_rows = rowbuf.at[pl.ds(0, NY)]
    pltpu.make_async_copy(own_rows, own_rows, recv_sem.at[0]).wait()

    def moved(blocks):
        region = rowbuf.at[pl.ds(0, blocks)]
        pltpu.make_async_copy(region, region, send_sem.at[0]).wait()

    for d in far_first(NX):
        pltpu.make_async_remote_copy(
            src_ref=rowbuf.at[pl.ds(0, NY)],
            dst_ref=rowbuf.at[pl.ds(d * NY, NY)],
            send_sem=send_sem.at[3],
            recv_sem=recv_sem.at[3],
            device_id=xdev(d),
            device_id_type=MESH,
        ).start()
    region_x = rowbuf.at[pl.ds(NY, (NX - 1) * NY)]
    sent.append((region_x, 3))
    wait_rows = expect(region_x, 3)

    wait_col()

    def col_place(j):
        return lax.rem(me_r - j + NR, NR)

    def row_place(i):
        return lax.rem(me_x - i // NY + NX, NX) * NY + lax.rem(i, NY)

    def col_prepare(n, carry):
        turned = colbuf[n].astype(f32).T
        left[n] = turned.astype(bf16)
        w = jnp.broadcast_to(turned[:, 57:58], (BLK, BLK))
        uleft[n] = (2.0 * 1.4426950408889634) / w
        return carry

    lax.fori_loop(0, NR, col_prepare, 0)

    wait_rows()

    def row_prepare(n, carry):
        w = rowbuf[n].astype(f32)[56:57, :]
        uright[n] = jnp.broadcast_to(1.0 / w, (8, BLK))
        return carry

    lax.fori_loop(0, NC, row_prepare, 0)

    pairs = slots // 2

    def build(p, carry):
        for h in range(2):
            j = col_place(idx[COL, 2 * p + h])
            i = row_place(idx[ROW, 2 * p + h])
            d = jnp.dot(left[j], rowbuf[i], preferred_element_type=f32)
            e = d * uleft[j] * uright[i][0:1, :]
            aff[p, :, h * BLK : (h + 1) * BLK] = jnp.exp2(e).astype(bf16)
        return carry

    lax.fori_loop(0, pairs, build, 0, unroll=8)

    def col_pass():
        def step(p, acc):
            s, t = 2 * p, 2 * p + 1
            lhs = jnp.concatenate(
                [
                    rsplit[idx[ROW, s]] * hot[idx[COLKEY, s]],
                    rsplit[idx[ROW, t]] * hot[idx[COLKEY, t]],
                ],
                axis=1,
            )
            return acc + lax.dot_general(
                lhs, aff[p], (((1,), (1,)), ((), ())), preferred_element_type=f32
            )

        acc = lax.fori_loop(0, pairs, step, jnp.zeros((2 * CP, BLK), f32), unroll=8)
        return acc[0:CP] + acc[CP:]

    sub8 = lax.broadcasted_iota(jnp.int32, (8, BLK), 0)

    def row_pass():
        def step(p, acc):
            s, t = 2 * p, 2 * p + 1
            lhs = csplit[idx[COL, s], 0] + csplit[idx[COL, t], 1]
            both = jnp.dot(lhs, aff[p], preferred_element_type=f32)
            acc = acc * idx[KEEP, s].astype(f32) + jnp.where(sub8 < 2, both[:, :BLK], 0.0)
            rowsums[s] = acc
            acc = acc * idx[KEEP, t].astype(f32) + jnp.where(sub8 < 2, 0.0, both[:, BLK:])
            rowsums[t] = acc
            return acc

        lax.fori_loop(0, pairs, step, jnp.zeros((8, BLK), f32), unroll=8)
        for i in range(NC):
            rowpick[i] = rowsums[idx[LAST, i]] * idx[HAS, i].astype(f32)
        return jnp.sum(rowpick[...], axis=1)

    def col_total(k, part):
        buf = zlast if k == SWEEPS - 1 else zvec.at[k]
        buf[0] = part.astype(buf.dtype)
        wait = push("z", lambda d: buf.at[0], buf, 5 + k)
        wait()
        total = buf[lax.rem(me_r, NR)].astype(f32)
        for r in range(1, NR):
            total = total + buf[lax.rem(me_r - r + NR, NR)].astype(f32)
        return total

    def row_over_x(k, part):
        bx = xlast if k == SWEEPS - 1 else xvec.at[k]
        bx[0] = part.astype(bx.dtype)
        wait = push("x", lambda d: bx.at[0], bx, 8 + k)

        def finish():
            wait()
            total = bx[me_x].astype(f32)
            for x in range(1, NX):
                total = total + bx[lax.rem(me_x - x + NX, NX)].astype(f32)
            return total

        return finish

    def row_over_y(k, part):
        by = ylast if k == SWEEPS - 1 else yvec.at[k]
        by[0] = part.astype(by.dtype)
        wait = push("y", lambda d: by.at[0], by, 11 + k)

        def finish():
            wait()
            total = by[me_y].astype(f32)
            for y in range(1, NY):
                total = total + by[lax.rem(me_y - y + NY, NY)].astype(f32)
            return total

        return finish

    def row_total(k, part):
        return row_over_y(k, row_over_x(k, part)())()

    def split(v):
        hi = v.astype(bf16).astype(f32)
        return hi, v - hi

    def spread_rows(vec):
        for n in range(NC):
            hi, lo = split(jnp.broadcast_to(vec[n : n + 1, :], (CP, BLK)))
            rsplit[n] = jnp.concatenate([hi, lo], axis=0).astype(bf16)

    def spread_cols(vec):
        for n in range(NR):
            hi, lo = split(jnp.broadcast_to(vec[n : n + 1, :], (8, BLK)))
            even = jnp.where(sub8 % 2 == 0, hi, lo)
            csplit[n, 0] = jnp.where(sub8 < 2, even, 0.0).astype(bf16)
            csplit[n, 1] = jnp.where((sub8 >= 2) & (sub8 < 4), even, 0.0).astype(bf16)

    first = lax.broadcasted_iota(jnp.int32, (NC, 2 * CP, BLK), 1)
    rsplit[...] = jnp.where(first < CP, 1.0, 0.0).astype(bf16)
    for k in range(SWEEPS):
        part = col_pass()
        cols_ref[...] = part
        cvec = SCALE / col_total(k, part)
        spread_cols(cvec)
        if k < SWEEPS - 1:
            part = row_pass()
            rows_ref[...] = part
            if k == 0:
                wait_basis = push("z", lambda d: basisbuf.at[0], basisbuf, 4)
            rvec = SCALE / row_total(k, part)
            spread_rows(rvec)
    cols_ref[...] = cvec

    over_x = row_over_x(SWEEPS - 1, row_pass())
    wait_basis()
    for j in range(NR):
        block = basisbuf[col_place(j)].astype(f32) * cvec[j : j + 1, :]
        sbas[j] = block.astype(bf16)

    def subspace(p, acc):
        for h in range(2):
            s = 2 * p + h
            product = jnp.dot(
                sbas[idx[COL, s]],
                aff[p, :, h * BLK : (h + 1) * BLK],
                preferred_element_type=f32,
            )
            acc = acc * idx[KEEP, s].astype(f32) + product
            sums[s] = acc
        return acc

    lax.fori_loop(0, pairs, subspace, jnp.zeros((COLS, BLK), f32), unroll=4)

    def pick(i, carry):
        share[i] = sums[idx[LAST, i]] * idx[HAS, i].astype(f32)
        return carry

    lax.fori_loop(0, NC, pick, 0)

    marked = [jnp.clip(marks_ref[2 * me_r + h] - me_r * NC, 0, NC - 1) for h in range(2)]
    both = jnp.concatenate([share[n] for n in marked], axis=0).T
    cells = BLK // NC
    for c in range(NC):
        marks[c] = both[c * cells : (c + 1) * cells]
    wait_marks = push("p", lambda d: marks.at[lax.rem(me_c + d, NC)], gotmarks, 21)
    over_y = row_over_y(SWEEPS - 1, over_x())

    def own_part(x):
        return share.at[pl.ds(x * NY, NY)]

    wait_share = push("x", lambda d: own_part(lax.rem(me_x + d, NX)), xshare, 14)
    rvec = SCALE / over_y()
    rows_ref[...] = rvec
    for n in range(NC):
        rlast[n] = jnp.broadcast_to(rvec[n : n + 1, :], (max(8, cells), BLK))
    lanes = lax.broadcasted_iota(jnp.int32, (cells, BLK), 1)
    own = lanes == me_c * cells + lax.broadcasted_iota(jnp.int32, (cells, BLK), 0)
    scales = [
        jnp.sum(jnp.where(own, rlast[n][0:cells], 0.0), axis=1, keepdims=True) for n in marked
    ]
    wait_marks()
    total = marks[me_c]
    for d in range(1, NC):
        total = total + gotmarks[d]
    masked = total * (jnp.where(lanes < COLS, scales[0], scales[1]) * (1.0 / SCALE))
    gram = jnp.zeros((COLS, COLS), f32)
    for h in range(2):
        block = masked[:, h * COLS : (h + 1) * COLS]
        gram = gram + lax.dot_general(
            block, block, (((0,), (0,)), ((), ())), precision=highest, preferred_element_type=f32
        )
    half_rows = COLS // 2
    packed = jnp.concatenate([gram[:half_rows], gram[half_rows:]], axis=1)
    part_rows = half_rows // NR
    for n in range(NR):
        gparts[n] = packed[n * part_rows : (n + 1) * part_rows]
    zgram[0] = gparts[me_r]
    push("z", lambda d: gparts.at[lax.rem(me_r + d, NR)], zgram, 16)()
    total = zgram[me_r]
    for n in range(1, NR):
        total = total + zgram[lax.rem(me_r - n + NR, NR)]

    def over(axis, buf, number, value):
        buf[0] = value
        return push(axis, lambda d: buf.at[0], buf, number)

    def added(buf, size, me):
        total = buf[me]
        for n in range(1, size):
            total = total + buf[lax.rem(me - n + size, size)]
        return total

    wait_pgram = over("p", pgram, 17, total)
    wait_share()

    def add_x(n, carry):
        total = share[me_x * NY + n]
        for d in range(1, NX):
            total = total + xshare[d, n]
        ysend[n] = total
        return carry

    lax.fori_loop(0, NY, add_x, 0)
    wait_yshare = push("y", lambda d: ysend.at[lax.rem(me_y + d, NY)], yshare, 15)
    wait_pgram()
    wait_zall = over("z", zall, 19, added(pgram, NC, me_c))
    wait_yshare()
    total = ysend[me_y]
    for d in range(1, NY):
        total = total + yshare[d]
    proj_ref[...] = total * (rows_ref[pl.ds(me_c, 1), :] * (1.0 / SCALE))
    wait_zall()
    for n in range(NR):
        gram_ref[n * part_rows : (n + 1) * part_rows, :] = zall[lax.rem(me_r - n + NR, NR)]
    drain()


def finish_kernel(gram_ref, proj_ref, rows_in, cols_in, ritz_ref, rows_ref, cols_ref, *, cells):
    rows_ref[...] = rows_in[...]
    cols_ref[...] = cols_in[...]
    half_rows = COLS // 2
    packed = gram_ref[...] * (1.0 / cells)
    gram = jnp.concatenate([packed[:, :COLS], packed[:, COLS:]], axis=0)
    proj = proj_ref[...]
    gs = [gram[n : n + 8] for n in range(0, COLS, 8)]
    ps = [proj[n : n + 8] for n in range(0, COLS, 8)]
    wide = 4
    for k in range(0, COLS, wide):
        top, row = k // 8, k % 8
        cols = [
            [jnp.broadcast_to(g[:, k + m : k + m + 1], (8, BLK)) for g in gs[top:]]
            for m in range(wide)
        ]
        flat = lambda v, i: jnp.broadcast_to(v[row + i : row + i + 1, :], (8, v.shape[1]))
        d = [[flat(cols[m][0], i) for m in range(wide)] for i in range(wide)]
        grow = [flat(gs[top], i) for i in range(wide)]
        prow = [flat(ps[top], i) for i in range(wide)]
        inv = []
        for i in range(wide):
            inv.append(1.0 / d[i][i])
            for j in range(i + 1, wide):
                factor = d[j][i] * inv[i]
                for m in range(j, wide):
                    d[j][m] = d[j][m] - factor * d[i][m]
                    d[m][j] = d[j][m]
                grow[j] = grow[j] - factor[:, :COLS] * grow[i]
                prow[j] = prow[j] - factor * prow[i]
                cols[j] = [a - factor * b for a, b in zip(cols[j], cols[i])]
        for i in range(wide):
            scale = 1.0 / jnp.sqrt(d[i][i][0:1])
            ritz_ref[k + i : k + i + 1, :] = prow[i][0:1] * scale
        for i in range(wide):
            grow[i] = grow[i] * inv[i][:, :COLS]
            prow[i] = prow[i] * inv[i]
        for n in range(top, COLS // 8):
            for i in range(wide):
                col = cols[i][n - top]
                gs[n] = gs[n] - col[:, :COLS] * grow[i]
                ps[n] = ps[n] - col * prow[i]


def body(mesh_sizes, profiles, cell_width, basis, block_lists, block_counts, landmarks):
    NR, NC, NX, NY = mesh_sizes
    slots = block_lists.shape[-1]
    vmem = pl.BlockSpec(memory_space=pltpu.VMEM)
    hbm = pl.BlockSpec(memory_space=pltpu.HBM)
    smem = pl.BlockSpec(memory_space=pltpu.SMEM)
    half_rows = COLS // 2
    gram, proj, rows, cols = pl.pallas_call(
        functools.partial(tile_kernel, (NR, NC, NX, NY, slots)),
        out_shape=(
            jax.ShapeDtypeStruct((half_rows, BLK), f32),
            jax.ShapeDtypeStruct((COLS, BLK), f32),
            jax.ShapeDtypeStruct((NC, BLK), f32),
            jax.ShapeDtypeStruct((CP, BLK), f32),
        ),
        in_specs=[hbm, hbm, hbm, hbm, smem, smem],
        out_specs=(vmem,) * 4,
        scratch_shapes=[
            pltpu.VMEM((PCS, BLK), bf16),
            pltpu.VMEM((1, BLK), bf16),
            pltpu.VMEM((1, 1, 2, slots), jnp.int32),
            pltpu.SemaphoreType.DMA((4,)),
            pltpu.VMEM((8, slots), jnp.int32),
            pltpu.SMEM((8, slots), jnp.int32),
            pltpu.VMEM((2, KDIM, BLK), f32),
            pltpu.VMEM((1, KDIM, BLK), bf16),
            pltpu.VMEM((NR, KDIM, BLK), bf16),
            pltpu.VMEM((NR, COLS, BLK), bf16),
            pltpu.VMEM((NC, KDIM, BLK), bf16),
            pltpu.VMEM((NR, BLK, KDIM), bf16),
            pltpu.VMEM((NR, BLK, BLK), f32),
            pltpu.VMEM((NC, 8, BLK), f32),
            pltpu.VMEM((CP + 1, 2 * CP, BLK), bf16),
            pltpu.VMEM((NC, 2 * CP, BLK), bf16),
            pltpu.VMEM((NR, 2, 8, BLK), bf16),
            pltpu.VMEM((NR, COLS, BLK), bf16),
            pltpu.VMEM((slots // 2, BLK, 2 * BLK), bf16),
            pltpu.VMEM((slots, COLS, BLK), f32),
            pltpu.VMEM((slots, 8, BLK), f32),
            pltpu.VMEM((NC, 8, BLK), f32),
            pltpu.VMEM((NC, COLS, BLK), f32),
            pltpu.VMEM((SWEEPS - 1, NR, CP, BLK), bf16),
            pltpu.VMEM((SWEEPS - 1, NX, NC, BLK), bf16),
            pltpu.VMEM((SWEEPS - 1, NY, NC, BLK), bf16),
            pltpu.VMEM((NR, CP, BLK), f32),
            pltpu.VMEM((NX, NC, BLK), f32),
            pltpu.VMEM((NY, NC, BLK), f32),
            pltpu.VMEM((NX, NY, COLS, BLK), f32),
            pltpu.VMEM((NY, COLS, BLK), f32),
            pltpu.VMEM((NY, COLS, BLK), f32),
            pltpu.VMEM((NC, max(8, BLK // NC), BLK), f32),
            pltpu.VMEM((NC, BLK // NC, BLK), f32),
            pltpu.VMEM((NC, BLK // NC, BLK), f32),
            pltpu.VMEM((NR, half_rows // NR, BLK), f32),
            pltpu.VMEM((NR, half_rows // NR, BLK), f32),
            pltpu.VMEM((NC, half_rows // NR, BLK), f32),
            pltpu.VMEM((NR, half_rows // NR, BLK), f32),
            pltpu.SemaphoreType.DMA((23,)),
            pltpu.SemaphoreType.DMA((23,)),
        ],
        compiler_params=pltpu.CompilerParams(collective_id=0, has_side_effects=True),
        name="tile",
    )(profiles, cell_width.reshape(1, BLK), basis, block_lists, block_counts, landmarks)
    ritz, rows, cols = pl.pallas_call(
        functools.partial(finish_kernel, cells=landmarks.shape[0] * BLK),
        out_shape=(
            jax.ShapeDtypeStruct((COLS, BLK), f32),
            jax.ShapeDtypeStruct((NC, BLK), f32),
            jax.ShapeDtypeStruct((CP, BLK), f32),
        ),
        in_specs=[vmem] * 4,
        out_specs=(vmem,) * 3,
        name="finish",
    )(gram, proj, rows, cols)
    return rows.reshape(-1), cols[:NR].reshape(-1), ritz


def solution(mesh):
    NR, NC = mesh.shape["row"], mesh.shape["col"]
    NX = {32: 4, 4: 2}[NC]
    placed = (
        P(None, ("col", "row")),
        P(("col", "row")),
        P(None, ("col", "row")),
        P("row", "col", None, None),
        P("row", "col"),
        P(),
    )
    return jax.shard_map(
        functools.partial(body, (NR, NC, NX, NC // NX)),
        mesh=mesh,
        in_specs=placed,
        out_specs=(P("row"), P("col"), P(None, ("row", "col"))),
        check_vma=False,
    )
```

```python
import functools

import jax
import jax.numpy as jnp
from jax import lax
from jax.experimental import pallas as pl
from jax.experimental.pallas import tpu as pltpu
from jax.sharding import PartitionSpec as P

BLK = 128
PCS = 50
COLS = 64
SWEEPS = 3
KDIM = 64
CP = 16
RP = 32
SCALE = 512.0
MESH = pl.DeviceIdType.MESH
highest = lax.Precision.HIGHEST
f32 = jnp.float32
bf16 = jnp.bfloat16

ROW, COL, ROWKEY, COLKEY, KEEP, LAST, HAS = range(7)


def far_first(size):
    return sorted(range(1, size), key=lambda d: abs(2 * d - size))


def slot_table(lists_ref, count, table_ref):
    slots = lists_ref.shape[-1]
    lane = lax.broadcasted_iota(jnp.int32, (1, slots), 1)
    live = (lane < count).astype(jnp.int32)
    packed = live * 1024 + lists_ref[0, 0, 0:1, :] * 32 + lists_ref[0, 0, 1:2, :]
    down = jnp.broadcast_to(packed, (slots, slots)).T
    number = lax.broadcasted_iota(jnp.int32, (slots, slots), 0)
    across = lax.broadcasted_iota(jnp.int32, (slots, slots), 1)
    unlive = lambda v: jnp.where(v >= 1024, (v >> 5) & 31, RP)
    key_across = unlive(packed) * slots + lane
    key_down = unlive(down) * slots + number
    rank = jnp.sum((key_down < key_across).astype(jnp.int32), axis=0, keepdims=True)
    place = jnp.broadcast_to(rank, (slots, slots)).T == across
    order = jnp.sum(jnp.where(place, down, 0), axis=0, keepdims=True)
    rowkey = unlive(order)
    rows_down = unlive(down)
    upto = jnp.sum((rows_down <= across).astype(jnp.int32), axis=0, keepdims=True)
    here = jnp.sum((rows_down == across).astype(jnp.int32), axis=0, keepdims=True)
    key8 = jnp.broadcast_to(rowkey, (8, slots))
    before = jnp.where(lane == 0, -1, pltpu.roll(key8, 1, 1)[0:1])
    table_ref[ROW : ROW + 1, :] = (order >> 5) & 31
    table_ref[COL : COL + 1, :] = order & 31
    table_ref[ROWKEY : ROWKEY + 1, :] = rowkey
    table_ref[COLKEY : COLKEY + 1, :] = jnp.where(order >= 1024, order & 31, CP)
    table_ref[KEEP : KEEP + 1, :] = (before == rowkey).astype(jnp.int32)
    table_ref[LAST : LAST + 1, :] = jnp.maximum(upto - 1, 0)
    table_ref[HAS : HAS + 1, :] = jnp.minimum(here, 1)


def tile_kernel(
    dims,
    prof_hbm,
    width_hbm,
    basis_hbm,
    lists_hbm,
    count_ref,
    marks_ref,
    gram_ref,
    proj_ref,
    rows_ref,
    cols_ref,
    prof_ref,
    width_ref,
    lists_ref,
    input_sem,
    table_ref,
    idx,
    msg32,
    rowout,
    colbuf,
    basisbuf,
    rowbuf,
    left,
    uleft,
    uright,
    hot,
    rsplit,
    csplit,
    sbas,
    aff,
    sums,
    rowsums,
    rowpick,
    share,
    zvec,
    xvec,
    yvec,
    zlast,
    xlast,
    ylast,
    xshare,
    ysend,
    yshare,
    rlast,
    marks,
    gotmarks,
    gparts,
    zgram,
    pgram,
    zall,
    send_sem,
    recv_sem,
):
    NR, NC, NX, NY, slots = dims
    me_r = lax.axis_index("row")
    me_c = lax.axis_index("col")
    me_x = me_c // NY
    me_y = me_c % NY
    own_block = (me_c % 2) * NR + me_r
    to_r = me_c // 2
    to_x = own_block // NY
    own_y = lax.rem(own_block, NY)
    stays = (to_r == me_r) & (to_x == me_x)

    def zdev(d):
        return (lax.rem(me_r + d, NR), me_c)

    def xdev(d):
        return (me_r, lax.rem(me_x + d, NX) * NY + me_y)

    def ydev(d):
        return (me_r, me_x * NY + lax.rem(me_y + d, NY))

    awaited = {}

    def expect(region, number):
        awaited[number] = region

        def wait():
            del awaited[number]
            pltpu.make_async_copy(region, region, recv_sem.at[number]).wait()

        return wait

    def drain():
        pl.when(stays)(lambda: moved(NY - 1))
        pl.when(jnp.logical_not(stays))(lambda: moved(NY))
        for number, region in list(awaited.items()):
            pltpu.make_async_copy(region, region, recv_sem.at[number]).wait()
        for region, number in sent:
            pltpu.make_async_copy(region, region, send_sem.at[number]).wait()

    def pdev(d):
        return (me_r, lax.rem(me_c + d, NC))

    def hops(d):
        return min(d // NY, NX - d // NY) + min(d % NY, NY - d % NY)

    groups = {"z": (NR, zdev), "x": (NX, xdev), "y": (NY, ydev), "p": (NC, pdev)}
    steps = {axis: far_first(groups[axis][0]) for axis in "zxy"}
    steps["p"] = sorted(range(1, NC), key=lambda d: -hops(d))
    sent = []

    def push(axis, src_of, dst, number):
        size, device = groups[axis]
        for d in steps[axis]:
            pltpu.make_async_remote_copy(
                src_ref=src_of(d),
                dst_ref=dst.at[d],
                send_sem=send_sem.at[number],
                recv_sem=recv_sem.at[number],
                device_id=device(d),
                device_id_type=MESH,
            ).start()
        region = dst.at[pl.ds(1, size - 1)]
        sent.append((region, number))
        return expect(region, number)

    inputs = [
        pltpu.make_async_copy(src, dst, input_sem.at[n])
        for n, (src, dst) in enumerate(
            (
                (prof_hbm, prof_ref),
                (width_hbm, width_ref),
                (lists_hbm, lists_ref),
                (basis_hbm, basisbuf.at[0]),
            )
        )
    ]
    for copy in inputs:
        copy.start()
    barrier = pltpu.get_barrier_semaphore()
    for axis in "pz":
        for d in steps[axis]:
            pl.semaphore_signal(
                barrier, inc=1, device_id=groups[axis][1](d), device_id_type=MESH
            )
    for n in range(NY):
        block = me_x * NY + n
        source = (lax.rem(block, NR), 2 * me_r + block // NR)

        @pl.when((source[0] != me_r) | (source[1] != me_c))
        def _(source=source):
            pl.semaphore_signal(barrier, inc=1, device_id=source, device_id_type=MESH)
    for copy in inputs:
        copy.wait()

    prof = prof_ref[...].astype(f32)
    half = jnp.sum(prof * prof, axis=0, keepdims=True) * -0.5
    h1 = half.astype(bf16).astype(f32)
    h2 = (half - h1).astype(bf16).astype(f32)
    h3 = half - h1 - h2
    width = width_ref[...].astype(f32)
    ones = jnp.ones((1, BLK), f32)
    msg32[...] = jnp.zeros_like(msg32)
    for side in range(2):
        msg32[side, 0:PCS, :] = prof
        a, b = (50, 53) if side == 0 else (53, 50)
        msg32[side, a : a + 1, :] = h1
        msg32[side, a + 1 : a + 2, :] = h2
        msg32[side, a + 2 : a + 3, :] = h3
        for n in range(3):
            msg32[side, b + n : b + n + 1, :] = ones
        w = 56 + side
        msg32[side, w : w + 1, :] = width
    colbuf[0] = msg32[1].astype(bf16)
    outgoing = rowout.at[0]
    rowout[0] = msg32[0].astype(bf16)

    near = NR + NC - 2
    far = NY - stays.astype(jnp.int32)

    it = lax.broadcasted_iota(jnp.int32, (2 * CP, BLK), 0)

    def tables(k, carry):
        hot[k] = ((it == k) | (it == k + CP)).astype(f32).astype(bf16)
        return carry

    lax.fori_loop(0, CP, tables, 0)
    hot[CP] = jnp.zeros((2 * CP, BLK), bf16)

    pl.semaphore_wait(barrier, near + far)

    for n in range(NY):
        here = stays & (me_y == n)

        @pl.when(jnp.logical_not(here))
        def _(n=n):
            pltpu.make_async_remote_copy(
                src_ref=rowout.at[0],
                dst_ref=rowbuf.at[own_y],
                send_sem=send_sem.at[0],
                recv_sem=recv_sem.at[0],
                device_id=(to_r, to_x * NY + n),
                device_id_type=MESH,
            ).start()

        @pl.when(here)
        def _():
            pltpu.make_async_copy(rowout.at[0], rowbuf.at[own_y], recv_sem.at[0]).start()

    wait_col = push("z", lambda d: colbuf.at[0], colbuf, 1)
    slot_table(lists_ref, count_ref[0, 0], table_ref)
    tabled = pltpu.make_async_copy(table_ref, idx, recv_sem.at[20])
    tabled.start()
    tabled.wait()
    own_rows = rowbuf.at[pl.ds(0, NY)]
    pltpu.make_async_copy(own_rows, own_rows, recv_sem.at[0]).wait()

    def moved(blocks):
        region = rowbuf.at[pl.ds(0, blocks)]
        pltpu.make_async_copy(region, region, send_sem.at[0]).wait()

    for d in far_first(NX):
        pltpu.make_async_remote_copy(
            src_ref=rowbuf.at[pl.ds(0, NY)],
            dst_ref=rowbuf.at[pl.ds(d * NY, NY)],
            send_sem=send_sem.at[3],
            recv_sem=recv_sem.at[3],
            device_id=xdev(d),
            device_id_type=MESH,
        ).start()
    region_x = rowbuf.at[pl.ds(NY, (NX - 1) * NY)]
    sent.append((region_x, 3))
    wait_rows = expect(region_x, 3)

    wait_col()

    def col_place(j):
        return lax.rem(me_r - j + NR, NR)

    def row_place(i):
        return lax.rem(me_x - i // NY + NX, NX) * NY + lax.rem(i, NY)

    def col_prepare(n, carry):
        turned = colbuf[n].astype(f32).T
        left[n] = turned.astype(bf16)
        w = jnp.broadcast_to(turned[:, 57:58], (BLK, BLK))
        uleft[n] = (2.0 * 1.4426950408889634) / w
        return carry

    lax.fori_loop(0, NR, col_prepare, 0)

    wait_rows()

    def row_prepare(n, carry):
        w = rowbuf[n].astype(f32)[56:57, :]
        uright[n] = jnp.broadcast_to(1.0 / w, (8, BLK))
        return carry

    lax.fori_loop(0, NC, row_prepare, 0)

    pairs = slots // 2

    def build(p, acc):
        halves = []
        for h in range(2):
            j = col_place(idx[COL, 2 * p + h])
            i = row_place(idx[ROW, 2 * p + h])
            d = jnp.dot(left[j], rowbuf[i], preferred_element_type=f32)
            e = d * uleft[j] * uright[i][0:1, :]
            halves.append(jnp.exp2(e).astype(bf16))
        block = jnp.concatenate(halves, axis=1)
        aff[p] = block
        keys = [idx[COLKEY, 2 * p + h] for h in range(2)]
        lhs = jnp.concatenate([hot[k, 0:CP, :] for k in keys], axis=1)
        return acc + lax.dot_general(
            lhs, block, (((1,), (1,)), ((), ())), preferred_element_type=f32
        )

    first_part = lax.fori_loop(0, pairs, build, jnp.zeros((CP, BLK), f32), unroll=8)

    def col_pass():
        def step(p, acc):
            s, t = 2 * p, 2 * p + 1
            lhs = jnp.concatenate(
                [
                    rsplit[idx[ROW, s]] * hot[idx[COLKEY, s]],
                    rsplit[idx[ROW, t]] * hot[idx[COLKEY, t]],
                ],
                axis=1,
            )
            return acc + lax.dot_general(
                lhs, aff[p], (((1,), (1,)), ((), ())), preferred_element_type=f32
            )

        acc = lax.fori_loop(0, pairs, step, jnp.zeros((2 * CP, BLK), f32), unroll=8)
        return acc[0:CP] + acc[CP:]

    sub8 = lax.broadcasted_iota(jnp.int32, (8, BLK), 0)

    def row_pass():
        def step(p, acc):
            s, t = 2 * p, 2 * p + 1
            lhs = csplit[idx[COL, s], 0] + csplit[idx[COL, t], 1]
            both = jnp.dot(lhs, aff[p], preferred_element_type=f32)
            acc = acc * idx[KEEP, s].astype(f32) + jnp.where(sub8 < 2, both[:, :BLK], 0.0)
            rowsums[s] = acc
            acc = acc * idx[KEEP, t].astype(f32) + jnp.where(sub8 < 2, 0.0, both[:, BLK:])
            rowsums[t] = acc
            return acc

        lax.fori_loop(0, pairs, step, jnp.zeros((8, BLK), f32), unroll=8)
        for i in range(NC):
            rowpick[i] = rowsums[idx[LAST, i]] * idx[HAS, i].astype(f32)
        return jnp.sum(rowpick[...], axis=1)

    def col_total(k, part):
        buf = zlast if k == SWEEPS - 1 else zvec.at[k]
        buf[0] = part.astype(buf.dtype)
        wait = push("z", lambda d: buf.at[0], buf, 5 + k)
        wait()
        total = buf[lax.rem(me_r, NR)].astype(f32)
        for r in range(1, NR):
            total = total + buf[lax.rem(me_r - r + NR, NR)].astype(f32)
        return total

    def row_over_x(k, part):
        bx = xlast if k == SWEEPS - 1 else xvec.at[k]
        bx[0] = part.astype(bx.dtype)
        wait = push("x", lambda d: bx.at[0], bx, 8 + k)

        def finish():
            wait()
            total = bx[me_x].astype(f32)
            for x in range(1, NX):
                total = total + bx[lax.rem(me_x - x + NX, NX)].astype(f32)
            return total

        return finish

    def row_over_y(k, part):
        by = ylast if k == SWEEPS - 1 else yvec.at[k]
        by[0] = part.astype(by.dtype)
        wait = push("y", lambda d: by.at[0], by, 11 + k)

        def finish():
            wait()
            total = by[me_y].astype(f32)
            for y in range(1, NY):
                total = total + by[lax.rem(me_y - y + NY, NY)].astype(f32)
            return total

        return finish

    def row_total(k, part):
        return row_over_y(k, row_over_x(k, part)())()

    def split(v):
        hi = v.astype(bf16).astype(f32)
        return hi, v - hi

    def spread_rows(vec):
        for n in range(NC):
            hi, lo = split(jnp.broadcast_to(vec[n : n + 1, :], (CP, BLK)))
            rsplit[n] = jnp.concatenate([hi, lo], axis=0).astype(bf16)

    def spread_cols(vec):
        for n in range(NR):
            hi, lo = split(jnp.broadcast_to(vec[n : n + 1, :], (8, BLK)))
            even = jnp.where(sub8 % 2 == 0, hi, lo)
            csplit[n, 0] = jnp.where(sub8 < 2, even, 0.0).astype(bf16)
            csplit[n, 1] = jnp.where((sub8 >= 2) & (sub8 < 4), even, 0.0).astype(bf16)

    for k in range(SWEEPS):
        part = first_part if k == 0 else col_pass()
        cols_ref[...] = part
        cvec = SCALE / col_total(k, part)
        spread_cols(cvec)
        if k < SWEEPS - 1:
            part = row_pass()
            rows_ref[...] = part
            if k == 0:
                wait_basis = push("z", lambda d: basisbuf.at[0], basisbuf, 4)
            rvec = SCALE / row_total(k, part)
            spread_rows(rvec)
    cols_ref[...] = cvec

    over_x = row_over_x(SWEEPS - 1, row_pass())
    wait_basis()
    for j in range(NR):
        block = basisbuf[col_place(j)].astype(f32) * cvec[j : j + 1, :]
        sbas[j] = block.astype(bf16)

    def subspace(p, acc):
        for h in range(2):
            s = 2 * p + h
            product = jnp.dot(
                sbas[idx[COL, s]],
                aff[p, :, h * BLK : (h + 1) * BLK],
                preferred_element_type=f32,
            )
            acc = acc * idx[KEEP, s].astype(f32) + product
            sums[s] = acc
        return acc

    lax.fori_loop(0, pairs, subspace, jnp.zeros((COLS, BLK), f32), unroll=4)

    def pick(i, carry):
        share[i] = sums[idx[LAST, i]] * idx[HAS, i].astype(f32)
        return carry

    lax.fori_loop(0, NC, pick, 0)

    marked = [jnp.clip(marks_ref[2 * me_r + h] - me_r * NC, 0, NC - 1) for h in range(2)]
    both = jnp.concatenate([share[n] for n in marked], axis=0).T
    cells = BLK // NC
    for c in range(NC):
        marks[c] = both[c * cells : (c + 1) * cells]
    wait_marks = push("p", lambda d: marks.at[lax.rem(me_c + d, NC)], gotmarks, 21)
    over_y = row_over_y(SWEEPS - 1, over_x())

    def own_part(x):
        return share.at[pl.ds(x * NY, NY)]

    wait_share = push("x", lambda d: own_part(lax.rem(me_x + d, NX)), xshare, 14)
    rvec = SCALE / over_y()
    rows_ref[...] = rvec
    for n in range(NC):
        rlast[n] = jnp.broadcast_to(rvec[n : n + 1, :], (max(8, cells), BLK))
    lanes = lax.broadcasted_iota(jnp.int32, (cells, BLK), 1)
    own = lanes == me_c * cells + lax.broadcasted_iota(jnp.int32, (cells, BLK), 0)
    scales = [
        jnp.sum(jnp.where(own, rlast[n][0:cells], 0.0), axis=1, keepdims=True) for n in marked
    ]
    wait_marks()
    total = marks[me_c]
    for d in range(1, NC):
        total = total + gotmarks[d]
    masked = total * (jnp.where(lanes < COLS, scales[0], scales[1]) * (1.0 / SCALE))
    gram = jnp.zeros((COLS, COLS), f32)
    for h in range(2):
        block = masked[:, h * COLS : (h + 1) * COLS]
        gram = gram + lax.dot_general(
            block, block, (((0,), (0,)), ((), ())), precision=highest, preferred_element_type=f32
        )
    half_rows = COLS // 2
    packed = jnp.concatenate([gram[:half_rows], gram[half_rows:]], axis=1)
    part_rows = half_rows // NR
    for n in range(NR):
        gparts[n] = packed[n * part_rows : (n + 1) * part_rows]
    zgram[0] = gparts[me_r]
    push("z", lambda d: gparts.at[lax.rem(me_r + d, NR)], zgram, 16)()
    total = zgram[me_r]
    for n in range(1, NR):
        total = total + zgram[lax.rem(me_r - n + NR, NR)]

    def over(axis, buf, number, value):
        buf[0] = value
        return push(axis, lambda d: buf.at[0], buf, number)

    def added(buf, size, me):
        total = buf[me]
        for n in range(1, size):
            total = total + buf[lax.rem(me - n + size, size)]
        return total

    wait_pgram = over("p", pgram, 17, total)
    wait_share()

    def add_x(n, carry):
        total = share[me_x * NY + n]
        for d in range(1, NX):
            total = total + xshare[d, n]
        ysend[n] = total
        return carry

    lax.fori_loop(0, NY, add_x, 0)
    wait_yshare = push("y", lambda d: ysend.at[lax.rem(me_y + d, NY)], yshare, 15)
    wait_pgram()
    wait_zall = over("z", zall, 19, added(pgram, NC, me_c))
    wait_yshare()
    total = ysend[me_y]
    for d in range(1, NY):
        total = total + yshare[d]
    proj_ref[...] = total * (rows_ref[pl.ds(me_c, 1), :] * (1.0 / SCALE))
    wait_zall()
    for n in range(NR):
        gram_ref[n * part_rows : (n + 1) * part_rows, :] = zall[lax.rem(me_r - n + NR, NR)]
    drain()


def finish_kernel(gram_ref, proj_ref, rows_in, cols_in, ritz_ref, rows_ref, cols_ref, *, cells):
    rows_ref[...] = rows_in[...]
    cols_ref[...] = cols_in[...]
    half_rows = COLS // 2
    packed = gram_ref[...] * (1.0 / cells)
    gram = jnp.concatenate([packed[:, :COLS], packed[:, COLS:]], axis=0)
    proj = proj_ref[...]
    gs = [gram[n : n + 8] for n in range(0, COLS, 8)]
    ps = [proj[n : n + 8] for n in range(0, COLS, 8)]
    wide = 4
    for k in range(0, COLS, wide):
        top, row = k // 8, k % 8
        cols = [
            [jnp.broadcast_to(g[:, k + m : k + m + 1], (8, BLK)) for g in gs[top:]]
            for m in range(wide)
        ]
        flat = lambda v, i: jnp.broadcast_to(v[row + i : row + i + 1, :], (8, v.shape[1]))
        d = [[flat(cols[m][0], i) for m in range(wide)] for i in range(wide)]
        grow = [flat(gs[top], i) for i in range(wide)]
        prow = [flat(ps[top], i) for i in range(wide)]
        inv = []
        for i in range(wide):
            inv.append(1.0 / d[i][i])
            for j in range(i + 1, wide):
                factor = d[j][i] * inv[i]
                for m in range(j, wide):
                    d[j][m] = d[j][m] - factor * d[i][m]
                    d[m][j] = d[j][m]
                grow[j] = grow[j] - factor[:, :COLS] * grow[i]
                prow[j] = prow[j] - factor * prow[i]
                cols[j] = [a - factor * b for a, b in zip(cols[j], cols[i])]
        for i in range(wide):
            scale = 1.0 / jnp.sqrt(d[i][i][0:1])
            ritz_ref[k + i : k + i + 1, :] = prow[i][0:1] * scale
        for i in range(wide):
            grow[i] = grow[i] * inv[i][:, :COLS]
            prow[i] = prow[i] * inv[i]
        for n in range(top, COLS // 8):
            for i in range(wide):
                col = cols[i][n - top]
                gs[n] = gs[n] - col[:, :COLS] * grow[i]
                ps[n] = ps[n] - col * prow[i]


def body(mesh_sizes, profiles, cell_width, basis, block_lists, block_counts, landmarks):
    NR, NC, NX, NY = mesh_sizes
    slots = block_lists.shape[-1]
    vmem = pl.BlockSpec(memory_space=pltpu.VMEM)
    hbm = pl.BlockSpec(memory_space=pltpu.HBM)
    smem = pl.BlockSpec(memory_space=pltpu.SMEM)
    half_rows = COLS // 2
    gram, proj, rows, cols = pl.pallas_call(
        functools.partial(tile_kernel, (NR, NC, NX, NY, slots)),
        out_shape=(
            jax.ShapeDtypeStruct((half_rows, BLK), f32),
            jax.ShapeDtypeStruct((COLS, BLK), f32),
            jax.ShapeDtypeStruct((NC, BLK), f32),
            jax.ShapeDtypeStruct((CP, BLK), f32),
        ),
        in_specs=[hbm, hbm, hbm, hbm, smem, smem],
        out_specs=(vmem,) * 4,
        scratch_shapes=[
            pltpu.VMEM((PCS, BLK), bf16),
            pltpu.VMEM((1, BLK), bf16),
            pltpu.VMEM((1, 1, 2, slots), jnp.int32),
            pltpu.SemaphoreType.DMA((4,)),
            pltpu.VMEM((8, slots), jnp.int32),
            pltpu.SMEM((8, slots), jnp.int32),
            pltpu.VMEM((2, KDIM, BLK), f32),
            pltpu.VMEM((1, KDIM, BLK), bf16),
            pltpu.VMEM((NR, KDIM, BLK), bf16),
            pltpu.VMEM((NR, COLS, BLK), bf16),
            pltpu.VMEM((NC, KDIM, BLK), bf16),
            pltpu.VMEM((NR, BLK, KDIM), bf16),
            pltpu.VMEM((NR, BLK, BLK), f32),
            pltpu.VMEM((NC, 8, BLK), f32),
            pltpu.VMEM((CP + 1, 2 * CP, BLK), bf16),
            pltpu.VMEM((NC, 2 * CP, BLK), bf16),
            pltpu.VMEM((NR, 2, 8, BLK), bf16),
            pltpu.VMEM((NR, COLS, BLK), bf16),
            pltpu.VMEM((slots // 2, BLK, 2 * BLK), bf16),
            pltpu.VMEM((slots, COLS, BLK), f32),
            pltpu.VMEM((slots, 8, BLK), f32),
            pltpu.VMEM((NC, 8, BLK), f32),
            pltpu.VMEM((NC, COLS, BLK), f32),
            pltpu.VMEM((SWEEPS - 1, NR, CP, BLK), bf16),
            pltpu.VMEM((SWEEPS - 1, NX, NC, BLK), bf16),
            pltpu.VMEM((SWEEPS - 1, NY, NC, BLK), bf16),
            pltpu.VMEM((NR, CP, BLK), f32),
            pltpu.VMEM((NX, NC, BLK), f32),
            pltpu.VMEM((NY, NC, BLK), f32),
            pltpu.VMEM((NX, NY, COLS, BLK), f32),
            pltpu.VMEM((NY, COLS, BLK), f32),
            pltpu.VMEM((NY, COLS, BLK), f32),
            pltpu.VMEM((NC, max(8, BLK // NC), BLK), f32),
            pltpu.VMEM((NC, BLK // NC, BLK), f32),
            pltpu.VMEM((NC, BLK // NC, BLK), f32),
            pltpu.VMEM((NR, half_rows // NR, BLK), f32),
            pltpu.VMEM((NR, half_rows // NR, BLK), f32),
            pltpu.VMEM((NC, half_rows // NR, BLK), f32),
            pltpu.VMEM((NR, half_rows // NR, BLK), f32),
            pltpu.SemaphoreType.DMA((23,)),
            pltpu.SemaphoreType.DMA((23,)),
        ],
        compiler_params=pltpu.CompilerParams(collective_id=0, has_side_effects=True),
        name="tile",
    )(profiles, cell_width.reshape(1, BLK), basis, block_lists, block_counts, landmarks)
    ritz, rows, cols = pl.pallas_call(
        functools.partial(finish_kernel, cells=landmarks.shape[0] * BLK),
        out_shape=(
            jax.ShapeDtypeStruct((COLS, BLK), f32),
            jax.ShapeDtypeStruct((NC, BLK), f32),
            jax.ShapeDtypeStruct((CP, BLK), f32),
        ),
        in_specs=[vmem] * 4,
        out_specs=(vmem,) * 3,
        name="finish",
    )(gram, proj, rows, cols)
    return rows.reshape(-1), cols[:NR].reshape(-1), ritz


def solution(mesh):
    NR, NC = mesh.shape["row"], mesh.shape["col"]
    NX = {32: 4, 4: 2}[NC]
    placed = (
        P(None, ("col", "row")),
        P(("col", "row")),
        P(None, ("col", "row")),
        P("row", "col", None, None),
        P("row", "col"),
        P(),
    )
    return jax.shard_map(
        functools.partial(body, (NR, NC, NX, NC // NX)),
        mesh=mesh,
        in_specs=placed,
        out_specs=(P("row"), P("col"), P(None, ("row", "col"))),
        check_vma=False,
    )
```

```python
import functools

import jax
import jax.numpy as jnp
from jax import lax
from jax.experimental import pallas as pl
from jax.experimental.pallas import tpu as pltpu
from jax.sharding import PartitionSpec as P

BLK = 128
PCS = 50
COLS = 64
SWEEPS = 3
KDIM = 64
CP = 16
RP = 32
SCALE = 512.0
MESH = pl.DeviceIdType.MESH
highest = lax.Precision.HIGHEST
f32 = jnp.float32
bf16 = jnp.bfloat16

ROW, COL, ROWKEY, COLKEY, KEEP, LAST, HAS = range(7)


def far_first(size):
    return sorted(range(1, size), key=lambda d: abs(2 * d - size))


def slot_table(lists_ref, count, table_ref):
    slots = lists_ref.shape[-1]
    lane = lax.broadcasted_iota(jnp.int32, (1, slots), 1)
    live = (lane < count).astype(jnp.int32)
    packed = live * 1024 + lists_ref[0, 0, 0:1, :] * 32 + lists_ref[0, 0, 1:2, :]
    down = jnp.broadcast_to(packed, (slots, slots)).T
    number = lax.broadcasted_iota(jnp.int32, (slots, slots), 0)
    across = lax.broadcasted_iota(jnp.int32, (slots, slots), 1)
    unlive = lambda v: jnp.where(v >= 1024, (v >> 5) & 31, RP)
    key_across = unlive(packed) * slots + lane
    key_down = unlive(down) * slots + number
    rank = jnp.sum((key_down < key_across).astype(jnp.int32), axis=0, keepdims=True)
    place = jnp.broadcast_to(rank, (slots, slots)).T == across
    order = jnp.sum(jnp.where(place, down, 0), axis=0, keepdims=True)
    rowkey = unlive(order)
    rows_down = unlive(down)
    upto = jnp.sum((rows_down <= across).astype(jnp.int32), axis=0, keepdims=True)
    here = jnp.sum((rows_down == across).astype(jnp.int32), axis=0, keepdims=True)
    key8 = jnp.broadcast_to(rowkey, (8, slots))
    before = jnp.where(lane == 0, -1, pltpu.roll(key8, 1, 1)[0:1])
    table_ref[ROW : ROW + 1, :] = (order >> 5) & 31
    table_ref[COL : COL + 1, :] = order & 31
    table_ref[ROWKEY : ROWKEY + 1, :] = rowkey
    table_ref[COLKEY : COLKEY + 1, :] = jnp.where(order >= 1024, order & 31, CP)
    table_ref[KEEP : KEEP + 1, :] = (before == rowkey).astype(jnp.int32)
    table_ref[LAST : LAST + 1, :] = jnp.maximum(upto - 1, 0)
    table_ref[HAS : HAS + 1, :] = jnp.minimum(here, 1)


def tile_kernel(
    dims,
    prof_hbm,
    width_hbm,
    basis_hbm,
    lists_hbm,
    count_ref,
    marks_ref,
    gram_ref,
    proj_ref,
    rows_ref,
    cols_ref,
    prof_ref,
    width_ref,
    lists_ref,
    input_sem,
    table_ref,
    idx,
    msg32,
    rowout,
    colbuf,
    basisbuf,
    rowbuf,
    left,
    uleft,
    uright,
    hot,
    rsplit,
    csplit,
    sbas,
    aff,
    sums,
    rowsums,
    rowpick,
    share,
    zvec,
    xvec,
    yvec,
    zlast,
    xlast,
    ylast,
    xshare,
    ysend,
    yshare,
    rlast,
    marks,
    gotmarks,
    gparts,
    zgram,
    pgram,
    zall,
    send_sem,
    recv_sem,
):
    NR, NC, NX, NY, slots = dims
    me_r = lax.axis_index("row")
    me_c = lax.axis_index("col")
    me_x = me_c // NY
    me_y = me_c % NY
    own_block = (me_c % 2) * NR + me_r
    to_r = me_c // 2
    to_x = own_block // NY
    own_y = lax.rem(own_block, NY)
    stays = (to_r == me_r) & (to_x == me_x)

    def zdev(d):
        return (lax.rem(me_r + d, NR), me_c)

    def xdev(d):
        return (me_r, lax.rem(me_x + d, NX) * NY + me_y)

    def ydev(d):
        return (me_r, me_x * NY + lax.rem(me_y + d, NY))

    awaited = {}

    def expect(region, number):
        awaited[number] = region

        def wait():
            del awaited[number]
            pltpu.make_async_copy(region, region, recv_sem.at[number]).wait()

        return wait

    def drain():
        pl.when(stays)(lambda: moved(NY - 1))
        pl.when(jnp.logical_not(stays))(lambda: moved(NY))
        for number, region in list(awaited.items()):
            pltpu.make_async_copy(region, region, recv_sem.at[number]).wait()
        for region, number in sent:
            pltpu.make_async_copy(region, region, send_sem.at[number]).wait()

    def pdev(d):
        return (me_r, lax.rem(me_c + d, NC))

    def hops(d):
        return min(d // NY, NX - d // NY) + min(d % NY, NY - d % NY)

    groups = {"z": (NR, zdev), "x": (NX, xdev), "y": (NY, ydev), "p": (NC, pdev)}
    steps = {axis: far_first(groups[axis][0]) for axis in "zxy"}
    steps["p"] = sorted(range(1, NC), key=lambda d: -hops(d))
    sent = []

    def push(axis, src_of, dst, number):
        size, device = groups[axis]
        for d in steps[axis]:
            pltpu.make_async_remote_copy(
                src_ref=src_of(d),
                dst_ref=dst.at[d],
                send_sem=send_sem.at[number],
                recv_sem=recv_sem.at[number],
                device_id=device(d),
                device_id_type=MESH,
            ).start()
        region = dst.at[pl.ds(1, size - 1)]
        sent.append((region, number))
        return expect(region, number)

    inputs = [
        pltpu.make_async_copy(src, dst, input_sem.at[n])
        for n, (src, dst) in enumerate(
            (
                (prof_hbm, prof_ref),
                (width_hbm, width_ref),
                (lists_hbm, lists_ref),
                (basis_hbm, basisbuf.at[0]),
            )
        )
    ]
    for copy in inputs:
        copy.start()
    barrier = pltpu.get_barrier_semaphore()
    for axis in "pz":
        for d in steps[axis]:
            pl.semaphore_signal(
                barrier, inc=1, device_id=groups[axis][1](d), device_id_type=MESH
            )
    for n in range(NY):
        block = me_x * NY + n
        source = (lax.rem(block, NR), 2 * me_r + block // NR)

        @pl.when((source[0] != me_r) | (source[1] != me_c))
        def _(source=source):
            pl.semaphore_signal(barrier, inc=1, device_id=source, device_id_type=MESH)
    for copy in inputs:
        copy.wait()

    prof = prof_ref[...].astype(f32)
    half = jnp.sum(prof * prof, axis=0, keepdims=True) * -0.5
    h1 = half.astype(bf16).astype(f32)
    h2 = (half - h1).astype(bf16).astype(f32)
    h3 = half - h1 - h2
    width = width_ref[...].astype(f32)
    ones = jnp.ones((1, BLK), f32)
    msg32[...] = jnp.zeros_like(msg32)
    for side in range(2):
        msg32[side, 0:PCS, :] = prof
        a, b = (50, 53) if side == 0 else (53, 50)
        msg32[side, a : a + 1, :] = h1
        msg32[side, a + 1 : a + 2, :] = h2
        msg32[side, a + 2 : a + 3, :] = h3
        for n in range(3):
            msg32[side, b + n : b + n + 1, :] = ones
        w = 56 + side
        msg32[side, w : w + 1, :] = width
    colbuf[0] = msg32[1].astype(bf16)
    outgoing = rowout.at[0]
    rowout[0] = msg32[0].astype(bf16)

    near = NR + NC - 2
    far = NY - stays.astype(jnp.int32)

    it = lax.broadcasted_iota(jnp.int32, (2 * CP, BLK), 0)

    def tables(k, carry):
        hot[k] = ((it == k) | (it == k + CP)).astype(f32).astype(bf16)
        return carry

    lax.fori_loop(0, CP, tables, 0)
    hot[CP] = jnp.zeros((2 * CP, BLK), bf16)

    pl.semaphore_wait(barrier, near + far)

    for n in range(NY):
        here = stays & (me_y == n)

        @pl.when(jnp.logical_not(here))
        def _(n=n):
            pltpu.make_async_remote_copy(
                src_ref=rowout.at[0],
                dst_ref=rowbuf.at[own_y],
                send_sem=send_sem.at[0],
                recv_sem=recv_sem.at[0],
                device_id=(to_r, to_x * NY + n),
                device_id_type=MESH,
            ).start()

        @pl.when(here)
        def _():
            pltpu.make_async_copy(rowout.at[0], rowbuf.at[own_y], recv_sem.at[0]).start()

    wait_col = push("z", lambda d: colbuf.at[0], colbuf, 1)
    slot_table(lists_ref, count_ref[0, 0], table_ref)
    tabled = pltpu.make_async_copy(table_ref, idx, recv_sem.at[20])
    tabled.start()
    tabled.wait()
    own_rows = rowbuf.at[pl.ds(0, NY)]
    pltpu.make_async_copy(own_rows, own_rows, recv_sem.at[0]).wait()

    def moved(blocks):
        region = rowbuf.at[pl.ds(0, blocks)]
        pltpu.make_async_copy(region, region, send_sem.at[0]).wait()

    for d in far_first(NX):
        pltpu.make_async_remote_copy(
            src_ref=rowbuf.at[pl.ds(0, NY)],
            dst_ref=rowbuf.at[pl.ds(d * NY, NY)],
            send_sem=send_sem.at[3],
            recv_sem=recv_sem.at[3],
            device_id=xdev(d),
            device_id_type=MESH,
        ).start()
    region_x = rowbuf.at[pl.ds(NY, (NX - 1) * NY)]
    sent.append((region_x, 3))
    wait_rows = expect(region_x, 3)

    wait_col()

    def col_place(j):
        return lax.rem(me_r - j + NR, NR)

    def row_place(i):
        return lax.rem(me_x - i // NY + NX, NX) * NY + lax.rem(i, NY)

    def col_prepare(n, carry):
        turned = colbuf[n].astype(f32).T
        left[n] = turned.astype(bf16)
        w = jnp.broadcast_to(turned[:, 57:58], (BLK, BLK))
        uleft[n] = (2.0 * 1.4426950408889634) / w
        return carry

    lax.fori_loop(0, NR, col_prepare, 0)

    wait_rows()

    def row_prepare(n, carry):
        w = rowbuf[n].astype(f32)[56:57, :]
        uright[n] = jnp.broadcast_to(1.0 / w, (8, BLK))
        return carry

    lax.fori_loop(0, NC, row_prepare, 0)

    pairs = slots // 2

    def build(p, acc):
        halves = []
        for h in range(2):
            j = col_place(idx[COL, 2 * p + h])
            i = row_place(idx[ROW, 2 * p + h])
            d = jnp.dot(left[j], rowbuf[i], preferred_element_type=f32)
            e = d * uleft[j] * uright[i][0:1, :]
            halves.append(jnp.exp2(e).astype(bf16))
        block = jnp.concatenate(halves, axis=1)
        aff[p] = block
        keys = [idx[COLKEY, 2 * p + h] for h in range(2)]
        lhs = jnp.concatenate([hot[k, 0:CP, :] for k in keys], axis=1)
        return acc + lax.dot_general(
            lhs, block, (((1,), (1,)), ((), ())), preferred_element_type=f32
        )

    first_part = lax.fori_loop(0, pairs, build, jnp.zeros((CP, BLK), f32), unroll=8)

    def col_pass():
        def step(p, acc):
            s, t = 2 * p, 2 * p + 1
            lhs = jnp.concatenate(
                [
                    rsplit[idx[ROW, s]] * hot[idx[COLKEY, s]],
                    rsplit[idx[ROW, t]] * hot[idx[COLKEY, t]],
                ],
                axis=1,
            )
            return acc + lax.dot_general(
                lhs, aff[p], (((1,), (1,)), ((), ())), preferred_element_type=f32
            )

        acc = lax.fori_loop(0, pairs, step, jnp.zeros((2 * CP, BLK), f32), unroll=16)
        return acc[0:CP] + acc[CP:]

    sub8 = lax.broadcasted_iota(jnp.int32, (8, BLK), 0)

    def row_pass():
        def step(p, acc):
            s, t = 2 * p, 2 * p + 1
            lhs = csplit[idx[COL, s], 0] + csplit[idx[COL, t], 1]
            both = jnp.dot(lhs, aff[p], preferred_element_type=f32)
            acc = acc * idx[KEEP, s].astype(f32) + jnp.where(sub8 < 2, both[:, :BLK], 0.0)
            rowsums[s] = acc
            acc = acc * idx[KEEP, t].astype(f32) + jnp.where(sub8 < 2, 0.0, both[:, BLK:])
            rowsums[t] = acc
            return acc

        lax.fori_loop(0, pairs, step, jnp.zeros((8, BLK), f32), unroll=16)
        for i in range(NC):
            rowpick[i] = rowsums[idx[LAST, i]] * idx[HAS, i].astype(f32)
        return jnp.sum(rowpick[...], axis=1)

    def col_total(k, part):
        buf = zlast if k == SWEEPS - 1 else zvec.at[k]
        buf[0] = part.astype(buf.dtype)
        wait = push("z", lambda d: buf.at[0], buf, 5 + k)
        wait()
        total = buf[lax.rem(me_r, NR)].astype(f32)
        for r in range(1, NR):
            total = total + buf[lax.rem(me_r - r + NR, NR)].astype(f32)
        return total

    def row_over_x(k, part):
        bx = xlast if k == SWEEPS - 1 else xvec.at[k]
        bx[0] = part.astype(bx.dtype)
        wait = push("x", lambda d: bx.at[0], bx, 8 + k)

        def finish():
            wait()
            total = bx[me_x].astype(f32)
            for x in range(1, NX):
                total = total + bx[lax.rem(me_x - x + NX, NX)].astype(f32)
            return total

        return finish

    def row_over_y(k, part):
        by = ylast if k == SWEEPS - 1 else yvec.at[k]
        by[0] = part.astype(by.dtype)
        wait = push("y", lambda d: by.at[0], by, 11 + k)

        def finish():
            wait()
            total = by[me_y].astype(f32)
            for y in range(1, NY):
                total = total + by[lax.rem(me_y - y + NY, NY)].astype(f32)
            return total

        return finish

    def row_total(k, part):
        return row_over_y(k, row_over_x(k, part)())()

    def split(v):
        hi = v.astype(bf16).astype(f32)
        return hi, v - hi

    def spread_rows(vec):
        for n in range(NC):
            hi, lo = split(jnp.broadcast_to(vec[n : n + 1, :], (CP, BLK)))
            rsplit[n] = jnp.concatenate([hi, lo], axis=0).astype(bf16)

    def spread_cols(vec):
        for n in range(NR):
            hi, lo = split(jnp.broadcast_to(vec[n : n + 1, :], (8, BLK)))
            even = jnp.where(sub8 % 2 == 0, hi, lo)
            csplit[n, 0] = jnp.where(sub8 < 2, even, 0.0).astype(bf16)
            csplit[n, 1] = jnp.where((sub8 >= 2) & (sub8 < 4), even, 0.0).astype(bf16)

    for k in range(SWEEPS):
        part = first_part if k == 0 else col_pass()
        cols_ref[...] = part
        cvec = SCALE / col_total(k, part)
        spread_cols(cvec)
        if k < SWEEPS - 1:
            part = row_pass()
            rows_ref[...] = part
            if k == 0:
                wait_basis = push("z", lambda d: basisbuf.at[0], basisbuf, 4)
            rvec = SCALE / row_total(k, part)
            spread_rows(rvec)
    cols_ref[...] = cvec

    over_x = row_over_x(SWEEPS - 1, row_pass())
    wait_basis()
    for j in range(NR):
        block = basisbuf[col_place(j)].astype(f32) * cvec[j : j + 1, :]
        sbas[j] = block.astype(bf16)

    def subspace(p, acc):
        for h in range(2):
            s = 2 * p + h
            product = jnp.dot(
                sbas[idx[COL, s]],
                aff[p, :, h * BLK : (h + 1) * BLK],
                preferred_element_type=f32,
            )
            acc = acc * idx[KEEP, s].astype(f32) + product
            sums[s] = acc
        return acc

    lax.fori_loop(0, pairs, subspace, jnp.zeros((COLS, BLK), f32), unroll=4)

    def pick(i, carry):
        share[i] = sums[idx[LAST, i]] * idx[HAS, i].astype(f32)
        return carry

    lax.fori_loop(0, NC, pick, 0)

    marked = [jnp.clip(marks_ref[2 * me_r + h] - me_r * NC, 0, NC - 1) for h in range(2)]
    both = jnp.concatenate([share[n] for n in marked], axis=0).T
    cells = BLK // NC
    for c in range(NC):
        marks[c] = both[c * cells : (c + 1) * cells]
    wait_marks = push("p", lambda d: marks.at[lax.rem(me_c + d, NC)], gotmarks, 21)
    over_y = row_over_y(SWEEPS - 1, over_x())

    def own_part(x):
        return share.at[pl.ds(x * NY, NY)]

    wait_share = push("x", lambda d: own_part(lax.rem(me_x + d, NX)), xshare, 14)
    rvec = SCALE / over_y()
    rows_ref[...] = rvec
    for n in range(NC):
        rlast[n] = jnp.broadcast_to(rvec[n : n + 1, :], (max(8, cells), BLK))
    lanes = lax.broadcasted_iota(jnp.int32, (cells, BLK), 1)
    own = lanes == me_c * cells + lax.broadcasted_iota(jnp.int32, (cells, BLK), 0)
    scales = [
        jnp.sum(jnp.where(own, rlast[n][0:cells], 0.0), axis=1, keepdims=True) for n in marked
    ]
    wait_marks()
    total = marks[me_c]
    for d in range(1, NC):
        total = total + gotmarks[d]
    masked = total * (jnp.where(lanes < COLS, scales[0], scales[1]) * (1.0 / SCALE))
    gram = jnp.zeros((COLS, COLS), f32)
    for h in range(2):
        block = masked[:, h * COLS : (h + 1) * COLS]
        gram = gram + lax.dot_general(
            block, block, (((0,), (0,)), ((), ())), precision=highest, preferred_element_type=f32
        )
    half_rows = COLS // 2
    packed = jnp.concatenate([gram[:half_rows], gram[half_rows:]], axis=1)
    part_rows = half_rows // NR
    for n in range(NR):
        gparts[n] = packed[n * part_rows : (n + 1) * part_rows]
    zgram[0] = gparts[me_r]
    push("z", lambda d: gparts.at[lax.rem(me_r + d, NR)], zgram, 16)()
    total = zgram[me_r]
    for n in range(1, NR):
        total = total + zgram[lax.rem(me_r - n + NR, NR)]

    def over(axis, buf, number, value):
        buf[0] = value
        return push(axis, lambda d: buf.at[0], buf, number)

    def added(buf, size, me):
        total = buf[me]
        for n in range(1, size):
            total = total + buf[lax.rem(me - n + size, size)]
        return total

    wait_pgram = over("p", pgram, 17, total)
    wait_share()

    def add_x(n, carry):
        total = share[me_x * NY + n]
        for d in range(1, NX):
            total = total + xshare[d, n]
        ysend[n] = total
        return carry

    lax.fori_loop(0, NY, add_x, 0)
    wait_yshare = push("y", lambda d: ysend.at[lax.rem(me_y + d, NY)], yshare, 15)
    wait_pgram()
    wait_zall = over("z", zall, 19, added(pgram, NC, me_c))
    wait_yshare()
    total = ysend[me_y]
    for d in range(1, NY):
        total = total + yshare[d]
    proj_ref[...] = total * (rows_ref[pl.ds(me_c, 1), :] * (1.0 / SCALE))
    wait_zall()
    for n in range(NR):
        gram_ref[n * part_rows : (n + 1) * part_rows, :] = zall[lax.rem(me_r - n + NR, NR)]
    drain()


def finish_kernel(gram_ref, proj_ref, rows_in, cols_in, ritz_ref, rows_ref, cols_ref, *, cells):
    rows_ref[...] = rows_in[...]
    cols_ref[...] = cols_in[...]
    half_rows = COLS // 2
    packed = gram_ref[...] * (1.0 / cells)
    gram = jnp.concatenate([packed[:, :COLS], packed[:, COLS:]], axis=0)
    proj = proj_ref[...]
    gs = [gram[n : n + 8] for n in range(0, COLS, 8)]
    ps = [proj[n : n + 8] for n in range(0, COLS, 8)]
    wide = 4
    for k in range(0, COLS, wide):
        top, row = k // 8, k % 8
        cols = [
            [jnp.broadcast_to(g[:, k + m : k + m + 1], (8, BLK)) for g in gs[top:]]
            for m in range(wide)
        ]
        flat = lambda v, i: jnp.broadcast_to(v[row + i : row + i + 1, :], (8, v.shape[1]))
        d = [[flat(cols[m][0], i) for m in range(wide)] for i in range(wide)]
        grow = [flat(gs[top], i) for i in range(wide)]
        prow = [flat(ps[top], i) for i in range(wide)]
        inv = []
        for i in range(wide):
            inv.append(1.0 / d[i][i])
            for j in range(i + 1, wide):
                factor = d[j][i] * inv[i]
                for m in range(j, wide):
                    d[j][m] = d[j][m] - factor * d[i][m]
                    d[m][j] = d[j][m]
                grow[j] = grow[j] - factor[:, :COLS] * grow[i]
                prow[j] = prow[j] - factor * prow[i]
                cols[j] = [a - factor * b for a, b in zip(cols[j], cols[i])]
        for i in range(wide):
            scale = 1.0 / jnp.sqrt(d[i][i][0:1])
            ritz_ref[k + i : k + i + 1, :] = prow[i][0:1] * scale
        for i in range(wide):
            grow[i] = grow[i] * inv[i][:, :COLS]
            prow[i] = prow[i] * inv[i]
        for n in range(top, COLS // 8):
            for i in range(wide):
                col = cols[i][n - top]
                gs[n] = gs[n] - col[:, :COLS] * grow[i]
                ps[n] = ps[n] - col * prow[i]


def body(mesh_sizes, profiles, cell_width, basis, block_lists, block_counts, landmarks):
    NR, NC, NX, NY = mesh_sizes
    slots = block_lists.shape[-1]
    vmem = pl.BlockSpec(memory_space=pltpu.VMEM)
    hbm = pl.BlockSpec(memory_space=pltpu.HBM)
    smem = pl.BlockSpec(memory_space=pltpu.SMEM)
    half_rows = COLS // 2
    gram, proj, rows, cols = pl.pallas_call(
        functools.partial(tile_kernel, (NR, NC, NX, NY, slots)),
        out_shape=(
            jax.ShapeDtypeStruct((half_rows, BLK), f32),
            jax.ShapeDtypeStruct((COLS, BLK), f32),
            jax.ShapeDtypeStruct((NC, BLK), f32),
            jax.ShapeDtypeStruct((CP, BLK), f32),
        ),
        in_specs=[hbm, hbm, hbm, hbm, smem, smem],
        out_specs=(vmem,) * 4,
        scratch_shapes=[
            pltpu.VMEM((PCS, BLK), bf16),
            pltpu.VMEM((1, BLK), bf16),
            pltpu.VMEM((1, 1, 2, slots), jnp.int32),
            pltpu.SemaphoreType.DMA((4,)),
            pltpu.VMEM((8, slots), jnp.int32),
            pltpu.SMEM((8, slots), jnp.int32),
            pltpu.VMEM((2, KDIM, BLK), f32),
            pltpu.VMEM((1, KDIM, BLK), bf16),
            pltpu.VMEM((NR, KDIM, BLK), bf16),
            pltpu.VMEM((NR, COLS, BLK), bf16),
            pltpu.VMEM((NC, KDIM, BLK), bf16),
            pltpu.VMEM((NR, BLK, KDIM), bf16),
            pltpu.VMEM((NR, BLK, BLK), f32),
            pltpu.VMEM((NC, 8, BLK), f32),
            pltpu.VMEM((CP + 1, 2 * CP, BLK), bf16),
            pltpu.VMEM((NC, 2 * CP, BLK), bf16),
            pltpu.VMEM((NR, 2, 8, BLK), bf16),
            pltpu.VMEM((NR, COLS, BLK), bf16),
            pltpu.VMEM((slots // 2, BLK, 2 * BLK), bf16),
            pltpu.VMEM((slots, COLS, BLK), f32),
            pltpu.VMEM((slots, 8, BLK), f32),
            pltpu.VMEM((NC, 8, BLK), f32),
            pltpu.VMEM((NC, COLS, BLK), f32),
            pltpu.VMEM((SWEEPS - 1, NR, CP, BLK), bf16),
            pltpu.VMEM((SWEEPS - 1, NX, NC, BLK), bf16),
            pltpu.VMEM((SWEEPS - 1, NY, NC, BLK), bf16),
            pltpu.VMEM((NR, CP, BLK), f32),
            pltpu.VMEM((NX, NC, BLK), f32),
            pltpu.VMEM((NY, NC, BLK), f32),
            pltpu.VMEM((NX, NY, COLS, BLK), f32),
            pltpu.VMEM((NY, COLS, BLK), f32),
            pltpu.VMEM((NY, COLS, BLK), f32),
            pltpu.VMEM((NC, max(8, BLK // NC), BLK), f32),
            pltpu.VMEM((NC, BLK // NC, BLK), f32),
            pltpu.VMEM((NC, BLK // NC, BLK), f32),
            pltpu.VMEM((NR, half_rows // NR, BLK), f32),
            pltpu.VMEM((NR, half_rows // NR, BLK), f32),
            pltpu.VMEM((NC, half_rows // NR, BLK), f32),
            pltpu.VMEM((NR, half_rows // NR, BLK), f32),
            pltpu.SemaphoreType.DMA((23,)),
            pltpu.SemaphoreType.DMA((23,)),
        ],
        compiler_params=pltpu.CompilerParams(collective_id=0, has_side_effects=True),
        name="tile",
    )(profiles, cell_width.reshape(1, BLK), basis, block_lists, block_counts, landmarks)
    ritz, rows, cols = pl.pallas_call(
        functools.partial(finish_kernel, cells=landmarks.shape[0] * BLK),
        out_shape=(
            jax.ShapeDtypeStruct((COLS, BLK), f32),
            jax.ShapeDtypeStruct((NC, BLK), f32),
            jax.ShapeDtypeStruct((CP, BLK), f32),
        ),
        in_specs=[vmem] * 4,
        out_specs=(vmem,) * 3,
        name="finish",
    )(gram, proj, rows, cols)
    return rows.reshape(-1), cols[:NR].reshape(-1), ritz


def solution(mesh):
    NR, NC = mesh.shape["row"], mesh.shape["col"]
    NX = {32: 4, 4: 2}[NC]
    placed = (
        P(None, ("col", "row")),
        P(("col", "row")),
        P(None, ("col", "row")),
        P("row", "col", None, None),
        P("row", "col"),
        P(),
    )
    return jax.shard_map(
        functools.partial(body, (NR, NC, NX, NC // NX)),
        mesh=mesh,
        in_specs=placed,
        out_specs=(P("row"), P("col"), P(None, ("row", "col"))),
        check_vma=False,
    )
```
